32 devices in a mesh: dp: 2 (over core), row: 4 (over z), col: 4 (over y, x).
Axes of the slice: x: 2, y: 2, z: 4, core: 2. Of those that a mesh axis runs over, the one named last changes fastest.
Arguments:
- inputs: bfloat16 [512, 12288], P('dp', 'col'), may hold values from -6 to 6
- weight_tiles: bfloat16 [4, 4, 432, 4096], P('row', 'col', 'dp'), may hold values from -0.109375 to 0.109375
- tile_rows: int32 [4, 4, 432], P('row', 'col'), may hold values from 0 to 191, as said below
- tile_cols: int32 [4, 4, 432], P('row', 'col'), may hold values from 0 to 47, as said below
- tile_counts: int32 [4, 4], P('row', 'col'), may hold values from 54 to 432, as said below
- act_grad: bfloat16 [512, 49152], P('dp', ('row', 'col')), may hold values from -6 to 6
Outputs:
- activation: bfloat16 [512, 49152], P('dp', ('row', 'col'))
- input_grad: bfloat16 [512, 12288], P(('dp', 'row'), 'col')
- tile_grads: bfloat16 [4, 4, 432, 4096], P('row', 'col', 'dp')
The draws below stay inside these ranges and needn't reach their ends.
Inputs may be any that keep to these rules, and one draw needn't show every extreme that they name: `tile_rows`: block row of a slot within its region; within each region the slots name distinct blocks. `tile_cols`: block column of a slot within its region. `tile_counts`: live slots of a region are its first ones; some region has all 432 slots live.
All inputs are finite; a program needn't handle non-finite values.
Results may differ from the reference program's by a relative error of at most 0.015.
Values may be sent and summed in bfloat16 or wider, within the bound.
No kernel may reach another device: no remote copies, remote signals or barrier semaphores. Data moves between devices by JAX's collectives and lax.ppermute only.
A program may use at most 128 MiB of HBM per device.

```python
import jax
import jax.numpy as jnp
from jax import lax

D = 12288
FF = 49152
MAXB = 432
TOKENS = 512
ROW_BLOCKS = 192
COL_BLOCKS = 48
N_ROW = 4
N_COL = 4


def tile_layout(key):
    layout_key = jax.random.fold_in(key, 11)
    region_keys = jax.random.split(layout_key, N_ROW * N_COL)
    region_blocks = FF // (64 * N_ROW) * (D // (64 * N_COL))
    chosen = jax.vmap(lambda one_key: jax.random.permutation(one_key, region_blocks)[:MAXB])(region_keys)
    return chosen.reshape(N_ROW, N_COL, MAXB).astype(jnp.int32)


def draw_tile_rows(key, part):
    return (tile_layout(key) // (D // (64 * N_COL))).astype(jnp.int32)


def draw_tile_cols(key, part):
    return (tile_layout(key) % (D // (64 * N_COL))).astype(jnp.int32)


def draw_tile_counts(key, part):
    count_key = jax.random.fold_in(key, 23)
    first, second = jax.random.split(count_key)
    counts = jax.random.randint(first, (N_ROW * N_COL,), (MAXB + 7) // 8, MAXB + 1)
    fullest = jax.random.randint(second, (), 0, N_ROW * N_COL)
    counts = jnp.where(jnp.arange(N_ROW * N_COL) == fullest, MAXB, counts)
    return counts.reshape(N_ROW, N_COL).astype(jnp.int32)


def raised(array, own_key, source, target, parts, factor):
    owner, partner = [(jnp.arange(array.shape[dim]) // (array.shape[dim] // parts)).reshape([-1 if axis == dim else 1 for axis in range(array.ndim)]) for dim in (source, target)]
    chosen = jax.random.permutation(own_key, parts)[partner]
    strong = (owner == chosen) | (owner == (partner + parts // 2) % parts)
    return jnp.where(strong, factor * array, array)


def block_levels(own_key, shape, shards, smallest, largest):
    def one(position, parts):
        heights = jax.random.uniform(jax.random.fold_in(jax.random.fold_in(own_key, 6), position), (parts,), jnp.float32, smallest / len(shards), largest / len(shards))
        return jnp.repeat(jnp.exp(heights), shape[position] // parts).reshape((-1,) + (1,) * (len(shape) - position - 1))

    loudness = one(*shards[0])
    for cut in shards[1:]:
        loudness = loudness * one(*cut)
    return loudness


def centred(key, dims, deviation, most, shards=(), dtype=jnp.bfloat16):
    gain = block_levels(key, dims, shards, -0.22, 0.18) if shards else 1.0
    values = jax.random.normal(key, dims, jnp.float32) * deviation * gain
    return jnp.minimum(jnp.maximum(values, -most), most).astype(dtype)


def bell_draw_with(own_key, extent, spread, bound, cuts, heavy, held_as=jnp.bfloat16):
    entries = spread * jax.random.normal(own_key, extent, jnp.float32)
    if cuts:
        entries = entries * block_levels(own_key, extent, cuts, -0.22, 0.18)
    return jnp.clip(raised(entries, jax.random.fold_in(own_key, 3), *heavy), -bound, bound).astype(held_as)


def setup_inputs(seed: int = 0) -> dict:
    arg_keys = jax.random.split(jax.random.key(seed), 7)
    inputs = centred(arg_keys[0], (TOKENS, D), 1.0, 6.0, ((0, 2), (1, 4)))
    weight_tiles = centred(arg_keys[1], (N_ROW, N_COL, MAXB, 4096), (D // 4) ** -0.5, 0.109375, ((0, 4), (1, 4), (2, 2)))
    tile_rows = draw_tile_rows(jax.random.fold_in(arg_keys[6], 71), 0)
    tile_cols = draw_tile_cols(jax.random.fold_in(arg_keys[6], 71), 0)
    tile_counts = draw_tile_counts(jax.random.fold_in(arg_keys[6], 71), 0)
    act_grad = bell_draw_with(arg_keys[5], (TOKENS, FF), 1.0, 6.0, ((0, 2), (1, 16)), (1, 0, 16, 2.0))
    return dict(inputs=inputs, weight_tiles=weight_tiles, tile_rows=tile_rows, tile_cols=tile_cols, tile_counts=tile_counts, act_grad=act_grad)


COEFF = 0.7978845608028654
CUBIC = 0.044715


def gelu_value(values):
    return 0.5 * values * (1.0 + jnp.tanh(COEFF * (values + CUBIC * values * values * values)))


def gelu_slope(values):
    inner = jnp.tanh(COEFF * (values + CUBIC * values * values * values))
    return 0.5 * (1.0 + inner) + 0.5 * values * (1.0 - inner * inner) * COEFF * (1.0 + 3.0 * CUBIC * values * values)


def reference(inputs, weight_tiles, tile_rows, tile_cols, tile_counts, act_grad):
    token_total = inputs.shape[0]
    input_blocks = inputs.astype(jnp.float32).T.reshape(N_COL, COL_BLOCKS, 64, token_total)
    row_range = jnp.arange(ROW_BLOCKS).astype(jnp.int32)
    col_range = jnp.arange(COL_BLOCKS).astype(jnp.int32)
    slot_range = jnp.arange(MAXB).astype(jnp.int32)

    def forward_row(carry, row_index):
        running = jnp.zeros((ROW_BLOCKS, 64, token_total), jnp.float32)
        for col_index in range(N_COL):
            tiles = weight_tiles[row_index, col_index].astype(jnp.float32).reshape(MAXB, 64, 64)
            alive = (slot_range < tile_counts[row_index, col_index]).astype(jnp.float32)
            gathered = input_blocks[col_index][tile_cols[row_index, col_index]]
            products = jnp.einsum("sik,skt->sit", tiles, gathered) * alive[:, None, None]
            selector = (tile_rows[row_index, col_index][:, None] == row_range[None, :]).astype(jnp.float32)
            running = running + jnp.einsum("sb,sit->bit", selector, products, precision=lax.Precision.HIGHEST)
        return carry, running.reshape(ROW_BLOCKS * 64, token_total)

    unused, pre_rows = lax.scan(forward_row, jnp.zeros((), jnp.float32), jnp.arange(N_ROW).astype(jnp.int32))
    pre = pre_rows.reshape(FF, token_total).T
    activation = gelu_value(pre).astype(jnp.bfloat16)
    grad_pre = (act_grad.astype(jnp.float32) * gelu_slope(pre)).astype(jnp.bfloat16)
    grad_blocks = grad_pre.astype(jnp.float32).T.reshape(N_ROW, ROW_BLOCKS, 64, token_total)

    def backward_row(carry, row_index):
        tile_list = []
        for col_index in range(N_COL):
            tiles = weight_tiles[row_index, col_index].astype(jnp.float32).reshape(MAXB, 64, 64)
            alive = (slot_range < tile_counts[row_index, col_index]).astype(jnp.float32)
            grads_here = grad_blocks[row_index][tile_rows[row_index, col_index]]
            inputs_here = input_blocks[col_index][tile_cols[row_index, col_index]]
            products = jnp.einsum("sik,sit->skt", tiles, grads_here) * alive[:, None, None]
            selector = (tile_cols[row_index, col_index][:, None] == col_range[None, :]).astype(jnp.float32)
            carry = carry.at[col_index].add(jnp.einsum("sc,skt->ckt", selector, products, precision=lax.Precision.HIGHEST))
            tile_term = jnp.einsum("sit,skt->sik", grads_here, inputs_here) * alive[:, None, None]
            tile_list.append(tile_term.reshape(MAXB, 4096).astype(jnp.bfloat16))
        return carry, jnp.stack(tile_list)

    start_grad = jnp.zeros((N_COL, COL_BLOCKS, 64, token_total), jnp.float32)
    input_total, tile_grads = lax.scan(backward_row, start_grad, jnp.arange(N_ROW).astype(jnp.int32))
    input_grad = input_total.reshape(D, token_total).T.astype(jnp.bfloat16)
    return activation, input_grad, tile_grads
```

```python
import functools

import jax
import jax.numpy as jnp
from jax import lax
from jax.experimental import pallas as pl
from jax.experimental.pallas import tpu as pltpu
from jax.sharding import PartitionSpec as P

COEFF = 0.7978845608028654
CUBIC = 0.044715
BLOCK = 64
VMEM_LIMIT = 60 * 1024 * 1024


def gelu_value(values):
    return 0.5 * values * (1.0 + jnp.tanh(COEFF * (values + CUBIC * values * values * values)))


def gelu_slope(values):
    inner = jnp.tanh(COEFF * (values + CUBIC * values * values * values))
    return 0.5 * (1.0 + inner) + 0.5 * values * (1.0 - inner * inner) * COEFF * (
        1.0 + 3.0 * CUBIC * values * values
    )


def widest_divisor(total, most):
    return max(divisor for divisor in range(1, most + 1) if total % divisor == 0)


def accumulate_kernel(unroll, count_ref, target_ref, source_ref, tiles_ref, table_ref, out_ref, total_ref):
    blocks = out_ref.shape[0]

    @pl.loop(0, blocks + 1)
    def _(block):
        total_ref[block] = jnp.zeros(total_ref.shape[1:], jnp.float32)

    count = count_ref[0]

    @pl.loop(0, pl.cdiv(count, unroll))
    def _(group):
        products = []
        places = []
        for lane in range(unroll):
            slot = group * unroll + lane
            places.append(jnp.where(slot < count, target_ref[slot], blocks))
            products.append(
                jnp.dot(tiles_ref[slot], table_ref[source_ref[slot]], preferred_element_type=jnp.float32)
            )
        for place, product in zip(places, products):
            total_ref[place] += product

    @pl.loop(0, blocks)
    def _(block):
        out_ref[block] = total_ref[block].astype(out_ref.dtype)


def accumulate(tiles, table, count, targets, sources, blocks):
    slots = tiles.shape[0]
    width = table.shape[2]
    whole = pl.BlockSpec(memory_space=pltpu.VMEM)
    scalars = pl.BlockSpec(memory_space=pltpu.SMEM)
    return pl.pallas_call(
        functools.partial(accumulate_kernel, widest_divisor(slots, 8)),
        out_shape=jax.ShapeDtypeStruct((blocks, BLOCK, width), jnp.bfloat16),
        in_specs=[scalars, scalars, scalars, whole, whole],
        out_specs=whole,
        scratch_shapes=[pltpu.VMEM((blocks + 1, BLOCK, width), jnp.float32)],
        compiler_params=pltpu.CompilerParams(vmem_limit_bytes=VMEM_LIMIT),
        cost_estimate=pl.CostEstimate(
            flops=2 * slots * BLOCK * BLOCK * width,
            bytes_accessed=2 * (tiles.size + table.size + blocks * BLOCK * width),
            transcendentals=0,
        ),
    )(count, targets, sources, tiles, table)


def outer_kernel(unroll, count_ref, row_ref, col_ref, grads_ref, inputs_ref, out_ref):
    slots = out_ref.shape[0]
    count = count_ref[0]

    @pl.loop(0, slots // unroll)
    def _(group):
        first = group * unroll

        @pl.when(first < count)
        def _():
            for lane in range(unroll):
                slot = first + lane
                product = jnp.dot(
                    grads_ref[row_ref[slot]], inputs_ref[col_ref[slot]], preferred_element_type=jnp.float32
                )
                out_ref[slot] = jnp.where(slot < count, product, 0.0).astype(out_ref.dtype)

        @pl.when(first >= count)
        def _():
            for lane in range(unroll):
                out_ref[first + lane] = jnp.zeros(out_ref.shape[1:], out_ref.dtype)


def outer(grads, inputs, count, rows, cols):
    slots = rows.shape[0]
    whole = pl.BlockSpec(memory_space=pltpu.VMEM)
    scalars = pl.BlockSpec(memory_space=pltpu.SMEM)
    return pl.pallas_call(
        functools.partial(outer_kernel, widest_divisor(slots, 8)),
        out_shape=jax.ShapeDtypeStruct((slots, BLOCK, BLOCK), jnp.bfloat16),
        in_specs=[scalars, scalars, scalars, whole, whole],
        out_specs=whole,
        compiler_params=pltpu.CompilerParams(vmem_limit_bytes=VMEM_LIMIT),
        cost_estimate=pl.CostEstimate(
            flops=2 * slots * BLOCK * BLOCK * grads.shape[2],
            bytes_accessed=2 * (grads.size + inputs.size + slots * BLOCK * BLOCK),
            transcendentals=0,
        ),
    )(count, rows, cols, grads, inputs)


def local(inputs, weight_tiles, tile_rows, tile_cols, tile_counts, act_grad):
    tokens = inputs.shape[0]
    in_blocks = inputs.shape[1] // BLOCK
    col_devices = lax.axis_size("col")
    share = act_grad.shape[1]
    out_blocks = share * col_devices // BLOCK
    slots = tile_rows.shape[2]
    rows = tile_rows.reshape(slots)
    cols = tile_cols.reshape(slots)
    count = tile_counts.reshape(1)

    inputs_t = inputs.T.reshape(in_blocks, BLOCK, tokens)
    tiles = lax.all_gather(weight_tiles, "dp", axis=2, tiled=True).reshape(slots, BLOCK, BLOCK)
    pre_partial = accumulate(tiles, inputs_t, count, rows, cols, out_blocks)
    pre = lax.psum_scatter(
        pre_partial.reshape(out_blocks * BLOCK, tokens), "col", scatter_dimension=0, tiled=True
    ).astype(jnp.float32)
    activation = gelu_value(pre).astype(jnp.bfloat16).T
    grad_share = (act_grad.T.astype(jnp.float32) * gelu_slope(pre)).astype(jnp.bfloat16)
    grads = lax.all_gather(grad_share, "col", axis=0, tiled=True).reshape(out_blocks, BLOCK, tokens)

    tiles_t = jnp.swapaxes(tiles, 1, 2)
    input_partial = accumulate(tiles_t, grads, count, cols, rows, in_blocks)
    input_grad = lax.psum_scatter(
        input_partial.reshape(in_blocks * BLOCK, tokens), "row", scatter_dimension=1, tiled=True
    ).T
    inputs_n = jnp.swapaxes(inputs_t, 1, 2)
    tile_partial = outer(grads, inputs_n, count, rows, cols).reshape(slots, BLOCK * BLOCK)
    tile_sum = lax.psum_scatter(tile_partial, "dp", scatter_dimension=0, tiled=True)
    tile_grads = tile_sum.reshape(1, 1, slots // lax.axis_size("dp"), BLOCK * BLOCK)
    return (activation, input_grad, tile_grads)


def solution(mesh):
    return jax.shard_map(
        local,
        mesh=mesh,
        in_specs=(
            P("dp", "col"),
            P("row", "col", "dp", None),
            P("row", "col", None),
            P("row", "col", None),
            P("row", "col"),
            P("dp", ("row", "col")),
        ),
        out_specs=(P("dp", ("row", "col")), P(("dp", "row"), "col"), P("row", "col", "dp", None)),
        check_vma=False,
    )
```

```python
import functools

import jax
import jax.numpy as jnp
from jax import lax
from jax.experimental import pallas as pl
from jax.experimental.pallas import tpu as pltpu
from jax.sharding import PartitionSpec as P

COEFF = 0.7978845608028654
CUBIC = 0.044715
BLOCK = 64
HALF = 32
CHUNKS = 2
MIB = 1024 * 1024
VMEM = pl.BlockSpec(memory_space=pltpu.VMEM)
SMEM = pl.BlockSpec(memory_space=pltpu.SMEM)
ANY = pl.BlockSpec(memory_space=pl.ANY)
NT = (((1,), (1,)), ((), ()))


def widest_divisor(total, most):
    return max(divisor for divisor in range(1, most + 1) if total % divisor == 0)


def unpack(packed):
    return jnp.concatenate([packed[:, :BLOCK], packed[:, BLOCK:]], axis=0)


def pack(square):
    return jnp.concatenate([square[:HALF], square[HALF:]], axis=1)


def matmul(left, right):
    return jnp.dot(left, right, preferred_element_type=jnp.float32)


def matmul_nt(left, right):
    return lax.dot_general(left, right, NT, preferred_element_type=jnp.float32)


def call(kernel, name, out_shape, in_specs, out_specs, operands, mib, flops, scratch=(), **more):
    moved = sum(operand.size * operand.dtype.itemsize for operand in operands)
    moved += sum(leaf.size * leaf.dtype.itemsize for leaf in jax.tree.leaves(out_shape))
    return pl.pallas_call(
        kernel,
        out_shape=out_shape,
        in_specs=in_specs,
        out_specs=out_specs,
        scratch_shapes=list(scratch),
        name=name,
        compiler_params=pltpu.CompilerParams(vmem_limit_bytes=mib * MIB),
        cost_estimate=pl.CostEstimate(flops=flops, bytes_accessed=moved, transcendentals=0),
        **more,
    )(*operands)


def half_counts(facts_ref, half_slots):
    count, dp = facts_ref[0], facts_ref[2]
    own = dp * half_slots
    other = half_slots - own
    return count, ((own, 0), (other, 1))


def add_products(facts_ref, target_ref, source_ref, tile_refs, table, total, width):
    spare = total.shape[0] - 1
    half_slots = tile_refs[0].shape[0]
    unroll = widest_divisor(half_slots, 8)
    count, halves = half_counts(facts_ref, half_slots)

    @pl.loop(0, spare + 1)
    def _(block):
        total[block] = jnp.zeros(total.shape[1:], jnp.float32)

    for first, which in halves:
        live = jnp.clip(count - first, 0, half_slots)

        @pl.loop(0, (live + unroll - 1) // unroll)
        def _(group):
            products = []
            places = []
            for lane in range(unroll):
                index = group * unroll + lane
                slot = first + index
                places.append(jnp.where(slot < count, target_ref[slot], spare))
                products.append(matmul(unpack(tile_refs[which][index]), table[source_ref[slot]]))
            for place, product in zip(places, products):
                total[place] += product


def forward_kernel(share_blocks, facts_ref, row_ref, col_ref, own_ref, other_ref, table_ref, *refs):
    *out_refs, total = refs
    half_blocks = share_blocks // 2
    add_products(facts_ref, row_ref, col_ref, (own_ref, other_ref), table_ref, total, table_ref.shape[2])
    me = facts_ref[1]
    for place, out_ref in enumerate(out_refs):
        first = (me ^ (3 - place // 2)) * share_blocks + (place % 2) * half_blocks

        @pl.loop(0, half_blocks)
        def _(block):
            out_ref[block] = total[first + block].astype(out_ref.dtype)


def forward(facts, rows, cols, own, other, table, share_blocks, shares):
    blocks = share_blocks * shares
    width = table.shape[2]
    piece = jax.ShapeDtypeStruct((share_blocks // 2, BLOCK, width), jnp.bfloat16)
    return call(
        functools.partial(forward_kernel, share_blocks),
        "forward",
        [piece] * (2 * shares),
        [SMEM] * 3 + [VMEM] * 3,
        [VMEM] * (2 * shares),
        (facts, rows, cols, own, other, table),
        20,
        2 * rows.shape[0] * BLOCK * BLOCK * width,
        [pltpu.VMEM((blocks + 1, BLOCK, width), jnp.float32)],
    )


def load_pieces(facts_ref, piece_refs, table, sem, share_blocks):
    half_blocks = share_blocks // 2
    me = facts_ref[1]
    copies = []
    for place, piece_ref in enumerate(piece_refs):
        first = (me ^ (place // 2)) * share_blocks + (place % 2) * half_blocks
        copies.append(
            pltpu.make_async_copy(piece_ref, table.at[pl.ds(first, half_blocks)], sem.at[place])
        )
    for copy in copies:
        copy.start()
    return copies


def backward_kernel(share_blocks, facts_ref, row_ref, col_ref, own_ref, other_ref, *refs):
    *piece_refs, out_ref, total, table, sem = refs
    for copy in load_pieces(facts_ref, piece_refs, table, sem, share_blocks):
        copy.wait()
    add_products(facts_ref, col_ref, row_ref, (own_ref, other_ref), table, total, table.shape[2])
    pairs = out_ref.shape[1] // (2 * BLOCK)
    for pair in range(pairs):
        both = jnp.concatenate([total[2 * pair], total[2 * pair + 1]], axis=0)
        out_ref[:, pair * 2 * BLOCK : (pair + 1) * 2 * BLOCK] = both.T.astype(out_ref.dtype)


def backward(facts, rows, cols, own, other, pieces, share_blocks, in_blocks):
    width = pieces[0].shape[2]
    blocks = share_blocks * len(pieces) // 2
    return call(
        functools.partial(backward_kernel, share_blocks),
        "backward",
        jax.ShapeDtypeStruct((width, in_blocks * BLOCK), jnp.bfloat16),
        [SMEM] * 3 + [VMEM] * 2 + [ANY] * len(pieces),
        VMEM,
        (facts, rows, cols, own, other, *pieces),
        20,
        2 * rows.shape[0] * BLOCK * BLOCK * width,
        [
            pltpu.VMEM((in_blocks + 1, BLOCK, width), jnp.float32),
            pltpu.VMEM((blocks, BLOCK, width), jnp.bfloat16),
            pltpu.SemaphoreType.DMA((len(pieces),)),
        ],
    )


def outer_kernel(share_blocks, mine, facts_ref, row_ref, col_ref, *refs):
    if mine:
        added_ref, *refs = refs
    *operand_refs, out_ref, table, sem = refs
    chunks = table.shape[0]
    input_refs, piece_refs = operand_refs[:chunks], operand_refs[chunks:]
    pieces = len(piece_refs) // chunks
    copies = []
    for chunk in range(chunks):
        copies += load_pieces(
            facts_ref, piece_refs[chunk * pieces : (chunk + 1) * pieces], table.at[chunk], sem.at[chunk], share_blocks
        )
    for copy in copies:
        copy.wait()
    half_slots = out_ref.shape[0]
    unroll = widest_divisor(half_slots, 8)
    count, halves = half_counts(facts_ref, half_slots)
    first_slot = halves[0][0] if mine else halves[1][0]

    @pl.loop(0, half_slots // unroll)
    def _(group):
        first = group * unroll

        @pl.when(first_slot + first < count)
        def _():
            for lane in range(unroll):
                index = first + lane
                slot = first_slot + index
                row, col = row_ref[slot], col_ref[slot]
                product = matmul_nt(table[0, row], input_refs[0][col])
                for chunk in range(1, chunks):
                    product += matmul_nt(table[chunk, row], input_refs[chunk][col])
                packed = pack(product)
                if mine:
                    packed += added_ref[index].astype(jnp.float32)
                out_ref[index] = jnp.where(slot < count, packed, 0.0).astype(out_ref.dtype)

        @pl.when(first_slot + first >= count)
        def _():
            for lane in range(unroll):
                out_ref[first + lane] = jnp.zeros(out_ref.shape[1:], out_ref.dtype)


def outer(facts, rows, cols, inputs, pieces, share_blocks, half_slots, added=None):
    chunks = len(inputs)
    width = inputs[0].shape[2]
    flat = [piece for chunk in pieces for piece in chunk]
    mine = added is not None
    blocks = share_blocks * len(pieces[0]) // 2
    return call(
        functools.partial(outer_kernel, share_blocks, mine),
        "outer_own" if mine else "outer_other",
        jax.ShapeDtypeStruct((half_slots, HALF, 2 * BLOCK), jnp.bfloat16),
        [SMEM] * 3 + [VMEM] * (int(mine) + chunks) + [ANY] * len(flat),
        VMEM,
        (facts, rows, cols, *([added] if mine else []), *inputs, *flat),
        20,
        2 * half_slots * BLOCK * BLOCK * width * chunks,
        [
            pltpu.VMEM((chunks, blocks, BLOCK, width), jnp.bfloat16),
            pltpu.SemaphoreType.DMA((chunks, len(pieces[0]))),
        ],
    )


def transpose_kernel(unroll, own_ref, other_ref, own_out, other_out):
    row = lax.broadcasted_iota(jnp.int32, (BLOCK, BLOCK), 0)
    col = lax.broadcasted_iota(jnp.int32, (BLOCK, BLOCK), 1)
    unit = (row == col).astype(jnp.bfloat16)

    @pl.loop(0, own_ref.shape[0] // unroll)
    def _(group):
        for lane in range(unroll):
            index = group * unroll + lane
            for source, target in ((own_ref, own_out), (other_ref, other_out)):
                target[index] = pack(matmul_nt(unit, unpack(source[index]))).astype(jnp.bfloat16)


def transpose_tiles(own, other):
    shape = jax.ShapeDtypeStruct(own.shape, own.dtype)
    return call(
        functools.partial(transpose_kernel, widest_divisor(own.shape[0], 4)),
        "transpose_tiles",
        [shape, shape],
        [VMEM] * 2,
        [VMEM] * 2,
        (own, other),
        12,
        2 * own.size * BLOCK * 2,
    )


def unit_order():
    row = lax.broadcasted_iota(jnp.int32, (2 * BLOCK, 2 * BLOCK), 0)
    col = lax.broadcasted_iota(jnp.int32, (2 * BLOCK, 2 * BLOCK), 1)
    kept = (row & BLOCK) + 2 * (row & (HALF - 1)) + ((row >> 5) & 1)
    return (kept == col).astype(jnp.bfloat16)


def units_to_rows_kernel(grad_ref, select_ref, *out_refs):
    order = unit_order()
    for pair in range(out_refs[0].shape[0] // 2):
        lanes = grad_ref[:, pair * 2 * BLOCK : (pair + 1) * 2 * BLOCK]
        turned = matmul_nt(order, lanes).astype(jnp.bfloat16)
        for chunk, out_ref in enumerate(out_refs):
            picked = matmul(turned, select_ref[chunk]).astype(jnp.bfloat16)
            out_ref[2 * pair] = picked[:BLOCK]
            out_ref[2 * pair + 1] = picked[BLOCK:]


def units_to_rows(act_grad, select):
    chunks, tokens, width = select.shape
    blocks = act_grad.shape[1] // BLOCK
    shape = jax.ShapeDtypeStruct((blocks, BLOCK, width), jnp.bfloat16)
    return call(
        units_to_rows_kernel,
        "units_to_rows",
        [shape] * chunks,
        [VMEM] * 2,
        [VMEM] * chunks,
        (act_grad, select),
        12,
        2 * act_grad.size * 2 * BLOCK * 3,
    )


def rows_to_units_kernel(chunks, select_ref, *refs):
    *act_refs, out_ref = refs
    order = unit_order()
    halves = len(act_refs) // chunks
    half_blocks = act_refs[0].shape[0]
    blocks = half_blocks * halves

    def block_of(chunk, block):
        return act_refs[chunk * halves + block // half_blocks][block % half_blocks]

    for pair in range(blocks // 2):
        turned = 0.0
        for chunk in range(chunks):
            both = jnp.concatenate([block_of(chunk, 2 * pair), block_of(chunk, 2 * pair + 1)], axis=0)
            turned = turned + matmul_nt(select_ref[chunk], both)
        out_ref[:, pair * 2 * BLOCK : (pair + 1) * 2 * BLOCK] = matmul(
            turned.astype(jnp.bfloat16), order
        ).astype(out_ref.dtype)


def rows_to_units(select, acts):
    chunks, tokens, width = select.shape
    flat = [piece for chunk in acts for piece in chunk]
    units = sum(piece.shape[0] for piece in acts[0]) * BLOCK
    return call(
        functools.partial(rows_to_units_kernel, chunks),
        "rows_to_units",
        jax.ShapeDtypeStruct((tokens, units), jnp.bfloat16),
        [VMEM] * (1 + len(flat)),
        VMEM,
        (select, *flat),
        12,
        2 * tokens * units * 2 * BLOCK * 3,
    )


def gelu_kernel(*refs):
    grad_ref, *refs = refs
    ins, (grad_a, grad_b, act_a, act_b) = refs[:6], refs[6:]
    half_blocks = grad_a.shape[0]
    for half, (grad_out, act_out) in enumerate(((grad_a, act_a), (grad_b, act_b))):
        parts = ins[3 * half : 3 * half + 3]

        @pl.loop(0, half_blocks)
        def _(block):
            pre = sum(part[block].astype(jnp.float32) for part in parts)
            square = pre * pre
            inner = jnp.tanh(COEFF * (pre + CUBIC * square * pre))
            front = 0.5 * (1.0 + inner)
            act_out[block] = (front * pre).astype(act_out.dtype)
            slope = front + 0.5 * pre * (1.0 - inner * inner) * COEFF * (1.0 + 3.0 * CUBIC * square)
            upstream = grad_ref[half * half_blocks + block].astype(jnp.float32)
            grad_out[block] = (upstream * slope).astype(grad_out.dtype)


def gelu(upstream, parts):
    shape = jax.ShapeDtypeStruct(parts[0].shape, jnp.bfloat16)
    return call(
        gelu_kernel,
        "gelu",
        [shape] * 4,
        [VMEM] * 7,
        [VMEM] * 4,
        (upstream, *parts),
        12,
        upstream.size * 20,
    )


def token_select(tokens, rows):
    width = tokens // CHUNKS
    part = width // rows
    chunk = jnp.arange(CHUNKS)[:, None, None]
    token = jnp.arange(tokens)[None, :, None]
    lane = jnp.arange(width)[None, None, :]
    kept = (lane // part) * part * CHUNKS + chunk * part + lane % part
    return (kept == token).astype(jnp.bfloat16)


def local(inputs, weight_tiles, tile_rows, tile_cols, tile_counts, act_grad):
    tokens = inputs.shape[0]
    in_blocks = inputs.shape[1] // BLOCK
    shares = lax.axis_size("col")
    row_devices = lax.axis_size("row")
    dp_devices = lax.axis_size("dp")
    share = act_grad.shape[1]
    share_blocks = share // BLOCK
    slots = tile_rows.shape[2]
    half_slots = weight_tiles.shape[2]
    width = tokens // CHUNKS
    part = width // row_devices
    assert shares == 4 and dp_devices == 2 and share_blocks % 2 == 0
    rows = tile_rows.reshape(slots)
    cols = tile_cols.reshape(slots)
    facts = jnp.stack([tile_counts.reshape(()), lax.axis_index("col"), lax.axis_index("dp")]).astype(jnp.int32)

    def across(values, bit):
        return lax.ppermute(values, "col", [(place, place ^ bit) for place in range(shares)])

    def other_core(values):
        return lax.ppermute(values, "dp", [(0, 1), (1, 0)])

    stored = weight_tiles.reshape(half_slots, 4096)
    other = other_core(stored).reshape(half_slots, HALF, 2 * BLOCK)
    own = stored.reshape(half_slots, HALF, 2 * BLOCK)
    tables = inputs.reshape(row_devices, CHUNKS, part, in_blocks * BLOCK).transpose(1, 3, 0, 2)
    tables = tables.reshape(CHUNKS, in_blocks, BLOCK, width)
    tables = [tables[chunk] for chunk in range(CHUNKS)]
    select = token_select(tokens, row_devices)

    partials = [forward(facts, rows, cols, own, other, table, share_blocks, shares) for table in tables]
    own_t, other_t = transpose_tiles(own, other)
    upstream = units_to_rows(act_grad, select)

    grads, acts, input_parts = [], [], []
    for chunk in range(CHUNKS):
        far_a, far_b, y_a, y_b, x_a, x_b, own_a, own_b = partials[chunk]
        relay_a, relay_b = across(far_a, 1), across(far_b, 2)
        near_a, near_b = across(x_a, 1), across(y_b, 2)
        last_a = across(y_a + relay_a, 2)
        last_b = across(x_b + relay_b, 1)
        g_a, g_b, a_a, a_b = gelu(upstream[chunk], (own_a, near_a, last_a, own_b, near_b, last_b))
        acts.append((a_a, a_b))
        gx_a, gy_b = across(g_a, 1), across(g_b, 2)
        gx_b, gy_a = across(g_b, 1), across(g_a, 2)
        gd_a, gd_b = across(gx_a, 2), across(gy_b, 1)
        grads.append((g_a, g_b, gx_a, gx_b, gy_a, gy_b, gd_a, gd_b))

    activation = rows_to_units(select, acts)
    me_row = lax.axis_index("row")
    for chunk in range(CHUNKS):
        partial = backward(facts, rows, cols, own_t, other_t, grads[chunk], share_blocks, in_blocks)
        if row_devices == 4:
            pieces = partial.reshape(row_devices, part, in_blocks * BLOCK)
            total = lax.dynamic_index_in_dim(pieces, me_row, 0, keepdims=False).astype(jnp.float32)
            for shift in (2, 1, 3):
                piece = lax.dynamic_index_in_dim(pieces, (me_row + shift) % row_devices, 0, keepdims=False)
                moved = lax.ppermute(
                    piece, "row", [(place, (place + shift) % row_devices) for place in range(row_devices)]
                )
                total = total + moved.astype(jnp.float32)
            input_parts.append(total.astype(jnp.bfloat16))
        else:
            input_parts.append(lax.psum_scatter(partial, "row", scatter_dimension=0, tiled=True))
    input_grad = jnp.concatenate(input_parts, axis=0)

    for_other = outer(facts, rows, cols, tables, grads, share_blocks, half_slots)
    tile_sum = outer(facts, rows, cols, tables, grads, share_blocks, half_slots, other_core(for_other))
    tile_grads = tile_sum.reshape(1, 1, half_slots, 4096)
    return (activation, input_grad, tile_grads)


def solution(mesh):
    return jax.shard_map(
        local,
        mesh=mesh,
        in_specs=(
            P("dp", "col"),
            P("row", "col", "dp", None),
            P("row", "col", None),
            P("row", "col", None),
            P("row", "col"),
            P("dp", ("row", "col")),
        ),
        out_specs=(P("dp", ("row", "col")), P(("dp", "row"), "col"), P("row", "col", "dp", None)),
        check_vma=False,
    )
```

```python
import functools

import jax
import jax.numpy as jnp
from jax import lax
from jax.experimental import pallas as pl
from jax.experimental.pallas import tpu as pltpu
from jax.sharding import PartitionSpec as P

COEFF = 0.7978845608028654
CUBIC = 0.044715
BLOCK = 64
HALF = 32
CHUNKS = 2
ADD_UNROLL = 54
OUTER_UNROLL = 27
TURN_UNROLL = 27
PLAIN_UNROLL = 8
MIB = 1024 * 1024
VMEM = pl.BlockSpec(memory_space=pltpu.VMEM)
SMEM = pl.BlockSpec(memory_space=pltpu.SMEM)
ANY = pl.BlockSpec(memory_space=pl.ANY)
NT = (((1,), (1,)), ((), ()))


def widest_divisor(total, most):
    return max(divisor for divisor in range(1, most + 1) if total % divisor == 0)


def unpack(packed):
    return jnp.concatenate([packed[:, :BLOCK], packed[:, BLOCK:]], axis=0)


def pack(square):
    return jnp.concatenate([square[:HALF], square[HALF:]], axis=1)


def matmul(left, right):
    return jnp.dot(left, right, preferred_element_type=jnp.float32)


def matmul_nt(left, right):
    return lax.dot_general(left, right, NT, preferred_element_type=jnp.float32)


def call(kernel, name, out_shape, in_specs, out_specs, operands, mib, flops, scratch=(), **more):
    moved = sum(operand.size * operand.dtype.itemsize for operand in operands)
    moved += sum(leaf.size * leaf.dtype.itemsize for leaf in jax.tree.leaves(out_shape))
    return pl.pallas_call(
        kernel,
        out_shape=out_shape,
        in_specs=in_specs,
        out_specs=out_specs,
        scratch_shapes=list(scratch),
        name=name,
        compiler_params=pltpu.CompilerParams(vmem_limit_bytes=mib * MIB),
        cost_estimate=pl.CostEstimate(flops=flops, bytes_accessed=moved, transcendentals=0),
        **more,
    )(*operands)


def plain_loop(total, body):
    unroll = widest_divisor(total, PLAIN_UNROLL)

    @pl.loop(0, total // unroll)
    def _(group):
        for lane in range(unroll):
            body(group * unroll + lane)


def half_counts(facts_ref, half_slots):
    count, dp = facts_ref[0], facts_ref[2]
    own = dp * half_slots
    other = half_slots - own
    return count, ((own, 0), (other, 1))


def add_products(facts_ref, target_ref, source_ref, tile_refs, table, total, width):
    spare = total.shape[0] - 1
    half_slots = tile_refs[0].shape[0]
    unroll = widest_divisor(half_slots, ADD_UNROLL)
    count, halves = half_counts(facts_ref, half_slots)

    def clear(block):
        total[block] = jnp.zeros(total.shape[1:], jnp.float32)

    plain_loop(spare, clear)

    for first, which in halves:
        live = jnp.clip(count - first, 0, half_slots)

        @pl.loop(0, (live + unroll - 1) // unroll)
        def _(group):
            products = []
            places = []
            for lane in range(unroll):
                index = group * unroll + lane
                slot = first + index
                places.append(jnp.where(slot < count, target_ref[slot], spare))
                products.append(matmul(unpack(tile_refs[which][index]), table[source_ref[slot]]))
            for place, product in zip(places, products):
                total[place] += product


def forward_kernel(share_blocks, facts_ref, row_ref, col_ref, own_ref, other_ref, table_ref, *refs):
    along_x, along_y, own_a, own_b, relay_x, relay_y, total = refs
    half_blocks = share_blocks // 2
    add_products(facts_ref, row_ref, col_ref, (own_ref, other_ref), table_ref, total, table_ref.shape[2])
    me = facts_ref[1]
    for out_ref, share, half in (
        (along_x.at[0], 3, 0),
        (along_x.at[1], 1, 0),
        (along_y.at[0], 3, 1),
        (along_y.at[1], 2, 1),
        (own_a, 0, 0),
        (own_b, 0, 1),
        (relay_x, 1, 1),
        (relay_y, 2, 0),
    ):
        first = (me ^ share) * share_blocks + half * half_blocks

        def write(block, out_ref=out_ref, first=first):
            out_ref[block] = total[first + block].astype(out_ref.dtype)

        plain_loop(half_blocks, write)


def forward(facts, rows, cols, own, other, table, share_blocks, shares):
    blocks = share_blocks * shares
    width = table.shape[2]
    half = (share_blocks // 2, BLOCK, width)
    piece = jax.ShapeDtypeStruct(half, jnp.bfloat16)
    two = jax.ShapeDtypeStruct((2, *half), jnp.bfloat16)
    return call(
        functools.partial(forward_kernel, share_blocks),
        "forward",
        [two] * 2 + [piece] * 4,
        [SMEM] * 3 + [VMEM] * 3,
        [VMEM] * 6,
        (facts, rows, cols, own, other, table),
        20,
        2 * rows.shape[0] * BLOCK * BLOCK * width,
        [pltpu.VMEM((blocks + 1, BLOCK, width), jnp.float32)],
    )


def load_pieces(facts_ref, piece_refs, table, sem, share_blocks):
    half_blocks = share_blocks // 2
    me = facts_ref[1]
    places = ((0, 0, share_blocks), (1, 0, share_blocks), (2, 0, share_blocks))
    places += ((3, 0, half_blocks), (3, half_blocks, half_blocks))
    copies = []
    for number, (piece_ref, (share, start, length)) in enumerate(zip(piece_refs, places)):
        first = (me ^ share) * share_blocks + start
        copies.append(pltpu.make_async_copy(piece_ref, table.at[pl.ds(first, length)], sem.at[number]))
    for copy in copies:
        copy.start()
    return copies


def backward_kernel(share_blocks, facts_ref, row_ref, col_ref, own_ref, other_ref, *refs):
    *piece_refs, out_ref, total, table, sem = refs
    for copy in load_pieces(facts_ref, piece_refs, table, sem, share_blocks):
        copy.wait()
    add_products(facts_ref, col_ref, row_ref, (own_ref, other_ref), table, total, table.shape[2])
    pairs = out_ref.shape[1] // (2 * BLOCK)
    for pair in range(pairs):
        both = jnp.concatenate([total[2 * pair], total[2 * pair + 1]], axis=0)
        out_ref[:, pair * 2 * BLOCK : (pair + 1) * 2 * BLOCK] = both.T.astype(out_ref.dtype)


def backward(facts, rows, cols, own, other, pieces, share_blocks, in_blocks):
    width = pieces[0].shape[2]
    blocks = 4 * share_blocks
    return call(
        functools.partial(backward_kernel, share_blocks),
        "backward",
        jax.ShapeDtypeStruct((width, in_blocks * BLOCK), jnp.bfloat16),
        [SMEM] * 3 + [VMEM] * 2 + [ANY] * len(pieces),
        VMEM,
        (facts, rows, cols, own, other, *pieces),
        20,
        2 * rows.shape[0] * BLOCK * BLOCK * width,
        [
            pltpu.VMEM((in_blocks + 1, BLOCK, width), jnp.float32),
            pltpu.VMEM((blocks, BLOCK, width), jnp.bfloat16),
            pltpu.SemaphoreType.DMA((len(pieces),)),
        ],
    )


def outer_kernel(share_blocks, mine, facts_ref, row_ref, col_ref, *refs):
    if mine:
        added_ref, *refs = refs
    *operand_refs, out_ref, table, sem = refs
    chunks = table.shape[0]
    input_refs, piece_refs = operand_refs[:chunks], operand_refs[chunks:]
    pieces = len(piece_refs) // chunks
    copies = []
    for chunk in range(chunks):
        copies += load_pieces(
            facts_ref, piece_refs[chunk * pieces : (chunk + 1) * pieces], table.at[chunk], sem.at[chunk], share_blocks
        )
    for copy in copies:
        copy.wait()
    half_slots = out_ref.shape[0]
    unroll = widest_divisor(half_slots, OUTER_UNROLL)
    count, halves = half_counts(facts_ref, half_slots)
    first_slot = halves[0][0] if mine else halves[1][0]

    @pl.loop(0, half_slots // unroll)
    def _(group):
        first = group * unroll

        @pl.when(first_slot + first < count)
        def _():
            for lane in range(unroll):
                index = first + lane
                slot = first_slot + index
                row, col = row_ref[slot], col_ref[slot]
                product = matmul_nt(table[0, row], input_refs[0][col])
                for chunk in range(1, chunks):
                    product += matmul_nt(table[chunk, row], input_refs[chunk][col])
                packed = pack(product)
                if mine:
                    packed += added_ref[index].astype(jnp.float32)
                out_ref[index] = jnp.where(slot < count, packed, 0.0).astype(out_ref.dtype)

        @pl.when(first_slot + first >= count)
        def _():
            for lane in range(unroll):
                out_ref[first + lane] = jnp.zeros(out_ref.shape[1:], out_ref.dtype)


def outer(facts, rows, cols, inputs, pieces, share_blocks, half_slots, added=None):
    chunks = len(inputs)
    width = inputs[0].shape[2]
    flat = [piece for chunk in pieces for piece in chunk]
    mine = added is not None
    blocks = 4 * share_blocks
    return call(
        functools.partial(outer_kernel, share_blocks, mine),
        "outer_own" if mine else "outer_other",
        jax.ShapeDtypeStruct((half_slots, HALF, 2 * BLOCK), jnp.bfloat16),
        [SMEM] * 3 + [VMEM] * (int(mine) + chunks) + [ANY] * len(flat),
        VMEM,
        (facts, rows, cols, *([added] if mine else []), *inputs, *flat),
        20,
        2 * half_slots * BLOCK * BLOCK * width * chunks,
        [
            pltpu.VMEM((chunks, blocks, BLOCK, width), jnp.bfloat16),
            pltpu.SemaphoreType.DMA((chunks, len(pieces[0]))),
        ],
    )


def transpose_kernel(unroll, own_ref, other_ref, own_out, other_out):
    row = lax.broadcasted_iota(jnp.int32, (BLOCK, BLOCK), 0)
    col = lax.broadcasted_iota(jnp.int32, (BLOCK, BLOCK), 1)
    unit = (row == col).astype(jnp.bfloat16)

    @pl.loop(0, own_ref.shape[0] // unroll)
    def _(group):
        for lane in range(unroll):
            index = group * unroll + lane
            for source, target in ((own_ref, own_out), (other_ref, other_out)):
                target[index] = pack(matmul_nt(unit, unpack(source[index]))).astype(jnp.bfloat16)


def transpose_tiles(own, other):
    shape = jax.ShapeDtypeStruct(own.shape, own.dtype)
    return call(
        functools.partial(transpose_kernel, widest_divisor(own.shape[0], TURN_UNROLL)),
        "transpose_tiles",
        [shape, shape],
        [VMEM] * 2,
        [VMEM] * 2,
        (own, other),
        12,
        2 * own.size * BLOCK * 2,
    )


def unit_order():
    row = lax.broadcasted_iota(jnp.int32, (2 * BLOCK, 2 * BLOCK), 0)
    col = lax.broadcasted_iota(jnp.int32, (2 * BLOCK, 2 * BLOCK), 1)
    kept = (row & BLOCK) + 2 * (row & (HALF - 1)) + ((row >> 5) & 1)
    return (kept == col).astype(jnp.bfloat16)


def token_rows_kernel(reorder, values_ref, select_ref, *out_refs):
    row = lax.broadcasted_iota(jnp.int32, (2 * BLOCK, 2 * BLOCK), 0)
    col = lax.broadcasted_iota(jnp.int32, (2 * BLOCK, 2 * BLOCK), 1)
    order = unit_order() if reorder else (row == col).astype(jnp.bfloat16)
    for pair in range(out_refs[0].shape[0] // 2):
        lanes = values_ref[:, pair * 2 * BLOCK : (pair + 1) * 2 * BLOCK]
        turned = matmul_nt(order, lanes).astype(jnp.bfloat16)
        for chunk, out_ref in enumerate(out_refs):
            picked = matmul(turned, select_ref[chunk]).astype(jnp.bfloat16)
            out_ref[2 * pair] = picked[:BLOCK]
            out_ref[2 * pair + 1] = picked[BLOCK:]


def token_rows(values, select, reorder):
    chunks, tokens, width = select.shape
    blocks = values.shape[1] // BLOCK
    shape = jax.ShapeDtypeStruct((blocks, BLOCK, width), jnp.bfloat16)
    return call(
        functools.partial(token_rows_kernel, reorder),
        "units_to_rows" if reorder else "features_to_rows",
        [shape] * chunks,
        [VMEM] * 2,
        [VMEM] * chunks,
        (values, select),
        12,
        2 * values.size * 2 * BLOCK * 3,
    )


def rows_to_units_kernel(select_ref, *refs):
    *act_refs, out_ref = refs
    order = unit_order()
    for pair in range(act_refs[0].shape[0] // 2):
        turned = 0.0
        for chunk, act_ref in enumerate(act_refs):
            both = jnp.concatenate([act_ref[2 * pair], act_ref[2 * pair + 1]], axis=0)
            turned = turned + matmul_nt(select_ref[chunk], both)
        out_ref[:, pair * 2 * BLOCK : (pair + 1) * 2 * BLOCK] = matmul(
            turned.astype(jnp.bfloat16), order
        ).astype(out_ref.dtype)


def rows_to_units(select, acts):
    chunks, tokens, width = select.shape
    units = acts[0].shape[0] * BLOCK
    return call(
        rows_to_units_kernel,
        "rows_to_units",
        jax.ShapeDtypeStruct((tokens, units), jnp.bfloat16),
        [VMEM] * (1 + len(acts)),
        VMEM,
        (select, *acts),
        12,
        2 * tokens * units * 2 * BLOCK * 3,
    )


def gelu_kernel(upstream_ref, own_a, near_a, last_a, own_b, near_b, last_b, grad_out, act_out):
    half_blocks = own_a.shape[0]
    for half, (own, near, last) in enumerate(((own_a, near_a, last_a), (own_b, near_b, last_b))):

        def one(block, half=half, own=own, near=near, last=last):
            pre = own[block].astype(jnp.float32) + near[1, block].astype(jnp.float32)
            pre = pre + last[block].astype(jnp.float32)
            square = pre * pre
            inner = jnp.tanh(COEFF * (pre + CUBIC * square * pre))
            front = 0.5 * (1.0 + inner)
            place = half * half_blocks + block
            act_out[place] = (front * pre).astype(act_out.dtype)
            slope = front + 0.5 * pre * (1.0 - inner * inner) * COEFF * (1.0 + 3.0 * CUBIC * square)
            grad_out[place] = (upstream_ref[place].astype(jnp.float32) * slope).astype(grad_out.dtype)

        plain_loop(half_blocks, one)


def gelu(upstream, parts):
    shape = jax.ShapeDtypeStruct(upstream.shape, jnp.bfloat16)
    return call(
        gelu_kernel,
        "gelu",
        [shape] * 2,
        [VMEM] * 7,
        [VMEM] * 2,
        (upstream, *parts),
        12,
        upstream.size * 20,
    )


def token_select(tokens, rows):
    width = tokens // CHUNKS
    part = width // rows
    chunk = jnp.arange(CHUNKS)[:, None, None]
    token = jnp.arange(tokens)[None, :, None]
    lane = jnp.arange(width)[None, None, :]
    kept = (lane // part) * part * CHUNKS + chunk * part + lane % part
    return (kept == token).astype(jnp.bfloat16)


def local(inputs, weight_tiles, tile_rows, tile_cols, tile_counts, act_grad):
    tokens = inputs.shape[0]
    in_blocks = inputs.shape[1] // BLOCK
    shares = lax.axis_size("col")
    row_devices = lax.axis_size("row")
    dp_devices = lax.axis_size("dp")
    share = act_grad.shape[1]
    share_blocks = share // BLOCK
    slots = tile_rows.shape[2]
    half_slots = weight_tiles.shape[2]
    width = tokens // CHUNKS
    part = width // row_devices
    assert shares == 4 and dp_devices == 2 and share_blocks % 2 == 0
    rows = tile_rows.reshape(slots)
    cols = tile_cols.reshape(slots)
    facts = jnp.stack([tile_counts.reshape(()), lax.axis_index("col"), lax.axis_index("dp")]).astype(jnp.int32)

    def across(values, bit):
        return lax.ppermute(values, "col", [(place, place ^ bit) for place in range(shares)])

    def other_core(values):
        return lax.ppermute(values, "dp", [(0, 1), (1, 0)])

    stored = weight_tiles.reshape(half_slots, 4096)
    other = other_core(stored).reshape(half_slots, HALF, 2 * BLOCK)
    own = stored.reshape(half_slots, HALF, 2 * BLOCK)
    select = token_select(tokens, row_devices)
    tables = token_rows(inputs, select, False)

    partials = [forward(facts, rows, cols, own, other, table, share_blocks, shares) for table in tables]
    own_t, other_t = transpose_tiles(own, other)
    upstream = token_rows(act_grad, select, True)

    grads, acts = [], []
    for chunk in range(CHUNKS):
        along_x, along_y, own_a, own_b, relay_x, relay_y = partials[chunk]
        from_x, from_y = across(along_x, 1), across(along_y, 2)
        last_a = across(relay_y + from_x[0], 2)
        last_b = across(relay_x + from_y[0], 1)
        grad, act = gelu(upstream[chunk], (own_a, from_x, last_a, own_b, from_y, last_b))
        acts.append(act)
        grad_x, grad_y = across(grad, 1), across(grad, 2)
        far_a = across(grad_x[: share_blocks // 2], 2)
        far_b = across(grad_y[share_blocks // 2 :], 1)
        grads.append((grad, grad_x, grad_y, far_a, far_b))

    activation = rows_to_units(select, acts)
    input_parts = []
    me_row = lax.axis_index("row")
    for chunk in range(CHUNKS):
        partial = backward(facts, rows, cols, own_t, other_t, grads[chunk], share_blocks, in_blocks)
        if row_devices == 4:
            pieces = partial.reshape(row_devices, part, in_blocks * BLOCK)
            total = lax.dynamic_index_in_dim(pieces, me_row, 0, keepdims=False).astype(jnp.float32)
            for shift in (2, 1, 3):
                piece = lax.dynamic_index_in_dim(pieces, (me_row + shift) % row_devices, 0, keepdims=False)
                moved = lax.ppermute(
                    piece, "row", [(place, (place + shift) % row_devices) for place in range(row_devices)]
                )
                total = total + moved.astype(jnp.float32)
            input_parts.append(total.astype(jnp.bfloat16))
        else:
            input_parts.append(lax.psum_scatter(partial, "row", scatter_dimension=0, tiled=True))
    input_grad = jnp.concatenate(input_parts, axis=0)

    for_other = outer(facts, rows, cols, tables, grads, share_blocks, half_slots)
    tile_sum = outer(facts, rows, cols, tables, grads, share_blocks, half_slots, other_core(for_other))
    tile_grads = tile_sum.reshape(1, 1, half_slots, 4096)
    return (activation, input_grad, tile_grads)


def solution(mesh):
    return jax.shard_map(
        local,
        mesh=mesh,
        in_specs=(
            P("dp", "col"),
            P("row", "col", "dp", None),
            P("row", "col", None),
            P("row", "col", None),
            P("row", "col"),
            P("dp", ("row", "col")),
        ),
        out_specs=(P("dp", ("row", "col")), P(("dp", "row"), "col"), P("row", "col", "dp", None)),
        check_vma=False,
    )
```

```python
import functools

import jax
import jax.numpy as jnp
from jax import lax
from jax.experimental import pallas as pl
from jax.experimental.pallas import tpu as pltpu
from jax.sharding import PartitionSpec as P

COEFF = 0.7978845608028654
CUBIC = 0.044715
BLOCK = 64
HALF = 32
CHUNKS = 2
ADD_UNROLL = 54
OUTER_UNROLL = 27
TURN_UNROLL = 27
PLAIN_UNROLL = 8
FLOPS_PER_US = 1_150_000_000
MIB = 1024 * 1024
VMEM = pl.BlockSpec(memory_space=pltpu.VMEM)
SMEM = pl.BlockSpec(memory_space=pltpu.SMEM)
ANY = pl.BlockSpec(memory_space=pl.ANY)
NT = (((1,), (1,)), ((), ()))


def widest_divisor(total, most):
    return max(divisor for divisor in range(1, most + 1) if total % divisor == 0)


def unpack(packed):
    return jnp.concatenate([packed[:, :BLOCK], packed[:, BLOCK:]], axis=0)


def pack(square):
    return jnp.concatenate([square[:HALF], square[HALF:]], axis=1)


def matmul(left, right):
    return jnp.dot(left, right, preferred_element_type=jnp.float32)


def matmul_nt(left, right):
    return lax.dot_general(left, right, NT, preferred_element_type=jnp.float32)


def call(kernel, name, out_shape, in_specs, out_specs, operands, mib, microseconds, scratch=(), **more):
    moved = sum(operand.size * operand.dtype.itemsize for operand in operands)
    moved += sum(leaf.size * leaf.dtype.itemsize for leaf in jax.tree.leaves(out_shape))
    return pl.pallas_call(
        kernel,
        out_shape=out_shape,
        in_specs=in_specs,
        out_specs=out_specs,
        scratch_shapes=list(scratch),
        name=name,
        compiler_params=pltpu.CompilerParams(vmem_limit_bytes=mib * MIB),
        cost_estimate=pl.CostEstimate(flops=microseconds * FLOPS_PER_US, bytes_accessed=moved, transcendentals=0),
        **more,
    )(*operands)


def plain_loop(total, body):
    unroll = widest_divisor(total, PLAIN_UNROLL)

    @pl.loop(0, total // unroll)
    def _(group):
        for lane in range(unroll):
            body(group * unroll + lane)


def half_counts(facts_ref, half_slots):
    count, dp = facts_ref[0], facts_ref[2]
    own = dp * half_slots
    other = half_slots - own
    return count, ((own, 0), (other, 1))


def add_products(facts_ref, target_ref, source_ref, tile_refs, table, total, width):
    spare = total.shape[0] - 1
    half_slots = tile_refs[0].shape[0]
    unroll = widest_divisor(half_slots, ADD_UNROLL)
    count, halves = half_counts(facts_ref, half_slots)

    def clear(block):
        total[block] = jnp.zeros(total.shape[1:], jnp.float32)

    plain_loop(spare, clear)

    for first, which in halves:
        live = jnp.clip(count - first, 0, half_slots)

        @pl.loop(0, (live + unroll - 1) // unroll)
        def _(group):
            products = []
            places = []
            for lane in range(unroll):
                index = group * unroll + lane
                slot = first + index
                places.append(jnp.where(slot < count, target_ref[slot], spare))
                products.append(matmul(unpack(tile_refs[which][index]), table[source_ref[slot]]))
            for place, product in zip(places, products):
                total[place] += product


def forward_kernel(share_blocks, facts_ref, row_ref, col_ref, own_ref, other_ref, table_ref, *refs):
    along_x, along_y, own_a, own_b, relay_x, relay_y, total = refs
    half_blocks = share_blocks // 2
    add_products(facts_ref, row_ref, col_ref, (own_ref, other_ref), table_ref, total, table_ref.shape[2])
    me = facts_ref[1]
    for out_ref, share, half in (
        (along_x.at[0], 3, 0),
        (along_x.at[1], 1, 0),
        (along_y.at[0], 3, 1),
        (along_y.at[1], 2, 1),
        (own_a, 0, 0),
        (own_b, 0, 1),
        (relay_x, 1, 1),
        (relay_y, 2, 0),
    ):
        first = (me ^ share) * share_blocks + half * half_blocks

        def write(block, out_ref=out_ref, first=first):
            out_ref[block] = total[first + block].astype(out_ref.dtype)

        plain_loop(half_blocks, write)


def forward(facts, rows, cols, own, other, table, share_blocks, shares):
    blocks = share_blocks * shares
    width = table.shape[2]
    half = (share_blocks // 2, BLOCK, width)
    piece = jax.ShapeDtypeStruct(half, jnp.bfloat16)
    two = jax.ShapeDtypeStruct((2, *half), jnp.bfloat16)
    return call(
        functools.partial(forward_kernel, share_blocks),
        "forward",
        [two] * 2 + [piece] * 4,
        [SMEM] * 3 + [VMEM] * 3,
        [VMEM] * 6,
        (facts, rows, cols, own, other, table),
        20,
        7,
        [pltpu.VMEM((blocks + 1, BLOCK, width), jnp.float32)],
    )


def load_pieces(facts_ref, piece_refs, table, sem, share_blocks):
    half_blocks = share_blocks // 2
    me = facts_ref[1]
    places = ((0, 0, share_blocks), (1, 0, share_blocks), (2, 0, share_blocks))
    places += ((3, 0, half_blocks), (3, half_blocks, half_blocks))
    copies = []
    for number, (piece_ref, (share, start, length)) in enumerate(zip(piece_refs, places)):
        first = (me ^ share) * share_blocks + start
        copies.append(pltpu.make_async_copy(piece_ref, table.at[pl.ds(first, length)], sem.at[number]))
    for copy in copies:
        copy.start()
    return copies


def backward_kernel(share_blocks, facts_ref, row_ref, col_ref, own_ref, other_ref, *refs):
    *piece_refs, out_ref, total, table, sem = refs
    for copy in load_pieces(facts_ref, piece_refs, table, sem, share_blocks):
        copy.wait()
    add_products(facts_ref, col_ref, row_ref, (own_ref, other_ref), table, total, table.shape[2])
    pairs = out_ref.shape[1] // (2 * BLOCK)
    for pair in range(pairs):
        both = jnp.concatenate([total[2 * pair], total[2 * pair + 1]], axis=0)
        out_ref[:, pair * 2 * BLOCK : (pair + 1) * 2 * BLOCK] = both.T.astype(out_ref.dtype)


def backward(facts, rows, cols, own, other, pieces, share_blocks, in_blocks):
    width = pieces[0].shape[2]
    blocks = 4 * share_blocks
    return call(
        functools.partial(backward_kernel, share_blocks),
        "backward",
        jax.ShapeDtypeStruct((width, in_blocks * BLOCK), jnp.bfloat16),
        [SMEM] * 3 + [VMEM] * 2 + [ANY] * len(pieces),
        VMEM,
        (facts, rows, cols, own, other, *pieces),
        20,
        7,
        [
            pltpu.VMEM((in_blocks + 1, BLOCK, width), jnp.float32),
            pltpu.VMEM((blocks, BLOCK, width), jnp.bfloat16),
            pltpu.SemaphoreType.DMA((len(pieces),)),
        ],
    )


def outer_kernel(share_blocks, mine, adds, facts_ref, row_ref, col_ref, *refs):
    added_refs, (input_ref, *piece_refs) = refs[:adds], refs[adds:-3]
    out_ref, table, sem = refs[-3:]
    for copy in load_pieces(facts_ref, piece_refs, table, sem, share_blocks):
        copy.wait()
    half_slots = out_ref.shape[0]
    unroll = widest_divisor(half_slots, OUTER_UNROLL)
    count, halves = half_counts(facts_ref, half_slots)
    first_slot = halves[0][0] if mine else halves[1][0]

    @pl.loop(0, half_slots // unroll)
    def _(group):
        first = group * unroll

        @pl.when(first_slot + first < count)
        def _():
            for lane in range(unroll):
                index = first + lane
                slot = first_slot + index
                packed = pack(matmul_nt(table[row_ref[slot]], input_ref[col_ref[slot]]))
                for added_ref in added_refs:
                    packed += added_ref[index].astype(jnp.float32)
                out_ref[index] = jnp.where(slot < count, packed, 0.0).astype(out_ref.dtype)

        @pl.when(first_slot + first >= count)
        def _():
            for lane in range(unroll):
                out_ref[first + lane] = jnp.zeros(out_ref.shape[1:], out_ref.dtype)


def outer(facts, rows, cols, inputs, pieces, share_blocks, half_slots, mine, added):
    blocks = 4 * share_blocks
    return call(
        functools.partial(outer_kernel, share_blocks, mine, len(added)),
        "outer_own" if mine else "outer_other",
        jax.ShapeDtypeStruct((half_slots, HALF, 2 * BLOCK), jnp.bfloat16),
        [SMEM] * 3 + [VMEM] * (len(added) + 1) + [ANY] * len(pieces),
        VMEM,
        (facts, rows, cols, *added, inputs, *pieces),
        20,
        5,
        [
            pltpu.VMEM((blocks, BLOCK, inputs.shape[2]), jnp.bfloat16),
            pltpu.SemaphoreType.DMA((len(pieces),)),
        ],
    )


def transpose_kernel(unroll, own_ref, other_ref, own_out, other_out):
    row = lax.broadcasted_iota(jnp.int32, (BLOCK, BLOCK), 0)
    col = lax.broadcasted_iota(jnp.int32, (BLOCK, BLOCK), 1)
    unit = (row == col).astype(jnp.bfloat16)

    @pl.loop(0, own_ref.shape[0] // unroll)
    def _(group):
        for lane in range(unroll):
            index = group * unroll + lane
            for source, target in ((own_ref, own_out), (other_ref, other_out)):
                target[index] = pack(matmul_nt(unit, unpack(source[index]))).astype(jnp.bfloat16)


def transpose_tiles(own, other):
    shape = jax.ShapeDtypeStruct(own.shape, own.dtype)
    return call(
        functools.partial(transpose_kernel, widest_divisor(own.shape[0], TURN_UNROLL)),
        "transpose_tiles",
        [shape, shape],
        [VMEM] * 2,
        [VMEM] * 2,
        (own, other),
        12,
        7,
    )


def unit_order():
    row = lax.broadcasted_iota(jnp.int32, (2 * BLOCK, 2 * BLOCK), 0)
    col = lax.broadcasted_iota(jnp.int32, (2 * BLOCK, 2 * BLOCK), 1)
    kept = (row & BLOCK) + 2 * (row & (HALF - 1)) + ((row >> 5) & 1)
    return (kept == col).astype(jnp.bfloat16)


def token_rows_kernel(reorder, values_ref, select_ref, *out_refs):
    row = lax.broadcasted_iota(jnp.int32, (2 * BLOCK, 2 * BLOCK), 0)
    col = lax.broadcasted_iota(jnp.int32, (2 * BLOCK, 2 * BLOCK), 1)
    order = unit_order() if reorder else (row == col).astype(jnp.bfloat16)
    for pair in range(out_refs[0].shape[0] // 2):
        lanes = values_ref[:, pair * 2 * BLOCK : (pair + 1) * 2 * BLOCK]
        turned = matmul_nt(order, lanes).astype(jnp.bfloat16)
        for chunk, out_ref in enumerate(out_refs):
            picked = matmul(turned, select_ref[chunk]).astype(jnp.bfloat16)
            out_ref[2 * pair] = picked[:BLOCK]
            out_ref[2 * pair + 1] = picked[BLOCK:]


def token_rows(values, select, reorder):
    chunks, tokens, width = select.shape
    blocks = values.shape[1] // BLOCK
    shape = jax.ShapeDtypeStruct((blocks, BLOCK, width), jnp.bfloat16)
    return call(
        functools.partial(token_rows_kernel, reorder),
        "units_to_rows" if reorder else "features_to_rows",
        [shape] * chunks,
        [VMEM] * 2,
        [VMEM] * chunks,
        (values, select),
        12,
        5,
    )


def rows_to_units_kernel(select_ref, *refs):
    *act_refs, out_ref = refs
    order = unit_order()
    for pair in range(act_refs[0].shape[0] // 2):
        turned = 0.0
        for chunk, act_ref in enumerate(act_refs):
            both = jnp.concatenate([act_ref[2 * pair], act_ref[2 * pair + 1]], axis=0)
            turned = turned + matmul_nt(select_ref[chunk], both)
        out_ref[:, pair * 2 * BLOCK : (pair + 1) * 2 * BLOCK] = matmul(
            turned.astype(jnp.bfloat16), order
        ).astype(out_ref.dtype)


def rows_to_units(select, acts):
    chunks, tokens, width = select.shape
    units = acts[0].shape[0] * BLOCK
    return call(
        rows_to_units_kernel,
        "rows_to_units",
        jax.ShapeDtypeStruct((tokens, units), jnp.bfloat16),
        [VMEM] * (1 + len(acts)),
        VMEM,
        (select, *acts),
        12,
        6,
    )


def gelu_kernel(upstream_ref, own_a, near_a, last_a, own_b, near_b, last_b, grad_out, act_out):
    half_blocks = own_a.shape[0]
    for half, (own, near, last) in enumerate(((own_a, near_a, last_a), (own_b, near_b, last_b))):

        def one(block, half=half, own=own, near=near, last=last):
            pre = own[block].astype(jnp.float32) + near[1, block].astype(jnp.float32)
            pre = pre + last[block].astype(jnp.float32)
            square = pre * pre
            inner = jnp.tanh(COEFF * (pre + CUBIC * square * pre))
            front = 0.5 * (1.0 + inner)
            place = half * half_blocks + block
            act_out[place] = (front * pre).astype(act_out.dtype)
            slope = front + 0.5 * pre * (1.0 - inner * inner) * COEFF * (1.0 + 3.0 * CUBIC * square)
            grad_out[place] = (upstream_ref[place].astype(jnp.float32) * slope).astype(grad_out.dtype)

        plain_loop(half_blocks, one)


def gelu(upstream, parts):
    shape = jax.ShapeDtypeStruct(upstream.shape, jnp.bfloat16)
    return call(
        gelu_kernel,
        "gelu",
        [shape] * 2,
        [VMEM] * 7,
        [VMEM] * 2,
        (upstream, *parts),
        12,
        2,
    )


def after(value, earlier):
    return lax.optimization_barrier((value, earlier))[0]


def token_select(tokens, rows):
    width = tokens // CHUNKS
    part = width // rows
    chunk = jnp.arange(CHUNKS)[:, None, None]
    token = jnp.arange(tokens)[None, :, None]
    lane = jnp.arange(width)[None, None, :]
    kept = (lane // part) * part * CHUNKS + chunk * part + lane % part
    return (kept == token).astype(jnp.bfloat16)


def local(inputs, weight_tiles, tile_rows, tile_cols, tile_counts, act_grad):
    tokens = inputs.shape[0]
    in_blocks = inputs.shape[1] // BLOCK
    shares = lax.axis_size("col")
    row_devices = lax.axis_size("row")
    dp_devices = lax.axis_size("dp")
    share = act_grad.shape[1]
    share_blocks = share // BLOCK
    slots = tile_rows.shape[2]
    half_slots = weight_tiles.shape[2]
    width = tokens // CHUNKS
    part = width // row_devices
    assert shares == 4 and dp_devices == 2 and share_blocks % 2 == 0
    rows = tile_rows.reshape(slots)
    cols = tile_cols.reshape(slots)
    facts = jnp.stack([tile_counts.reshape(()), lax.axis_index("col"), lax.axis_index("dp")]).astype(jnp.int32)

    def across(values, bit):
        return lax.ppermute(values, "col", [(place, place ^ bit) for place in range(shares)])

    def other_core(values):
        return lax.ppermute(values, "dp", [(0, 1), (1, 0)])

    own = weight_tiles.reshape(half_slots, HALF, 2 * BLOCK)
    other = other_core(own)
    select = token_select(tokens, row_devices)
    tables = token_rows(inputs, select, False)

    partials = [forward(facts, rows, cols, own, other, table, share_blocks, shares) for table in tables]
    upstream = list(token_rows(act_grad, after(select, partials[1][2]), True))
    own_t, other_t = transpose_tiles(after(own, upstream[1]), after(other, upstream[1]))
    upstream[0] = after(upstream[0], own_t)

    grads, acts = [], []
    for chunk in range(CHUNKS):
        along_x, along_y, own_a, own_b, relay_x, relay_y = partials[chunk]
        from_x, from_y = across(along_x, 1), across(along_y, 2)
        last_a = across(relay_y + from_x[0], 2)
        last_b = across(relay_x + from_y[0], 1)
        grad, act = gelu(upstream[chunk], (own_a, from_x, last_a, own_b, from_y, last_b))
        acts.append(act)
        grads.append([grad, across(grad, 1), across(grad, 2)])

    activation = rows_to_units(select, acts)
    grads[0][1] = after(grads[0][1], activation)
    for chunk in range(CHUNKS):
        grad, grad_x, grad_y = grads[chunk]
        far_a = across(grad_x[: share_blocks // 2], 2)
        far_b = across(grad_y[share_blocks // 2 :], 1)
        grads[chunk] += [far_a, far_b]

    me_row = lax.axis_index("row")

    def to_rows(partial):
        pieces = partial.reshape(row_devices, part, in_blocks * BLOCK)
        mine = lax.dynamic_index_in_dim(pieces, me_row, 0, keepdims=False)
        if row_devices != 4:
            return [lax.psum_scatter(partial, "row", scatter_dimension=0, tiled=True)]
        moved = []
        for shift in (2, 1, 3):
            piece = lax.dynamic_index_in_dim(pieces, (me_row + shift) % row_devices, 0, keepdims=False)
            pairs = [(place, (place + shift) % row_devices) for place in range(row_devices)]
            moved.append(lax.ppermute(piece, "row", pairs))
        return [mine] + moved

    def add_up(parts, earlier):
        parts = [after(parts[0], earlier)] + parts[1:]
        return sum(part.astype(jnp.float32) for part in parts).astype(jnp.bfloat16)

    def input_sums(chunk):
        return backward(facts, rows, cols, own_t, other_t, grads[chunk], share_blocks, in_blocks)

    def tile_part(chunk, earlier, mine, added):
        table = after(tables[chunk], earlier)
        return outer(facts, rows, cols, table, grads[chunk], share_blocks, half_slots, mine, added)

    first = input_sums(0)
    row_parts = to_rows(first)
    other_first = tile_part(0, first, False, [])
    grads[1][3] = after(grads[1][3], other_first)
    second = input_sums(1)
    first_sum = add_up(row_parts, second)
    row_parts = to_rows(second)
    other_second = tile_part(1, first_sum, False, [])
    own_first = tile_part(0, other_second, True, [other_core(other_first)])
    own_second = tile_part(1, other_second, True, [own_first, other_core(other_second)])
    second_sum = add_up(row_parts, own_second)
    input_grad = jnp.concatenate([first_sum, second_sum], axis=0)
    tile_grads = own_second.reshape(1, 1, half_slots, 4096)
    return (activation, input_grad, tile_grads)


def solution(mesh):
    return jax.shard_map(
        local,
        mesh=mesh,
        in_specs=(
            P("dp", "col"),
            P("row", "col", "dp", None),
            P("row", "col", None),
            P("row", "col", None),
            P("row", "col"),
            P("dp", ("row", "col")),
        ),
        out_specs=(P("dp", ("row", "col")), P(("dp", "row"), "col"), P("row", "col", "dp", None)),
        check_vma=False,
    )
```

```python
import functools

import jax
import jax.numpy as jnp
from jax import lax
from jax.experimental import pallas as pl
from jax.experimental.pallas import tpu as pltpu
from jax.sharding import PartitionSpec as P

COEFF = 0.7978845608028654
CUBIC = 0.044715
BLOCK = 64
HALF = 32
CHUNKS = 2
ADD_UNROLL = 54
OUTER_UNROLL = 27
TURN_UNROLL = 27
PLAIN_UNROLL = 8
FLOPS_PER_US = 1_150_000_000
MIB = 1024 * 1024
VMEM = pl.BlockSpec(memory_space=pltpu.VMEM)
SMEM = pl.BlockSpec(memory_space=pltpu.SMEM)
ANY = pl.BlockSpec(memory_space=pl.ANY)
NT = (((1,), (1,)), ((), ()))


def widest_divisor(total, most):
    return max(divisor for divisor in range(1, most + 1) if total % divisor == 0)


def unpack(packed):
    return jnp.concatenate([packed[:, :BLOCK], packed[:, BLOCK:]], axis=0)


def pack(square):
    return jnp.concatenate([square[:HALF], square[HALF:]], axis=1)


def matmul(left, right):
    return jnp.dot(left, right, preferred_element_type=jnp.float32)


def matmul_nt(left, right):
    return lax.dot_general(left, right, NT, preferred_element_type=jnp.float32)


def call(kernel, name, out_shape, in_specs, out_specs, operands, mib, microseconds, scratch=(), **more):
    moved = sum(operand.size * operand.dtype.itemsize for operand in operands)
    moved += sum(leaf.size * leaf.dtype.itemsize for leaf in jax.tree.leaves(out_shape))
    return pl.pallas_call(
        kernel,
        out_shape=out_shape,
        in_specs=in_specs,
        out_specs=out_specs,
        scratch_shapes=list(scratch),
        name=name,
        compiler_params=pltpu.CompilerParams(vmem_limit_bytes=mib * MIB),
        cost_estimate=pl.CostEstimate(
            flops=microseconds * FLOPS_PER_US, bytes_accessed=moved if microseconds else 0, transcendentals=0
        ),
        **more,
    )(*operands)


def plain_loop(total, body):
    unroll = widest_divisor(total, PLAIN_UNROLL)

    @pl.loop(0, total // unroll)
    def _(group):
        for lane in range(unroll):
            body(group * unroll + lane)


def half_counts(facts_ref, half_slots):
    count, dp = facts_ref[0], facts_ref[2]
    own = dp * half_slots
    other = half_slots - own
    return count, ((own, 0), (other, 1))


def add_products(facts_ref, target_ref, source_ref, tile_refs, table, total, width):
    spare = total.shape[0] - 1
    half_slots = tile_refs[0].shape[0]
    unroll = widest_divisor(half_slots, ADD_UNROLL)
    count, halves = half_counts(facts_ref, half_slots)

    def clear(block):
        total[block] = jnp.zeros(total.shape[1:], jnp.float32)

    plain_loop(spare, clear)

    for first, which in halves:
        live = jnp.clip(count - first, 0, half_slots)

        @pl.loop(0, (live + unroll - 1) // unroll)
        def _(group):
            products = []
            places = []
            for lane in range(unroll):
                index = group * unroll + lane
                slot = first + index
                places.append(jnp.where(slot < count, target_ref[slot], spare))
                products.append(matmul(unpack(tile_refs[which][index]), table[source_ref[slot]]))
            for place, product in zip(places, products):
                total[place] += product


def forward_kernel(share_blocks, facts_ref, row_ref, col_ref, own_ref, other_ref, table_ref, *refs):
    along_x, along_y, own_a, own_b, relay_x, relay_y, total = refs
    half_blocks = share_blocks // 2
    add_products(facts_ref, row_ref, col_ref, (own_ref, other_ref), table_ref, total, table_ref.shape[2])
    me = facts_ref[1]
    for out_ref, share, half in (
        (along_x.at[0], 3, 0),
        (along_x.at[1], 1, 0),
        (along_y.at[0], 3, 1),
        (along_y.at[1], 2, 1),
        (own_a, 0, 0),
        (own_b, 0, 1),
        (relay_x, 1, 1),
        (relay_y, 2, 0),
    ):
        first = (me ^ share) * share_blocks + half * half_blocks

        def write(block, out_ref=out_ref, first=first):
            out_ref[block] = total[first + block].astype(out_ref.dtype)

        plain_loop(half_blocks, write)


def forward(facts, rows, cols, own, other, table, share_blocks, shares):
    blocks = share_blocks * shares
    width = table.shape[2]
    half = (share_blocks // 2, BLOCK, width)
    piece = jax.ShapeDtypeStruct(half, jnp.bfloat16)
    two = jax.ShapeDtypeStruct((2, *half), jnp.bfloat16)
    return call(
        functools.partial(forward_kernel, share_blocks),
        "forward",
        [two] * 2 + [piece] * 4,
        [SMEM] * 3 + [VMEM] * 3,
        [VMEM] * 6,
        (facts, rows, cols, own, other, table),
        20,
        7,
        [pltpu.VMEM((blocks + 1, BLOCK, width), jnp.float32)],
    )


def load_pieces(facts_ref, piece_refs, table, sem, share_blocks):
    half_blocks = share_blocks // 2
    me = facts_ref[1]
    places = ((0, 0, share_blocks), (1, 0, share_blocks), (2, 0, share_blocks))
    places += ((3, 0, half_blocks), (3, half_blocks, half_blocks))
    copies = []
    for number, (piece_ref, (share, start, length)) in enumerate(zip(piece_refs, places)):
        first = (me ^ share) * share_blocks + start
        copies.append(pltpu.make_async_copy(piece_ref, table.at[pl.ds(first, length)], sem.at[number]))
    for copy in copies:
        copy.start()
    return copies


def backward_kernel(share_blocks, facts_ref, row_ref, col_ref, own_ref, other_ref, *refs):
    *piece_refs, out_ref, total, table, sem = refs
    for copy in load_pieces(facts_ref, piece_refs, table, sem, share_blocks):
        copy.wait()
    add_products(facts_ref, col_ref, row_ref, (own_ref, other_ref), table, total, table.shape[2])
    pairs = out_ref.shape[1] // (2 * BLOCK)
    for pair in range(pairs):
        both = jnp.concatenate([total[2 * pair], total[2 * pair + 1]], axis=0)
        out_ref[:, pair * 2 * BLOCK : (pair + 1) * 2 * BLOCK] = both.T.astype(out_ref.dtype)


def backward(facts, rows, cols, own, other, pieces, share_blocks, in_blocks):
    width = pieces[0].shape[2]
    blocks = 4 * share_blocks
    return call(
        functools.partial(backward_kernel, share_blocks),
        "backward",
        jax.ShapeDtypeStruct((width, in_blocks * BLOCK), jnp.bfloat16),
        [SMEM] * 3 + [VMEM] * 2 + [ANY] * len(pieces),
        VMEM,
        (facts, rows, cols, own, other, *pieces),
        20,
        7,
        [
            pltpu.VMEM((in_blocks + 1, BLOCK, width), jnp.float32),
            pltpu.VMEM((blocks, BLOCK, width), jnp.bfloat16),
            pltpu.SemaphoreType.DMA((len(pieces),)),
        ],
    )


def outer_kernel(share_blocks, mine, adds, facts_ref, row_ref, col_ref, *refs):
    added_refs, (input_ref, *piece_refs) = refs[:adds], refs[adds:-3]
    out_ref, table, sem = refs[-3:]
    for copy in load_pieces(facts_ref, piece_refs, table, sem, share_blocks):
        copy.wait()
    half_slots = out_ref.shape[0]
    unroll = widest_divisor(half_slots, OUTER_UNROLL)
    count, halves = half_counts(facts_ref, half_slots)
    first_slot = halves[0][0] if mine else halves[1][0]

    @pl.loop(0, half_slots // unroll)
    def _(group):
        first = group * unroll

        @pl.when(first_slot + first < count)
        def _():
            for lane in range(unroll):
                index = first + lane
                slot = first_slot + index
                packed = pack(matmul_nt(table[row_ref[slot]], input_ref[col_ref[slot]]))
                for added_ref in added_refs:
                    packed += added_ref[index].astype(jnp.float32)
                out_ref[index] = jnp.where(slot < count, packed, 0.0).astype(out_ref.dtype)

        @pl.when(first_slot + first >= count)
        def _():
            for lane in range(unroll):
                out_ref[first + lane] = jnp.zeros(out_ref.shape[1:], out_ref.dtype)


def outer(facts, rows, cols, inputs, pieces, share_blocks, half_slots, mine, added):
    blocks = 4 * share_blocks
    return call(
        functools.partial(outer_kernel, share_blocks, mine, len(added)),
        "outer_own" if mine else "outer_other",
        jax.ShapeDtypeStruct((half_slots, HALF, 2 * BLOCK), jnp.bfloat16),
        [SMEM] * 3 + [VMEM] * (len(added) + 1) + [ANY] * len(pieces),
        VMEM,
        (facts, rows, cols, *added, inputs, *pieces),
        20,
        5,
        [
            pltpu.VMEM((blocks, BLOCK, inputs.shape[2]), jnp.bfloat16),
            pltpu.SemaphoreType.DMA((len(pieces),)),
        ],
    )


def transpose_kernel(unroll, own_ref, other_ref, own_out, other_out):
    row = lax.broadcasted_iota(jnp.int32, (BLOCK, BLOCK), 0)
    col = lax.broadcasted_iota(jnp.int32, (BLOCK, BLOCK), 1)
    unit = (row == col).astype(jnp.bfloat16)

    @pl.loop(0, own_ref.shape[0] // unroll)
    def _(group):
        for lane in range(unroll):
            index = group * unroll + lane
            for source, target in ((own_ref, own_out), (other_ref, other_out)):
                target[index] = pack(matmul_nt(unit, unpack(source[index]))).astype(jnp.bfloat16)


def transpose_tiles(own, other):
    shape = jax.ShapeDtypeStruct(own.shape, own.dtype)
    return call(
        functools.partial(transpose_kernel, widest_divisor(own.shape[0], TURN_UNROLL)),
        "transpose_tiles",
        [shape, shape],
        [VMEM] * 2,
        [VMEM] * 2,
        (own, other),
        12,
        7,
    )


def unit_order():
    row = lax.broadcasted_iota(jnp.int32, (2 * BLOCK, 2 * BLOCK), 0)
    col = lax.broadcasted_iota(jnp.int32, (2 * BLOCK, 2 * BLOCK), 1)
    kept = (row & BLOCK) + 2 * (row & (HALF - 1)) + ((row >> 5) & 1)
    return (kept == col).astype(jnp.bfloat16)


def token_rows_kernel(reorder, values_ref, select_ref, *out_refs):
    row = lax.broadcasted_iota(jnp.int32, (2 * BLOCK, 2 * BLOCK), 0)
    col = lax.broadcasted_iota(jnp.int32, (2 * BLOCK, 2 * BLOCK), 1)
    order = unit_order() if reorder else (row == col).astype(jnp.bfloat16)
    for pair in range(out_refs[0].shape[0] // 2):
        lanes = values_ref[:, pair * 2 * BLOCK : (pair + 1) * 2 * BLOCK]
        turned = matmul_nt(order, lanes).astype(jnp.bfloat16)
        for chunk, out_ref in enumerate(out_refs):
            picked = matmul(turned, select_ref[chunk]).astype(jnp.bfloat16)
            out_ref[2 * pair] = picked[:BLOCK]
            out_ref[2 * pair + 1] = picked[BLOCK:]


def token_rows(values, select, reorder):
    chunks, tokens, width = select.shape
    blocks = values.shape[1] // BLOCK
    shape = jax.ShapeDtypeStruct((blocks, BLOCK, width), jnp.bfloat16)
    return call(
        functools.partial(token_rows_kernel, reorder),
        "units_to_rows" if reorder else "features_to_rows",
        [shape] * chunks,
        [VMEM] * 2,
        [VMEM] * chunks,
        (values, select),
        12,
        5,
    )


def rows_to_units_kernel(select_ref, *refs):
    *act_refs, out_ref = refs
    order = unit_order()
    for pair in range(act_refs[0].shape[0] // 2):
        turned = 0.0
        for chunk, act_ref in enumerate(act_refs):
            both = jnp.concatenate([act_ref[2 * pair], act_ref[2 * pair + 1]], axis=0)
            turned = turned + matmul_nt(select_ref[chunk], both)
        out_ref[:, pair * 2 * BLOCK : (pair + 1) * 2 * BLOCK] = matmul(
            turned.astype(jnp.bfloat16), order
        ).astype(out_ref.dtype)


def rows_to_units(select, acts):
    chunks, tokens, width = select.shape
    units = acts[0].shape[0] * BLOCK
    return call(
        rows_to_units_kernel,
        "rows_to_units",
        jax.ShapeDtypeStruct((tokens, units), jnp.bfloat16),
        [VMEM] * (1 + len(acts)),
        VMEM,
        (select, *acts),
        12,
        6,
    )


def gelu_kernel(upstream_ref, own_a, near_a, last_a, own_b, near_b, last_b, grad_out, act_out):
    half_blocks = own_a.shape[0]
    for half, (own, near, last) in enumerate(((own_a, near_a, last_a), (own_b, near_b, last_b))):

        def one(block, half=half, own=own, near=near, last=last):
            pre = own[block].astype(jnp.float32) + near[1, block].astype(jnp.float32)
            pre = pre + last[block].astype(jnp.float32)
            square = pre * pre
            inner = jnp.tanh(COEFF * (pre + CUBIC * square * pre))
            front = 0.5 * (1.0 + inner)
            place = half * half_blocks + block
            act_out[place] = (front * pre).astype(act_out.dtype)
            slope = front + 0.5 * pre * (1.0 - inner * inner) * COEFF * (1.0 + 3.0 * CUBIC * square)
            grad_out[place] = (upstream_ref[place].astype(jnp.float32) * slope).astype(grad_out.dtype)

        plain_loop(half_blocks, one)


def gelu(upstream, parts):
    shape = jax.ShapeDtypeStruct(upstream.shape, jnp.bfloat16)
    return call(
        gelu_kernel,
        "gelu",
        [shape] * 2,
        [VMEM] * 7,
        [VMEM] * 2,
        (upstream, *parts),
        12,
        2,
    )


def after(value, earlier):
    return lax.optimization_barrier((value, earlier))[0]


def token_select(tokens, rows):
    width = tokens // CHUNKS
    part = width // rows
    chunk = jnp.arange(CHUNKS)[:, None, None]
    token = jnp.arange(tokens)[None, :, None]
    lane = jnp.arange(width)[None, None, :]
    kept = (lane // part) * part * CHUNKS + chunk * part + lane % part
    return (kept == token).astype(jnp.bfloat16)


def local(inputs, weight_tiles, tile_rows, tile_cols, tile_counts, act_grad):
    tokens = inputs.shape[0]
    in_blocks = inputs.shape[1] // BLOCK
    shares = lax.axis_size("col")
    row_devices = lax.axis_size("row")
    dp_devices = lax.axis_size("dp")
    share = act_grad.shape[1]
    share_blocks = share // BLOCK
    slots = tile_rows.shape[2]
    half_slots = weight_tiles.shape[2]
    width = tokens // CHUNKS
    part = width // row_devices
    assert shares == 4 and dp_devices == 2 and share_blocks % 2 == 0
    rows = tile_rows.reshape(slots)
    cols = tile_cols.reshape(slots)
    facts = jnp.stack([tile_counts.reshape(()), lax.axis_index("col"), lax.axis_index("dp")]).astype(jnp.int32)

    def across(values, bit):
        return lax.ppermute(values, "col", [(place, place ^ bit) for place in range(shares)])

    def other_core(values):
        return lax.ppermute(values, "dp", [(0, 1), (1, 0)])

    own = weight_tiles.reshape(half_slots, HALF, 2 * BLOCK)
    other = other_core(own)
    select = token_select(tokens, row_devices)
    tables = token_rows(inputs, select, False)

    partials = [forward(facts, rows, cols, own, other, table, share_blocks, shares) for table in tables]
    upstream = list(token_rows(act_grad, after(select, partials[1][2]), True))
    own_t, other_t = transpose_tiles(after(own, upstream[1]), after(other, upstream[1]))
    upstream[0] = after(upstream[0], own_t)

    grads, acts = [], []
    from_x = from_y = None
    for chunk in range(CHUNKS):
        along_x, along_y, own_a, own_b, relay_x, relay_y = partials[chunk]
        if chunk:
            along_x, along_y = after(along_x, from_x), after(along_y, from_y)
        from_x, from_y = across(along_x, 1), across(along_y, 2)
        sum_y, sum_x = relay_y + from_x[0], relay_x + from_y[0]
        if chunk:
            sum_y, sum_x = after(sum_y, grads[0][1]), after(sum_x, grads[0][2])
        last_a, last_b = across(sum_y, 2), across(sum_x, 1)
        grad, act = gelu(upstream[chunk], (own_a, from_x, last_a, own_b, from_y, last_b))
        acts.append(act)
        grads.append([grad, across(grad, 1), across(grad, 2)])

    for chunk in range(CHUNKS):
        grad, grad_x, grad_y = grads[chunk]
        far_a = across(grad_x[: share_blocks // 2], 2)
        far_b = across(grad_y[share_blocks // 2 :], 1)
        grads[chunk] += [far_a, far_b]

    me_row = lax.axis_index("row")

    def take(values, index):
        return lax.dynamic_index_in_dim(values, index, 0, keepdims=False)

    def to_rows(partial):
        if row_devices != 4:
            return [lax.psum_scatter(partial, "row", scatter_dimension=0, tiled=True)], partial, partial
        low, high = me_row & 1, me_row >> 1
        pieces = partial.reshape(2, 2, part, in_blocks * BLOCK)
        sent, kept = (lax.dynamic_index_in_dim(pieces, bit, 1, keepdims=False) for bit in (1 - low, low))
        moved = lax.ppermute(sent, "row", [(place, place ^ 1) for place in range(4)])
        both = take(kept, 1 - high).astype(jnp.float32) + take(moved, 1 - high).astype(jnp.float32)
        last = lax.ppermute(both.astype(jnp.bfloat16), "row", [(place, place ^ 2) for place in range(4)])
        return [last, take(kept, high), take(moved, high)], both, sent

    def add_up(parts, earlier):
        parts = [*parts[:-1], after(parts[-1], earlier)]
        return sum(part.astype(jnp.float32) for part in parts).astype(jnp.bfloat16)

    def input_sums(chunk):
        return backward(facts, rows, cols, own_t, other_t, grads[chunk], share_blocks, in_blocks)

    def tile_part(chunk, earlier, mine, added):
        table = after(tables[chunk], earlier)
        return outer(facts, rows, cols, table, grads[chunk], share_blocks, half_slots, mine, added)

    first = input_sums(0)
    row_parts, halfway, sent = to_rows(first)
    activation = rows_to_units(after(select, first), acts)
    other_first = tile_part(0, activation, False, [])
    *first_parts, grads[1][4] = lax.optimization_barrier((*row_parts, after(grads[1][4], other_first)))
    second = input_sums(1)
    row_parts, halfway, sent = to_rows(second)
    own_first = tile_part(0, sent, True, [other_core(other_first)])
    other_second = tile_part(1, after(halfway, own_first), False, [])
    own_second = tile_part(1, other_second, True, [own_first, other_core(other_second)])
    first_sum = add_up(first_parts, other_second)
    second_sum = add_up(row_parts, own_second)
    input_grad = jnp.concatenate([first_sum, second_sum], axis=0)
    tile_grads = own_second.reshape(1, 1, half_slots, 4096)
    return (activation, input_grad, tile_grads)


def solution(mesh):
    return jax.shard_map(
        local,
        mesh=mesh,
        in_specs=(
            P("dp", "col"),
            P("row", "col", "dp", None),
            P("row", "col", None),
            P("row", "col", None),
            P("row", "col"),
            P("dp", ("row", "col")),
        ),
        out_specs=(P("dp", ("row", "col")), P(("dp", "row"), "col"), P("row", "col", "dp", None)),
        check_vma=False,
    )
```

```python
import functools

import jax
import jax.numpy as jnp
from jax import lax
from jax.experimental import pallas as pl
from jax.experimental.pallas import tpu as pltpu
from jax.sharding import PartitionSpec as P

COEFF = 0.7978845608028654
CUBIC = 0.044715
BLOCK = 64
HALF = 32
CHUNKS = 2
ADD_UNROLL = 54
OUTER_UNROLL = 27
TURN_UNROLL = 27
PLAIN_UNROLL = 8
FLOPS_PER_US = 1_150_000_000
MIB = 1024 * 1024
VMEM = pl.BlockSpec(memory_space=pltpu.VMEM)
SMEM = pl.BlockSpec(memory_space=pltpu.SMEM)
ANY = pl.BlockSpec(memory_space=pl.ANY)
NT = (((1,), (1,)), ((), ()))


def widest_divisor(total, most):
    return max(divisor for divisor in range(1, most + 1) if total % divisor == 0)


def unpack(packed):
    return jnp.concatenate([packed[:, :BLOCK], packed[:, BLOCK:]], axis=0)


def pack(square):
    return jnp.concatenate([square[:HALF], square[HALF:]], axis=1)


def matmul(left, right):
    return jnp.dot(left, right, preferred_element_type=jnp.float32)


def matmul_nt(left, right):
    return lax.dot_general(left, right, NT, preferred_element_type=jnp.float32)


def call(kernel, name, out_shape, in_specs, out_specs, operands, mib, microseconds, scratch=(), **more):
    moved = sum(operand.size * operand.dtype.itemsize for operand in operands)
    moved += sum(leaf.size * leaf.dtype.itemsize for leaf in jax.tree.leaves(out_shape))
    return pl.pallas_call(
        kernel,
        out_shape=out_shape,
        in_specs=in_specs,
        out_specs=out_specs,
        scratch_shapes=list(scratch),
        name=name,
        compiler_params=pltpu.CompilerParams(vmem_limit_bytes=mib * MIB),
        cost_estimate=pl.CostEstimate(
            flops=microseconds * FLOPS_PER_US, bytes_accessed=moved if microseconds else 0, transcendentals=0
        ),
        **more,
    )(*operands)


def plain_loop(total, body):
    unroll = widest_divisor(total, PLAIN_UNROLL)

    @pl.loop(0, total // unroll)
    def _(group):
        for lane in range(unroll):
            body(group * unroll + lane)


def half_counts(facts_ref, half_slots):
    count, dp = facts_ref[0], facts_ref[2]
    own = dp * half_slots
    other = half_slots - own
    return count, ((own, 0), (other, 1))


def add_products(facts_ref, target_ref, source_ref, tile_refs, table, total, width):
    spare = total.shape[0] - 1
    half_slots = tile_refs[0].shape[0]
    unroll = widest_divisor(half_slots, ADD_UNROLL)
    count, halves = half_counts(facts_ref, half_slots)

    def clear(block):
        total[block] = jnp.zeros(total.shape[1:], jnp.float32)

    plain_loop(spare, clear)

    for first, which in halves:
        live = jnp.clip(count - first, 0, half_slots)

        @pl.loop(0, (live + unroll - 1) // unroll)
        def _(group):
            products = []
            places = []
            for lane in range(unroll):
                index = group * unroll + lane
                slot = first + index
                places.append(jnp.where(slot < count, target_ref[slot], spare))
                products.append(matmul(unpack(tile_refs[which][index]), table[source_ref[slot]]))
            for place, product in zip(places, products):
                total[place] += product


def forward_kernel(share_blocks, facts_ref, row_ref, col_ref, own_ref, other_ref, table_ref, *refs):
    along_x, along_y, own_a, own_b, relay_x, relay_y, total = refs
    half_blocks = share_blocks // 2
    add_products(facts_ref, row_ref, col_ref, (own_ref, other_ref), table_ref, total, table_ref.shape[2])
    me = facts_ref[1]
    for out_ref, share, half in (
        (along_x.at[0], 3, 0),
        (along_x.at[1], 1, 0),
        (along_y.at[0], 3, 1),
        (along_y.at[1], 2, 1),
        (own_a, 0, 0),
        (own_b, 0, 1),
        (relay_x, 1, 1),
        (relay_y, 2, 0),
    ):
        first = (me ^ share) * share_blocks + half * half_blocks

        def write(block, out_ref=out_ref, first=first):
            out_ref[block] = total[first + block].astype(out_ref.dtype)

        plain_loop(half_blocks, write)


def forward(facts, rows, cols, own, other, table, share_blocks, shares):
    blocks = share_blocks * shares
    width = table.shape[2]
    half = (share_blocks // 2, BLOCK, width)
    piece = jax.ShapeDtypeStruct(half, jnp.bfloat16)
    two = jax.ShapeDtypeStruct((2, *half), jnp.bfloat16)
    return call(
        functools.partial(forward_kernel, share_blocks),
        "forward",
        [two] * 2 + [piece] * 4,
        [SMEM] * 3 + [VMEM] * 3,
        [VMEM] * 6,
        (facts, rows, cols, own, other, table),
        20,
        7,
        [pltpu.VMEM((blocks + 1, BLOCK, width), jnp.float32)],
    )


def load_pieces(facts_ref, piece_refs, table, sem, share_blocks):
    half_blocks = share_blocks // 2
    me = facts_ref[1]
    places = ((0, 0, share_blocks), (1, 0, share_blocks), (2, 0, share_blocks))
    places += ((3, 0, half_blocks), (3, half_blocks, half_blocks))
    copies = []
    for number, (piece_ref, (share, start, length)) in enumerate(zip(piece_refs, places)):
        first = (me ^ share) * share_blocks + start
        copies.append(pltpu.make_async_copy(piece_ref, table.at[pl.ds(first, length)], sem.at[number]))
    for copy in copies:
        copy.start()
    return copies


def backward_kernel(share_blocks, facts_ref, row_ref, col_ref, own_ref, other_ref, *refs):
    *piece_refs, out_ref, total, table, sem = refs
    for copy in load_pieces(facts_ref, piece_refs, table, sem, share_blocks):
        copy.wait()
    add_products(facts_ref, col_ref, row_ref, (own_ref, other_ref), table, total, table.shape[2])
    pairs = out_ref.shape[1] // (2 * BLOCK)
    for pair in range(pairs):
        both = jnp.concatenate([total[2 * pair], total[2 * pair + 1]], axis=0)
        out_ref[:, pair * 2 * BLOCK : (pair + 1) * 2 * BLOCK] = both.T.astype(out_ref.dtype)


def backward(facts, rows, cols, own, other, pieces, share_blocks, in_blocks):
    width = pieces[0].shape[2]
    blocks = 4 * share_blocks
    return call(
        functools.partial(backward_kernel, share_blocks),
        "backward",
        jax.ShapeDtypeStruct((width, in_blocks * BLOCK), jnp.bfloat16),
        [SMEM] * 3 + [VMEM] * 2 + [ANY] * len(pieces),
        VMEM,
        (facts, rows, cols, own, other, *pieces),
        20,
        7,
        [
            pltpu.VMEM((in_blocks + 1, BLOCK, width), jnp.float32),
            pltpu.VMEM((blocks, BLOCK, width), jnp.bfloat16),
            pltpu.SemaphoreType.DMA((len(pieces),)),
        ],
    )


def outer_kernel(share_blocks, mine, adds, facts_ref, row_ref, col_ref, *refs):
    added_refs, (input_ref, *piece_refs) = refs[:adds], refs[adds:-3]
    out_ref, table, sem = refs[-3:]
    for copy in load_pieces(facts_ref, piece_refs, table, sem, share_blocks):
        copy.wait()
    half_slots = out_ref.shape[0]
    unroll = widest_divisor(half_slots, OUTER_UNROLL)
    count, halves = half_counts(facts_ref, half_slots)
    first_slot = halves[0][0] if mine else halves[1][0]

    @pl.loop(0, half_slots // unroll)
    def _(group):
        first = group * unroll

        @pl.when(first_slot + first < count)
        def _():
            for lane in range(unroll):
                index = first + lane
                slot = first_slot + index
                packed = pack(matmul_nt(table[row_ref[slot]], input_ref[col_ref[slot]]))
                for added_ref in added_refs:
                    packed += added_ref[index].astype(jnp.float32)
                out_ref[index] = jnp.where(slot < count, packed, 0.0).astype(out_ref.dtype)

        @pl.when(first_slot + first >= count)
        def _():
            for lane in range(unroll):
                out_ref[first + lane] = jnp.zeros(out_ref.shape[1:], out_ref.dtype)


def outer(facts, rows, cols, inputs, pieces, share_blocks, half_slots, mine, added):
    blocks = 4 * share_blocks
    return call(
        functools.partial(outer_kernel, share_blocks, mine, len(added)),
        "outer_own" if mine else "outer_other",
        jax.ShapeDtypeStruct((half_slots, HALF, 2 * BLOCK), jnp.bfloat16),
        [SMEM] * 3 + [VMEM] * (len(added) + 1) + [ANY] * len(pieces),
        VMEM,
        (facts, rows, cols, *added, inputs, *pieces),
        20,
        5,
        [
            pltpu.VMEM((blocks, BLOCK, inputs.shape[2]), jnp.bfloat16),
            pltpu.SemaphoreType.DMA((len(pieces),)),
        ],
    )


def transpose_kernel(unroll, own_ref, other_ref, own_out, other_out):
    row = lax.broadcasted_iota(jnp.int32, (BLOCK, BLOCK), 0)
    col = lax.broadcasted_iota(jnp.int32, (BLOCK, BLOCK), 1)
    unit = (row == col).astype(jnp.bfloat16)

    @pl.loop(0, own_ref.shape[0] // unroll)
    def _(group):
        for lane in range(unroll):
            index = group * unroll + lane
            for source, target in ((own_ref, own_out), (other_ref, other_out)):
                target[index] = pack(matmul_nt(unit, unpack(source[index]))).astype(jnp.bfloat16)


def transpose_tiles(own, other):
    shape = jax.ShapeDtypeStruct(own.shape, own.dtype)
    return call(
        functools.partial(transpose_kernel, widest_divisor(own.shape[0], TURN_UNROLL)),
        "transpose_tiles",
        [shape, shape],
        [VMEM] * 2,
        [VMEM] * 2,
        (own, other),
        12,
        7,
    )


def unit_order():
    row = lax.broadcasted_iota(jnp.int32, (2 * BLOCK, 2 * BLOCK), 0)
    col = lax.broadcasted_iota(jnp.int32, (2 * BLOCK, 2 * BLOCK), 1)
    kept = (row & BLOCK) + 2 * (row & (HALF - 1)) + ((row >> 5) & 1)
    return (kept == col).astype(jnp.bfloat16)


def token_rows_kernel(reorder, values_ref, select_ref, *out_refs):
    row = lax.broadcasted_iota(jnp.int32, (2 * BLOCK, 2 * BLOCK), 0)
    col = lax.broadcasted_iota(jnp.int32, (2 * BLOCK, 2 * BLOCK), 1)
    order = unit_order() if reorder else (row == col).astype(jnp.bfloat16)
    for pair in range(out_refs[0].shape[0] // 2):
        lanes = values_ref[:, pair * 2 * BLOCK : (pair + 1) * 2 * BLOCK]
        turned = matmul_nt(order, lanes).astype(jnp.bfloat16)
        for chunk, out_ref in enumerate(out_refs):
            picked = matmul(turned, select_ref[chunk]).astype(jnp.bfloat16)
            out_ref[2 * pair] = picked[:BLOCK]
            out_ref[2 * pair + 1] = picked[BLOCK:]


def token_rows(values, select, reorder):
    chunks, tokens, width = select.shape
    blocks = values.shape[1] // BLOCK
    shape = jax.ShapeDtypeStruct((blocks, BLOCK, width), jnp.bfloat16)
    return call(
        functools.partial(token_rows_kernel, reorder),
        "units_to_rows" if reorder else "features_to_rows",
        [shape] * chunks,
        [VMEM] * 2,
        [VMEM] * chunks,
        (values, select),
        12,
        5,
    )


def rows_to_units_kernel(select_ref, *refs):
    *act_refs, out_ref = refs
    order = unit_order()
    for pair in range(act_refs[0].shape[0] // 2):
        turned = 0.0
        for chunk, act_ref in enumerate(act_refs):
            both = jnp.concatenate([act_ref[2 * pair], act_ref[2 * pair + 1]], axis=0)
            turned = turned + matmul_nt(select_ref[chunk], both)
        out_ref[:, pair * 2 * BLOCK : (pair + 1) * 2 * BLOCK] = matmul(
            turned.astype(jnp.bfloat16), order
        ).astype(out_ref.dtype)


def rows_to_units(select, acts):
    chunks, tokens, width = select.shape
    units = acts[0].shape[0] * BLOCK
    return call(
        rows_to_units_kernel,
        "rows_to_units",
        jax.ShapeDtypeStruct((tokens, units), jnp.bfloat16),
        [VMEM] * (1 + len(acts)),
        VMEM,
        (select, *acts),
        12,
        6,
    )


def gelu_kernel(upstream_ref, own_a, near_a, last_a, own_b, near_b, last_b, grad_out, act_out):
    half_blocks = own_a.shape[0]
    for half, (own, near, last) in enumerate(((own_a, near_a, last_a), (own_b, near_b, last_b))):

        def one(block, half=half, own=own, near=near, last=last):
            pre = own[block].astype(jnp.float32) + near[1, block].astype(jnp.float32)
            pre = pre + last[block].astype(jnp.float32)
            square = pre * pre
            inner = jnp.tanh(COEFF * (pre + CUBIC * square * pre))
            front = 0.5 * (1.0 + inner)
            place = half * half_blocks + block
            act_out[place] = (front * pre).astype(act_out.dtype)
            slope = front + 0.5 * pre * (1.0 - inner * inner) * COEFF * (1.0 + 3.0 * CUBIC * square)
            grad_out[place] = (upstream_ref[place].astype(jnp.float32) * slope).astype(grad_out.dtype)

        plain_loop(half_blocks, one)


def gelu(upstream, parts):
    shape = jax.ShapeDtypeStruct(upstream.shape, jnp.bfloat16)
    return call(
        gelu_kernel,
        "gelu",
        [shape] * 2,
        [VMEM] * 7,
        [VMEM] * 2,
        (upstream, *parts),
        12,
        2,
    )


def after(value, earlier):
    return lax.optimization_barrier((value, earlier))[0]


def token_select(tokens, rows):
    width = tokens // CHUNKS
    part = width // rows
    chunk = jnp.arange(CHUNKS)[:, None, None]
    token = jnp.arange(tokens)[None, :, None]
    lane = jnp.arange(width)[None, None, :]
    kept = (lane // part) * part * CHUNKS + chunk * part + lane % part
    return (kept == token).astype(jnp.bfloat16)


def local(inputs, weight_tiles, tile_rows, tile_cols, tile_counts, act_grad):
    tokens = inputs.shape[0]
    in_blocks = inputs.shape[1] // BLOCK
    shares = lax.axis_size("col")
    row_devices = lax.axis_size("row")
    dp_devices = lax.axis_size("dp")
    share = act_grad.shape[1]
    share_blocks = share // BLOCK
    slots = tile_rows.shape[2]
    half_slots = weight_tiles.shape[2]
    width = tokens // CHUNKS
    part = width // row_devices
    assert shares == 4 and dp_devices == 2 and share_blocks % 2 == 0
    rows = tile_rows.reshape(slots)
    cols = tile_cols.reshape(slots)
    facts = jnp.stack([tile_counts.reshape(()), lax.axis_index("col"), lax.axis_index("dp")]).astype(jnp.int32)

    def across(values, bit):
        return lax.ppermute(values, "col", [(place, place ^ bit) for place in range(shares)])

    def other_core(values):
        return lax.ppermute(values, "dp", [(0, 1), (1, 0)])

    own = weight_tiles.reshape(half_slots, HALF, 2 * BLOCK)
    other = other_core(own)
    select = token_select(tokens, row_devices)
    tables = token_rows(inputs, select, False)

    partials = [forward(facts, rows, cols, own, other, table, share_blocks, shares) for table in tables]
    upstream = list(token_rows(act_grad, after(select, partials[1][2]), True))
    own_t, other_t = transpose_tiles(after(own, upstream[1]), after(other, upstream[1]))

    grads, acts = [], []
    for chunk in range(CHUNKS):
        along_x, along_y, own_a, own_b, relay_x, relay_y = partials[chunk]
        from_x, from_y = across(along_x, 1), across(along_y, 2)
        sum_y, sum_x = relay_y + from_x[0], relay_x + from_y[0]
        if chunk:
            sum_y = after(sum_y, own_t)
        last_a, last_b = across(sum_y, 2), across(sum_x, 1)
        grad, act = gelu(upstream[chunk], (own_a, from_x, last_a, own_b, from_y, last_b))
        acts.append(act)
        sent_x = sent_y = grad
        if chunk:
            sent_x, sent_y = after(grad, grads[0][1]), after(grad, grads[0][2])
        grads.append([grad, across(sent_x, 1), across(sent_y, 2)])

    for chunk in range(CHUNKS):
        grad, grad_x, grad_y = grads[chunk]
        far_a = across(grad_x[: share_blocks // 2], 2)
        far_b = across(grad_y[share_blocks // 2 :], 1)
        grads[chunk] += [far_a, far_b]

    me_row = lax.axis_index("row")

    def take(values, index):
        return lax.dynamic_index_in_dim(values, index, 0, keepdims=False)

    def to_rows(partial):
        if row_devices != 4:
            return [lax.psum_scatter(partial, "row", scatter_dimension=0, tiled=True)], partial, partial
        low, high = me_row & 1, me_row >> 1
        pieces = partial.reshape(2, 2, part, in_blocks * BLOCK)
        sent, kept = (lax.dynamic_index_in_dim(pieces, bit, 1, keepdims=False) for bit in (1 - low, low))
        moved = lax.ppermute(sent, "row", [(place, place ^ 1) for place in range(4)])
        both = take(kept, 1 - high).astype(jnp.float32) + take(moved, 1 - high).astype(jnp.float32)
        last = lax.ppermute(both.astype(jnp.bfloat16), "row", [(place, place ^ 2) for place in range(4)])
        return [last, take(kept, high), take(moved, high)], both, sent

    def add_up(parts, earlier):
        parts = [*parts[:-1], after(parts[-1], earlier)]
        return sum(part.astype(jnp.float32) for part in parts).astype(jnp.bfloat16)

    def input_sums(chunk):
        return backward(facts, rows, cols, own_t, other_t, grads[chunk], share_blocks, in_blocks)

    def tile_part(chunk, earlier, mine, added):
        table = after(tables[chunk], earlier)
        return outer(facts, rows, cols, table, grads[chunk], share_blocks, half_slots, mine, added)

    first = input_sums(0)
    row_parts, halfway, sent = to_rows(first)
    activation = rows_to_units(after(select, sent), acts)
    other_first = tile_part(0, activation, False, [])
    *first_parts, grads[1][4] = lax.optimization_barrier((*row_parts, after(grads[1][4], other_first)))
    second = input_sums(1)
    row_parts, halfway, sent = to_rows(second)
    own_first = tile_part(0, sent, True, [other_core(other_first)])
    other_second = tile_part(1, after(halfway, own_first), False, [])
    own_second = tile_part(1, other_second, True, [own_first, other_core(other_second)])
    first_sum = add_up(first_parts, other_second)
    second_sum = add_up(row_parts, own_second)
    input_grad = jnp.concatenate([first_sum, second_sum], axis=0)
    tile_grads = own_second.reshape(1, 1, half_slots, 4096)
    return (activation, input_grad, tile_grads)


def solution(mesh):
    return jax.shard_map(
        local,
        mesh=mesh,
        in_specs=(
            P("dp", "col"),
            P("row", "col", "dp", None),
            P("row", "col", None),
            P("row", "col", None),
            P("row", "col"),
            P("dp", ("row", "col")),
        ),
        out_specs=(P("dp", ("row", "col")), P(("dp", "row"), "col"), P("row", "col", "dp", None)),
        check_vma=False,
    )
```

```python
import functools

import jax
import jax.numpy as jnp
from jax import lax
from jax.experimental import pallas as pl
from jax.experimental.pallas import tpu as pltpu
from jax.sharding import PartitionSpec as P

COEFF = 0.7978845608028654
CUBIC = 0.044715
BLOCK = 64
HALF = 32
CHUNKS = 2
ADD_UNROLL = 54
OUTER_UNROLL = 27
TURN_UNROLL = 27
PLAIN_UNROLL = 8
FLOPS_PER_US = 1_150_000_000
MIB = 1024 * 1024
VMEM = pl.BlockSpec(memory_space=pltpu.VMEM)
SMEM = pl.BlockSpec(memory_space=pltpu.SMEM)
HBM = pl.BlockSpec(memory_space=pltpu.HBM)
NT = (((1,), (1,)), ((), ()))


def widest_divisor(total, most):
    return max(divisor for divisor in range(1, most + 1) if total % divisor == 0)


def unpack(packed):
    return jnp.concatenate([packed[:, :BLOCK], packed[:, BLOCK:]], axis=0)


def pack(square):
    return jnp.concatenate([square[:HALF], square[HALF:]], axis=1)


def matmul(left, right):
    return jnp.dot(left, right, preferred_element_type=jnp.float32)


def matmul_nt(left, right):
    return lax.dot_general(left, right, NT, preferred_element_type=jnp.float32)


def call(kernel, name, out_shape, in_specs, out_specs, operands, mib, microseconds, scratch=(), **more):
    moved = sum(operand.size * operand.dtype.itemsize for operand in operands)
    moved += sum(leaf.size * leaf.dtype.itemsize for leaf in jax.tree.leaves(out_shape))
    return pl.pallas_call(
        kernel,
        out_shape=out_shape,
        in_specs=in_specs,
        out_specs=out_specs,
        scratch_shapes=list(scratch),
        name=name,
        compiler_params=pltpu.CompilerParams(vmem_limit_bytes=mib * MIB),
        cost_estimate=pl.CostEstimate(
            flops=microseconds * FLOPS_PER_US, bytes_accessed=moved if microseconds else 0, transcendentals=0
        ),
        **more,
    )(*operands)


def plain_loop(total, body):
    unroll = widest_divisor(total, PLAIN_UNROLL)

    @pl.loop(0, total // unroll)
    def _(group):
        for lane in range(unroll):
            body(group * unroll + lane)


def half_counts(facts_ref, half_slots):
    count, dp = facts_ref[0], facts_ref[2]
    own = dp * half_slots
    other = half_slots - own
    return count, ((own, 0), (other, 1))


def add_products(facts_ref, target_ref, source_ref, tile_refs, table, total, width):
    spare = total.shape[0] - 1
    half_slots = tile_refs[0].shape[0]
    unroll = widest_divisor(half_slots, ADD_UNROLL)
    count, halves = half_counts(facts_ref, half_slots)

    def clear(block):
        total[block] = jnp.zeros(total.shape[1:], jnp.float32)

    plain_loop(spare, clear)

    for first, which in halves:
        live = jnp.clip(count - first, 0, half_slots)

        @pl.loop(0, (live + unroll - 1) // unroll)
        def _(group):
            products = []
            places = []
            for lane in range(unroll):
                index = group * unroll + lane
                slot = first + index
                places.append(jnp.where(slot < count, target_ref[slot], spare))
                products.append(matmul(unpack(tile_refs[which][index]), table[source_ref[slot]]))
            for place, product in zip(places, products):
                total[place] += product


def forward_kernel(share_blocks, facts_ref, row_ref, col_ref, own_ref, other_ref, table_ref, *refs):
    along_x, along_y, own_a, own_b, relay_x, relay_y, total = refs
    half_blocks = share_blocks // 2
    add_products(facts_ref, row_ref, col_ref, (own_ref, other_ref), table_ref, total, table_ref.shape[2])
    me = facts_ref[1]
    for out_ref, share, half in (
        (along_x.at[0], 3, 0),
        (along_x.at[1], 1, 0),
        (along_y.at[0], 3, 1),
        (along_y.at[1], 2, 1),
        (own_a, 0, 0),
        (own_b, 0, 1),
        (relay_x, 1, 1),
        (relay_y, 2, 0),
    ):
        first = (me ^ share) * share_blocks + half * half_blocks

        def write(block, out_ref=out_ref, first=first):
            out_ref[block] = total[first + block].astype(out_ref.dtype)

        plain_loop(half_blocks, write)


def forward(facts, rows, cols, own, other, table, share_blocks, shares):
    blocks = share_blocks * shares
    width = table.shape[2]
    half = (share_blocks // 2, BLOCK, width)
    piece = jax.ShapeDtypeStruct(half, jnp.bfloat16)
    two = jax.ShapeDtypeStruct((2, *half), jnp.bfloat16)
    return call(
        functools.partial(forward_kernel, share_blocks),
        "forward",
        [two] * 2 + [piece] * 4,
        [SMEM] * 3 + [VMEM] * 3,
        [VMEM] * 6,
        (facts, rows, cols, own, other, table),
        16,
        0,
        [pltpu.VMEM((blocks + 1, BLOCK, width), jnp.float32)],
    )


def load_pieces(facts_ref, piece_refs, table, sem, share_blocks):
    half_blocks = share_blocks // 2
    me = facts_ref[1]
    places = ((0, 0, share_blocks), (1, 0, share_blocks), (2, 0, share_blocks))
    places += ((3, 0, half_blocks), (3, half_blocks, half_blocks))
    copies = []
    for number, (piece_ref, (share, start, length)) in enumerate(zip(piece_refs, places)):
        first = (me ^ share) * share_blocks + start
        copies.append(pltpu.make_async_copy(piece_ref, table.at[pl.ds(first, length)], sem.at[number]))
    for copy in copies:
        copy.start()
    return copies


def backward_kernel(share_blocks, facts_ref, row_ref, col_ref, own_ref, other_ref, *refs):
    *piece_refs, out_ref, total, table, sem = refs
    for copy in load_pieces(facts_ref, piece_refs, table, sem, share_blocks):
        copy.wait()
    add_products(facts_ref, col_ref, row_ref, (own_ref, other_ref), table, total, table.shape[2])
    pairs = out_ref.shape[1] // (2 * BLOCK)
    for pair in range(pairs):
        both = jnp.concatenate([total[2 * pair], total[2 * pair + 1]], axis=0)
        out_ref[:, pair * 2 * BLOCK : (pair + 1) * 2 * BLOCK] = both.T.astype(out_ref.dtype)


def backward(facts, rows, cols, own, other, pieces, share_blocks, in_blocks):
    width = pieces[0].shape[2]
    blocks = 4 * share_blocks
    return call(
        functools.partial(backward_kernel, share_blocks),
        "backward",
        jax.ShapeDtypeStruct((width, in_blocks * BLOCK), jnp.bfloat16),
        [SMEM] * 3 + [VMEM] * 2 + [HBM] * len(pieces),
        VMEM,
        (facts, rows, cols, own, other, *pieces),
        12,
        7,
        [
            pltpu.VMEM((in_blocks + 1, BLOCK, width), jnp.float32),
            pltpu.VMEM((blocks, BLOCK, width), jnp.bfloat16),
            pltpu.SemaphoreType.DMA((len(pieces),)),
        ],
    )


def outer_kernel(share_blocks, mine, adds, facts_ref, row_ref, col_ref, *refs):
    added_refs, (input_ref, *piece_refs) = refs[:adds], refs[adds:-3]
    out_ref, table, sem = refs[-3:]
    for copy in load_pieces(facts_ref, piece_refs, table, sem, share_blocks):
        copy.wait()
    half_slots = out_ref.shape[0]
    unroll = widest_divisor(half_slots, OUTER_UNROLL)
    count, halves = half_counts(facts_ref, half_slots)
    first_slot = halves[0][0] if mine else halves[1][0]

    @pl.loop(0, half_slots // unroll)
    def _(group):
        first = group * unroll

        @pl.when(first_slot + first < count)
        def _():
            for lane in range(unroll):
                index = first + lane
                slot = first_slot + index
                packed = pack(matmul_nt(table[row_ref[slot]], input_ref[col_ref[slot]]))
                for added_ref in added_refs:
                    packed += added_ref[index].astype(jnp.float32)
                out_ref[index] = jnp.where(slot < count, packed, 0.0).astype(out_ref.dtype)

        @pl.when(first_slot + first >= count)
        def _():
            for lane in range(unroll):
                out_ref[first + lane] = jnp.zeros(out_ref.shape[1:], out_ref.dtype)


def outer(facts, rows, cols, inputs, pieces, share_blocks, half_slots, mine, added):
    blocks = 4 * share_blocks
    return call(
        functools.partial(outer_kernel, share_blocks, mine, len(added)),
        "outer_own" if mine else "outer_other",
        jax.ShapeDtypeStruct((half_slots, HALF, 2 * BLOCK), jnp.bfloat16),
        [SMEM] * 3 + [VMEM] * (len(added) + 1) + [HBM] * len(pieces),
        VMEM,
        (facts, rows, cols, *added, inputs, *pieces),
        12,
        5,
        [
            pltpu.VMEM((blocks, BLOCK, inputs.shape[2]), jnp.bfloat16),
            pltpu.SemaphoreType.DMA((len(pieces),)),
        ],
    )


def transpose_kernel(unroll, own_ref, other_ref, own_out, other_out):
    row = lax.broadcasted_iota(jnp.int32, (BLOCK, BLOCK), 0)
    col = lax.broadcasted_iota(jnp.int32, (BLOCK, BLOCK), 1)
    unit = (row == col).astype(jnp.bfloat16)

    @pl.loop(0, own_ref.shape[0] // unroll)
    def _(group):
        for lane in range(unroll):
            index = group * unroll + lane
            for source, target in ((own_ref, own_out), (other_ref, other_out)):
                target[index] = pack(matmul_nt(unit, unpack(source[index]))).astype(jnp.bfloat16)


def transpose_tiles(own, other):
    shape = jax.ShapeDtypeStruct(own.shape, own.dtype)
    return call(
        functools.partial(transpose_kernel, widest_divisor(own.shape[0], TURN_UNROLL)),
        "transpose_tiles",
        [shape, shape],
        [VMEM] * 2,
        [VMEM] * 2,
        (own, other),
        10,
        0,
    )


def unit_order():
    row = lax.broadcasted_iota(jnp.int32, (2 * BLOCK, 2 * BLOCK), 0)
    col = lax.broadcasted_iota(jnp.int32, (2 * BLOCK, 2 * BLOCK), 1)
    kept = (row & BLOCK) + 2 * (row & (HALF - 1)) + ((row >> 5) & 1)
    return (kept == col).astype(jnp.bfloat16)


def token_rows_kernel(reorder, values_ref, select_ref, *out_refs):
    row = lax.broadcasted_iota(jnp.int32, (2 * BLOCK, 2 * BLOCK), 0)
    col = lax.broadcasted_iota(jnp.int32, (2 * BLOCK, 2 * BLOCK), 1)
    order = unit_order() if reorder else (row == col).astype(jnp.bfloat16)
    for pair in range(out_refs[0].shape[0] // 2):
        lanes = values_ref[:, pair * 2 * BLOCK : (pair + 1) * 2 * BLOCK]
        turned = matmul_nt(order, lanes).astype(jnp.bfloat16)
        for chunk, out_ref in enumerate(out_refs):
            picked = matmul(turned, select_ref[chunk]).astype(jnp.bfloat16)
            out_ref[2 * pair] = picked[:BLOCK]
            out_ref[2 * pair + 1] = picked[BLOCK:]


def token_rows(values, select, reorder):
    chunks, tokens, width = select.shape
    blocks = values.shape[1] // BLOCK
    shape = jax.ShapeDtypeStruct((blocks, BLOCK, width), jnp.bfloat16)
    return call(
        functools.partial(token_rows_kernel, reorder),
        "units_to_rows" if reorder else "features_to_rows",
        [shape] * chunks,
        [VMEM] * 2,
        [VMEM] * chunks,
        (values, select),
        6,
        0,
    )


def rows_to_units_kernel(select_ref, *refs):
    *act_refs, out_ref = refs
    order = unit_order()
    for pair in range(act_refs[0].shape[0] // 2):
        turned = 0.0
        for chunk, act_ref in enumerate(act_refs):
            both = jnp.concatenate([act_ref[2 * pair], act_ref[2 * pair + 1]], axis=0)
            turned = turned + matmul_nt(select_ref[chunk], both)
        out_ref[:, pair * 2 * BLOCK : (pair + 1) * 2 * BLOCK] = matmul(
            turned.astype(jnp.bfloat16), order
        ).astype(out_ref.dtype)


def rows_to_units(select, acts):
    chunks, tokens, width = select.shape
    units = acts[0].shape[0] * BLOCK
    return call(
        rows_to_units_kernel,
        "rows_to_units",
        jax.ShapeDtypeStruct((tokens, units), jnp.bfloat16),
        [VMEM] * (1 + len(acts)),
        VMEM,
        (select, *acts),
        6,
        0,
    )


def gelu_kernel(upstream_hbm, own_a, near_a, last_a, own_b, near_b, last_b, grad_out, act_out, upstream_ref, held, sem):
    half_blocks = own_a.shape[0]
    copies = [pltpu.make_async_copy(upstream_hbm, upstream_ref, sem.at[6])]
    for number, source in enumerate((own_a, near_a.at[1], last_a, own_b, near_b.at[1], last_b)):
        copies.append(pltpu.make_async_copy(source, held.at[number], sem.at[number]))
    for copy in copies:
        copy.start()
    for copy in copies:
        copy.wait()
    for half in range(2):

        def one(block, half=half):
            pre = held[3 * half, block].astype(jnp.float32) + held[3 * half + 1, block].astype(jnp.float32)
            pre = pre + held[3 * half + 2, block].astype(jnp.float32)
            square = pre * pre
            inner = jnp.tanh(COEFF * (pre + CUBIC * square * pre))
            front = 0.5 * (1.0 + inner)
            place = half * half_blocks + block
            act_out[place] = (front * pre).astype(act_out.dtype)
            slope = front + 0.5 * pre * (1.0 - inner * inner) * COEFF * (1.0 + 3.0 * CUBIC * square)
            grad_out[place] = (upstream_ref[place].astype(jnp.float32) * slope).astype(grad_out.dtype)

        plain_loop(half_blocks, one)


def gelu(upstream, parts):
    shape = jax.ShapeDtypeStruct(upstream.shape, jnp.bfloat16)
    return call(
        gelu_kernel,
        "gelu",
        [shape] * 2,
        [HBM] * 7,
        [VMEM] * 2,
        (upstream, *parts),
        8,
        0,
        [
            pltpu.VMEM(upstream.shape, jnp.bfloat16),
            pltpu.VMEM((6, *parts[0].shape), jnp.bfloat16),
            pltpu.SemaphoreType.DMA((7,)),
        ],
    )


def after(value, earlier):
    return lax.optimization_barrier((value, earlier))[0]


def token_select(tokens, rows):
    width = tokens // CHUNKS
    part = width // rows
    chunk = jnp.arange(CHUNKS)[:, None, None]
    token = jnp.arange(tokens)[None, :, None]
    lane = jnp.arange(width)[None, None, :]
    kept = (lane // part) * part * CHUNKS + chunk * part + lane % part
    return (kept == token).astype(jnp.bfloat16)


def local(inputs, weight_tiles, tile_rows, tile_cols, tile_counts, act_grad):
    tokens = inputs.shape[0]
    in_blocks = inputs.shape[1] // BLOCK
    shares = lax.axis_size("col")
    row_devices = lax.axis_size("row")
    dp_devices = lax.axis_size("dp")
    share = act_grad.shape[1]
    share_blocks = share // BLOCK
    slots = tile_rows.shape[2]
    half_slots = weight_tiles.shape[2]
    width = tokens // CHUNKS
    part = width // row_devices
    assert shares == 4 and dp_devices == 2 and share_blocks % 2 == 0
    rows = tile_rows.reshape(slots)
    cols = tile_cols.reshape(slots)
    facts = jnp.stack([tile_counts.reshape(()), lax.axis_index("col"), lax.axis_index("dp")]).astype(jnp.int32)

    def across(values, bit):
        return lax.ppermute(values, "col", [(place, place ^ bit) for place in range(shares)])

    def other_core(values):
        return lax.ppermute(values, "dp", [(0, 1), (1, 0)])

    own = weight_tiles.reshape(half_slots, HALF, 2 * BLOCK)
    other = other_core(own)
    select = token_select(tokens, row_devices)
    tables = token_rows(inputs, select, False)

    partials = [forward(facts, rows, cols, own, other, table, share_blocks, shares) for table in tables]
    upstream = list(token_rows(act_grad, after(select, partials[1][2]), True))
    own_t, other_t = transpose_tiles(after(own, upstream[1]), after(other, upstream[1]))

    terms, sums = [], []
    for chunk in range(CHUNKS):
        along_x, along_y, own_a, own_b, relay_x, relay_y = partials[chunk]
        from_x, from_y = across(along_x, 1), across(along_y, 2)
        sum_y, sum_x = relay_y + from_x[0], relay_x + from_y[0]
        if chunk:
            sum_y = after(sum_y, own_t)
        last_a, last_b = across(sum_y, 2), across(sum_x, 1)
        sums += [sum_y, sum_x]
        terms.append((own_a, from_x, last_a, own_b, from_y, last_b))
    upstream[0] = after(upstream[0], sums)

    grads, acts = [], []
    for chunk in range(CHUNKS):
        grad, act = gelu(upstream[chunk], terms[chunk])
        acts.append(act)
        sent_x = sent_y = grad
        if chunk:
            sent_x, sent_y = after(grad, grads[0][1]), after(grad, grads[0][2])
        grads.append([grad, across(sent_x, 1), across(sent_y, 2)])

    for chunk in range(CHUNKS):
        grad, grad_x, grad_y = grads[chunk]
        far_a = across(grad_x[: share_blocks // 2], 2)
        far_b = across(grad_y[share_blocks // 2 :], 1)
        grads[chunk] += [far_a, far_b]

    me_row = lax.axis_index("row")

    def take(values, index):
        return lax.dynamic_index_in_dim(values, index, 0, keepdims=False)

    def to_rows(partial):
        if row_devices != 4:
            return [lax.psum_scatter(partial, "row", scatter_dimension=0, tiled=True)], partial, partial
        low, high = me_row & 1, me_row >> 1
        pieces = partial.reshape(2, 2, part, in_blocks * BLOCK)
        sent, kept = (lax.dynamic_index_in_dim(pieces, bit, 1, keepdims=False) for bit in (1 - low, low))
        moved = lax.ppermute(sent, "row", [(place, place ^ 1) for place in range(4)])
        both = take(kept, 1 - high).astype(jnp.float32) + take(moved, 1 - high).astype(jnp.float32)
        last = lax.ppermute(both.astype(jnp.bfloat16), "row", [(place, place ^ 2) for place in range(4)])
        return [last, take(kept, high), take(moved, high)], both, sent

    def add_up(parts, earlier):
        parts = [*parts[:-1], after(parts[-1], earlier)]
        return sum(part.astype(jnp.float32) for part in parts).astype(jnp.bfloat16)

    def input_sums(chunk):
        return backward(facts, rows, cols, own_t, other_t, grads[chunk], share_blocks, in_blocks)

    def tile_part(chunk, earlier, mine, added):
        table = after(tables[chunk], earlier)
        return outer(facts, rows, cols, table, grads[chunk], share_blocks, half_slots, mine, added)

    first = input_sums(0)
    row_parts, halfway, sent = to_rows(first)
    activation = rows_to_units(after(select, sent), acts)
    other_first = tile_part(0, activation, False, [])
    *first_parts, grads[1][4] = lax.optimization_barrier((*row_parts, after(grads[1][4], other_first)))
    second = input_sums(1)
    row_parts, halfway, sent = to_rows(second)
    own_first = tile_part(0, sent, True, [other_core(other_first)])
    other_second = tile_part(1, after(halfway, own_first), False, [])
    own_second = tile_part(1, other_second, True, [own_first, other_core(other_second)])
    first_sum = add_up(first_parts, other_second)
    second_sum = add_up(row_parts, own_second)
    input_grad = jnp.concatenate([first_sum, second_sum], axis=0)
    tile_grads = own_second.reshape(1, 1, half_slots, 4096)
    return (activation, input_grad, tile_grads)


def solution(mesh):
    return jax.shard_map(
        local,
        mesh=mesh,
        in_specs=(
            P("dp", "col"),
            P("row", "col", "dp", None),
            P("row", "col", None),
            P("row", "col", None),
            P("row", "col"),
            P("dp", ("row", "col")),
        ),
        out_specs=(P("dp", ("row", "col")), P(("dp", "row"), "col"), P("row", "col", "dp", None)),
        check_vma=False,
    )
```

```python
import functools

import jax
import jax.numpy as jnp
from jax import lax
from jax.experimental import pallas as pl
from jax.experimental.pallas import tpu as pltpu
from jax.sharding import PartitionSpec as P

COEFF = 0.7978845608028654
CUBIC = 0.044715
BLOCK = 64
HALF = 32
CHUNKS = 2
ADD_UNROLL = 54
OUTER_UNROLL = 27
TURN_UNROLL = 27
PLAIN_UNROLL = 8
FLOPS_PER_US = 1_150_000_000
MIB = 1024 * 1024
VMEM = pl.BlockSpec(memory_space=pltpu.VMEM)
SMEM = pl.BlockSpec(memory_space=pltpu.SMEM)
HBM = pl.BlockSpec(memory_space=pltpu.HBM)
NT = (((1,), (1,)), ((), ()))


def widest_divisor(total, most):
    return max(divisor for divisor in range(1, most + 1) if total % divisor == 0)


def unpack(packed):
    return jnp.concatenate([packed[:, :BLOCK], packed[:, BLOCK:]], axis=0)


def pack(square):
    return jnp.concatenate([square[:HALF], square[HALF:]], axis=1)


def matmul(left, right):
    return jnp.dot(left, right, preferred_element_type=jnp.float32)


def matmul_nt(left, right):
    return lax.dot_general(left, right, NT, preferred_element_type=jnp.float32)


def call(kernel, name, out_shape, in_specs, out_specs, operands, mib, microseconds, scratch=(), **more):
    moved = sum(operand.size * operand.dtype.itemsize for operand in operands)
    moved += sum(leaf.size * leaf.dtype.itemsize for leaf in jax.tree.leaves(out_shape))
    return pl.pallas_call(
        kernel,
        out_shape=out_shape,
        in_specs=in_specs,
        out_specs=out_specs,
        scratch_shapes=list(scratch),
        name=name,
        compiler_params=pltpu.CompilerParams(vmem_limit_bytes=mib * MIB),
        cost_estimate=pl.CostEstimate(
            flops=microseconds * FLOPS_PER_US, bytes_accessed=moved if microseconds else 0, transcendentals=0
        ),
        **more,
    )(*operands)


def plain_loop(total, body):
    unroll = widest_divisor(total, PLAIN_UNROLL)

    @pl.loop(0, total // unroll)
    def _(group):
        for lane in range(unroll):
            body(group * unroll + lane)


def half_counts(facts_ref, half_slots):
    count, dp = facts_ref[0], facts_ref[2]
    own = dp * half_slots
    other = half_slots - own
    return count, ((own, 0), (other, 1))


def add_products(facts_ref, target_ref, source_ref, tile_refs, table, total, width):
    spare = total.shape[0] - 1
    half_slots = tile_refs[0].shape[0]
    unroll = widest_divisor(half_slots, ADD_UNROLL)
    count, halves = half_counts(facts_ref, half_slots)

    def clear(block):
        total[block] = jnp.zeros(total.shape[1:], jnp.float32)

    plain_loop(spare, clear)

    for first, which in halves:
        live = jnp.clip(count - first, 0, half_slots)

        @pl.loop(0, (live + unroll - 1) // unroll)
        def _(group):
            products = []
            places = []
            for lane in range(unroll):
                index = group * unroll + lane
                slot = first + index
                places.append(jnp.where(slot < count, target_ref[slot], spare))
                products.append(matmul(unpack(tile_refs[which][index]), table[source_ref[slot]]))
            for place, product in zip(places, products):
                total[place] += product


def forward_kernel(share_blocks, facts_ref, row_ref, col_ref, own_ref, other_ref, table_ref, *refs):
    along_x, along_y, own_a, own_b, relay_x, relay_y, total = refs
    half_blocks = share_blocks // 2
    add_products(facts_ref, row_ref, col_ref, (own_ref, other_ref), table_ref, total, table_ref.shape[2])
    me = facts_ref[1]
    for out_ref, share, half in (
        (along_x.at[0], 3, 0),
        (along_x.at[1], 1, 0),
        (along_y.at[0], 3, 1),
        (along_y.at[1], 2, 1),
        (own_a, 0, 0),
        (own_b, 0, 1),
        (relay_x, 1, 1),
        (relay_y, 2, 0),
    ):
        first = (me ^ share) * share_blocks + half * half_blocks

        def write(block, out_ref=out_ref, first=first):
            out_ref[block] = total[first + block].astype(out_ref.dtype)

        plain_loop(half_blocks, write)


def forward(facts, rows, cols, own, other, table, share_blocks, shares):
    blocks = share_blocks * shares
    width = table.shape[2]
    half = (share_blocks // 2, BLOCK, width)
    piece = jax.ShapeDtypeStruct(half, jnp.bfloat16)
    two = jax.ShapeDtypeStruct((2, *half), jnp.bfloat16)
    return call(
        functools.partial(forward_kernel, share_blocks),
        "forward",
        [two] * 2 + [piece] * 4,
        [SMEM] * 3 + [VMEM] * 3,
        [VMEM] * 6,
        (facts, rows, cols, own, other, table),
        16,
        0,
        [pltpu.VMEM((blocks + 1, BLOCK, width), jnp.float32)],
    )


def load_pieces(facts_ref, piece_refs, table, sem, share_blocks):
    half_blocks = share_blocks // 2
    me = facts_ref[1]
    places = ((0, 0, share_blocks), (1, 0, share_blocks), (2, 0, share_blocks))
    places += ((3, 0, half_blocks), (3, half_blocks, half_blocks))
    copies = []
    for number, (piece_ref, (share, start, length)) in enumerate(zip(piece_refs, places)):
        first = (me ^ share) * share_blocks + start
        copies.append(pltpu.make_async_copy(piece_ref, table.at[pl.ds(first, length)], sem.at[number]))
    for copy in copies:
        copy.start()
    return copies


def backward_kernel(share_blocks, facts_ref, row_ref, col_ref, own_ref, other_ref, *refs):
    *piece_refs, out_ref, total, table, sem = refs
    for copy in load_pieces(facts_ref, piece_refs, table, sem, share_blocks):
        copy.wait()
    add_products(facts_ref, col_ref, row_ref, (own_ref, other_ref), table, total, table.shape[2])
    pairs = out_ref.shape[1] // (2 * BLOCK)
    for pair in range(pairs):
        both = jnp.concatenate([total[2 * pair], total[2 * pair + 1]], axis=0)
        out_ref[:, pair * 2 * BLOCK : (pair + 1) * 2 * BLOCK] = both.T.astype(out_ref.dtype)


def backward(facts, rows, cols, own, other, pieces, share_blocks, in_blocks):
    width = pieces[0].shape[2]
    blocks = 4 * share_blocks
    return call(
        functools.partial(backward_kernel, share_blocks),
        "backward",
        jax.ShapeDtypeStruct((width, in_blocks * BLOCK), jnp.bfloat16),
        [SMEM] * 3 + [VMEM] * 2 + [HBM] * len(pieces),
        VMEM,
        (facts, rows, cols, own, other, *pieces),
        12,
        7,
        [
            pltpu.VMEM((in_blocks + 1, BLOCK, width), jnp.float32),
            pltpu.VMEM((blocks, BLOCK, width), jnp.bfloat16),
            pltpu.SemaphoreType.DMA((len(pieces),)),
        ],
    )


def outer_kernel(share_blocks, mine, adds, facts_ref, row_ref, col_ref, *refs):
    added_refs, (input_ref, *piece_refs) = refs[:adds], refs[adds:-3]
    out_ref, table, sem = refs[-3:]
    for copy in load_pieces(facts_ref, piece_refs, table, sem, share_blocks):
        copy.wait()
    half_slots = out_ref.shape[0]
    unroll = widest_divisor(half_slots, OUTER_UNROLL)
    count, halves = half_counts(facts_ref, half_slots)
    first_slot = halves[0][0] if mine else halves[1][0]

    @pl.loop(0, half_slots // unroll)
    def _(group):
        first = group * unroll

        @pl.when(first_slot + first < count)
        def _():
            for lane in range(unroll):
                index = first + lane
                slot = first_slot + index
                packed = pack(matmul_nt(table[row_ref[slot]], input_ref[col_ref[slot]]))
                for added_ref in added_refs:
                    packed += added_ref[index].astype(jnp.float32)
                out_ref[index] = jnp.where(slot < count, packed, 0.0).astype(out_ref.dtype)

        @pl.when(first_slot + first >= count)
        def _():
            for lane in range(unroll):
                out_ref[first + lane] = jnp.zeros(out_ref.shape[1:], out_ref.dtype)


def outer(facts, rows, cols, inputs, pieces, share_blocks, half_slots, mine, added):
    blocks = 4 * share_blocks
    return call(
        functools.partial(outer_kernel, share_blocks, mine, len(added)),
        "outer_own" if mine else "outer_other",
        jax.ShapeDtypeStruct((half_slots, HALF, 2 * BLOCK), jnp.bfloat16),
        [SMEM] * 3 + [VMEM] * (len(added) + 1) + [HBM] * len(pieces),
        VMEM,
        (facts, rows, cols, *added, inputs, *pieces),
        12,
        5,
        [
            pltpu.VMEM((blocks, BLOCK, inputs.shape[2]), jnp.bfloat16),
            pltpu.SemaphoreType.DMA((len(pieces),)),
        ],
    )


def transpose_kernel(unroll, own_ref, other_ref, own_out, other_out):
    row = lax.broadcasted_iota(jnp.int32, (BLOCK, BLOCK), 0)
    col = lax.broadcasted_iota(jnp.int32, (BLOCK, BLOCK), 1)
    unit = (row == col).astype(jnp.bfloat16)

    @pl.loop(0, own_ref.shape[0] // unroll)
    def _(group):
        for lane in range(unroll):
            index = group * unroll + lane
            for source, target in ((own_ref, own_out), (other_ref, other_out)):
                target[index] = pack(matmul_nt(unit, unpack(source[index]))).astype(jnp.bfloat16)


def transpose_tiles(own, other):
    shape = jax.ShapeDtypeStruct(own.shape, own.dtype)
    return call(
        functools.partial(transpose_kernel, widest_divisor(own.shape[0], TURN_UNROLL)),
        "transpose_tiles",
        [shape, shape],
        [VMEM] * 2,
        [VMEM] * 2,
        (own, other),
        10,
        0,
    )


def unit_order():
    row = lax.broadcasted_iota(jnp.int32, (2 * BLOCK, 2 * BLOCK), 0)
    col = lax.broadcasted_iota(jnp.int32, (2 * BLOCK, 2 * BLOCK), 1)
    kept = (row & BLOCK) + 2 * (row & (HALF - 1)) + ((row >> 5) & 1)
    return (kept == col).astype(jnp.bfloat16)


def token_rows_kernel(reorder, values_ref, select_ref, *out_refs):
    row = lax.broadcasted_iota(jnp.int32, (2 * BLOCK, 2 * BLOCK), 0)
    col = lax.broadcasted_iota(jnp.int32, (2 * BLOCK, 2 * BLOCK), 1)
    order = unit_order() if reorder else (row == col).astype(jnp.bfloat16)
    for pair in range(out_refs[0].shape[0] // 2):
        lanes = values_ref[:, pair * 2 * BLOCK : (pair + 1) * 2 * BLOCK]
        turned = matmul_nt(order, lanes).astype(jnp.bfloat16)
        for chunk, out_ref in enumerate(out_refs):
            picked = matmul(turned, select_ref[chunk]).astype(jnp.bfloat16)
            out_ref[2 * pair] = picked[:BLOCK]
            out_ref[2 * pair + 1] = picked[BLOCK:]


def token_rows(values, select, reorder):
    chunks, tokens, width = select.shape
    blocks = values.shape[1] // BLOCK
    shape = jax.ShapeDtypeStruct((blocks, BLOCK, width), jnp.bfloat16)
    return call(
        functools.partial(token_rows_kernel, reorder),
        "units_to_rows" if reorder else "features_to_rows",
        [shape] * chunks,
        [VMEM] * 2,
        [VMEM] * chunks,
        (values, select),
        6,
        0,
    )


def rows_to_units_kernel(select_ref, *refs):
    *act_refs, out_ref = refs
    order = unit_order()
    for pair in range(act_refs[0].shape[0] // 2):
        turned = 0.0
        for chunk, act_ref in enumerate(act_refs):
            both = jnp.concatenate([act_ref[2 * pair], act_ref[2 * pair + 1]], axis=0)
            turned = turned + matmul_nt(select_ref[chunk], both)
        out_ref[:, pair * 2 * BLOCK : (pair + 1) * 2 * BLOCK] = matmul(
            turned.astype(jnp.bfloat16), order
        ).astype(out_ref.dtype)


def rows_to_units(select, acts):
    chunks, tokens, width = select.shape
    units = acts[0].shape[0] * BLOCK
    return call(
        rows_to_units_kernel,
        "rows_to_units",
        jax.ShapeDtypeStruct((tokens, units), jnp.bfloat16),
        [VMEM] * (1 + len(acts)),
        VMEM,
        (select, *acts),
        6,
        0,
    )


def gelu_kernel(upstream_hbm, own_a, near_a, last_a, own_b, near_b, last_b, grad_out, act_out, upstream_ref, held, sem):
    half_blocks = own_a.shape[0]
    copies = [pltpu.make_async_copy(upstream_hbm, upstream_ref, sem.at[6])]
    for number, source in enumerate((own_a, near_a.at[1], last_a, own_b, near_b.at[1], last_b)):
        copies.append(pltpu.make_async_copy(source, held.at[number], sem.at[number]))
    for copy in copies:
        copy.start()
    for copy in copies:
        copy.wait()
    for half in range(2):

        def one(block, half=half):
            pre = held[3 * half, block].astype(jnp.float32) + held[3 * half + 1, block].astype(jnp.float32)
            pre = pre + held[3 * half + 2, block].astype(jnp.float32)
            square = pre * pre
            inner = jnp.tanh(COEFF * (pre + CUBIC * square * pre))
            front = 0.5 * (1.0 + inner)
            place = half * half_blocks + block
            act_out[place] = (front * pre).astype(act_out.dtype)
            slope = front + 0.5 * pre * (1.0 - inner * inner) * COEFF * (1.0 + 3.0 * CUBIC * square)
            grad_out[place] = (upstream_ref[place].astype(jnp.float32) * slope).astype(grad_out.dtype)

        plain_loop(half_blocks, one)


def gelu(upstream, parts):
    shape = jax.ShapeDtypeStruct(upstream.shape, jnp.bfloat16)
    return call(
        gelu_kernel,
        "gelu",
        [shape] * 2,
        [HBM] * 7,
        [VMEM] * 2,
        (upstream, *parts),
        8,
        0,
        [
            pltpu.VMEM(upstream.shape, jnp.bfloat16),
            pltpu.VMEM((6, *parts[0].shape), jnp.bfloat16),
            pltpu.SemaphoreType.DMA((7,)),
        ],
    )


def after(value, earlier):
    return lax.optimization_barrier((value, earlier))[0]


def token_select(tokens, rows):
    width = tokens // CHUNKS
    part = width // rows
    chunk = jnp.arange(CHUNKS)[:, None, None]
    token = jnp.arange(tokens)[None, :, None]
    lane = jnp.arange(width)[None, None, :]
    kept = (lane // part) * part * CHUNKS + chunk * part + lane % part
    return (kept == token).astype(jnp.bfloat16)


def local(inputs, weight_tiles, tile_rows, tile_cols, tile_counts, act_grad):
    tokens = inputs.shape[0]
    in_blocks = inputs.shape[1] // BLOCK
    shares = lax.axis_size("col")
    row_devices = lax.axis_size("row")
    dp_devices = lax.axis_size("dp")
    share = act_grad.shape[1]
    share_blocks = share // BLOCK
    slots = tile_rows.shape[2]
    half_slots = weight_tiles.shape[2]
    width = tokens // CHUNKS
    part = width // row_devices
    assert shares == 4 and dp_devices == 2 and share_blocks % 2 == 0
    rows = tile_rows.reshape(slots)
    cols = tile_cols.reshape(slots)
    facts = jnp.stack([tile_counts.reshape(()), lax.axis_index("col"), lax.axis_index("dp")]).astype(jnp.int32)

    def across(values, bit):
        return lax.ppermute(values, "col", [(place, place ^ bit) for place in range(shares)])

    def other_core(values):
        return lax.ppermute(values, "dp", [(0, 1), (1, 0)])

    own = weight_tiles.reshape(half_slots, HALF, 2 * BLOCK)
    other = other_core(own)
    select = token_select(tokens, row_devices)
    tables = token_rows(inputs, select, False)

    partials = [forward(facts, rows, cols, own, other, table, share_blocks, shares) for table in tables]
    upstream = list(token_rows(act_grad, after(select, partials[1][2]), True))
    own_t, other_t = transpose_tiles(after(own, upstream[1]), after(other, upstream[1]))

    terms = []
    for chunk in range(CHUNKS):
        along_x, along_y, own_a, own_b, relay_x, relay_y = partials[chunk]
        from_x, from_y = across(along_x, 1), across(along_y, 2)
        sum_y, sum_x = relay_y + from_x[0], relay_x + from_y[0]
        if chunk:
            sum_y = after(sum_y, own_t)
        last_a, last_b = across(sum_y, 2), across(sum_x, 1)
        terms.append((own_a, from_x, last_a, own_b, from_y, last_b))
    upstream[0] = after(upstream[0], terms[1])

    grads, acts = [], []
    for chunk in range(CHUNKS):
        grad, act = gelu(upstream[chunk], terms[chunk])
        acts.append(act)
        sent_x = sent_y = grad
        if chunk:
            sent_x, sent_y = after(grad, grads[0][1]), after(grad, grads[0][2])
        grads.append([grad, across(sent_x, 1), across(sent_y, 2)])

    activation = rows_to_units(select, acts)
    grads[0][1] = after(grads[0][1], activation)
    for chunk in range(CHUNKS):
        grad, grad_x, grad_y = grads[chunk]
        far_a = across(grad_x[: share_blocks // 2], 2)
        far_b = across(grad_y[share_blocks // 2 :], 1)
        grads[chunk] += [far_a, far_b]

    me_row = lax.axis_index("row")

    def take(values, index):
        return lax.dynamic_index_in_dim(values, index, 0, keepdims=False)

    def to_rows(partial):
        if row_devices != 4:
            return [lax.psum_scatter(partial, "row", scatter_dimension=0, tiled=True)], partial, partial
        low, high = me_row & 1, me_row >> 1
        pieces = partial.reshape(2, 2, part, in_blocks * BLOCK)
        sent, kept = (lax.dynamic_index_in_dim(pieces, bit, 1, keepdims=False) for bit in (1 - low, low))
        moved = lax.ppermute(sent, "row", [(place, place ^ 1) for place in range(4)])
        both = take(kept, 1 - high).astype(jnp.float32) + take(moved, 1 - high).astype(jnp.float32)
        last = lax.ppermute(both.astype(jnp.bfloat16), "row", [(place, place ^ 2) for place in range(4)])
        return [last, take(kept, high), take(moved, high)], both, sent

    def add_up(parts, earlier):
        parts = [*parts[:-1], after(parts[-1], earlier)]
        return sum(part.astype(jnp.float32) for part in parts).astype(jnp.bfloat16)

    def input_sums(chunk):
        return backward(facts, rows, cols, own_t, other_t, grads[chunk], share_blocks, in_blocks)

    def tile_part(chunk, earlier, mine, added):
        table = after(tables[chunk], earlier)
        return outer(facts, rows, cols, table, grads[chunk], share_blocks, half_slots, mine, added)

    first = input_sums(0)
    row_parts, halfway, sent = to_rows(first)
    other_first = tile_part(0, (sent, grads[1][1], grads[1][2]), False, [])
    *first_parts, grads[1][4] = lax.optimization_barrier((*row_parts, after(grads[1][4], other_first)))
    second = input_sums(1)
    row_parts, halfway, sent = to_rows(second)
    own_first = tile_part(0, sent, True, [other_core(other_first)])
    other_second = tile_part(1, after(halfway, own_first), False, [])
    own_second = tile_part(1, other_second, True, [own_first, other_core(other_second)])
    first_sum = add_up(first_parts, other_second)
    second_sum = add_up(row_parts, own_second)
    input_grad = jnp.concatenate([first_sum, second_sum], axis=0)
    tile_grads = own_second.reshape(1, 1, half_slots, 4096)
    return (activation, input_grad, tile_grads)


def solution(mesh):
    return jax.shard_map(
        local,
        mesh=mesh,
        in_specs=(
            P("dp", "col"),
            P("row", "col", "dp", None),
            P("row", "col", None),
            P("row", "col", None),
            P("row", "col"),
            P("dp", ("row", "col")),
        ),
        out_specs=(P("dp", ("row", "col")), P(("dp", "row"), "col"), P("row", "col", "dp", None)),
        check_vma=False,
    )
```

```python
import functools

import jax
import jax.numpy as jnp
from jax import lax
from jax.experimental import pallas as pl
from jax.experimental.pallas import tpu as pltpu
from jax.sharding import PartitionSpec as P

COEFF = 0.7978845608028654
CUBIC = 0.044715
BLOCK = 64
HALF = 32
CHUNKS = 2
ADD_UNROLL = 54
OUTER_UNROLL = 27
TURN_UNROLL = 27
PLAIN_UNROLL = 8
FLOPS_PER_US = 1_150_000_000
MIB = 1024 * 1024
VMEM = pl.BlockSpec(memory_space=pltpu.VMEM)
SMEM = pl.BlockSpec(memory_space=pltpu.SMEM)
HBM = pl.BlockSpec(memory_space=pltpu.HBM)
NT = (((1,), (1,)), ((), ()))


def widest_divisor(total, most):
    return max(divisor for divisor in range(1, most + 1) if total % divisor == 0)


def unpack(packed):
    return jnp.concatenate([packed[:, :BLOCK], packed[:, BLOCK:]], axis=0)


def pack(square):
    return jnp.concatenate([square[:HALF], square[HALF:]], axis=1)


def matmul(left, right):
    return jnp.dot(left, right, preferred_element_type=jnp.float32)


def matmul_nt(left, right):
    return lax.dot_general(left, right, NT, preferred_element_type=jnp.float32)


def call(kernel, name, out_shape, in_specs, out_specs, operands, mib, microseconds, scratch=(), **more):
    moved = sum(operand.size * operand.dtype.itemsize for operand in operands)
    moved += sum(leaf.size * leaf.dtype.itemsize for leaf in jax.tree.leaves(out_shape))
    return pl.pallas_call(
        kernel,
        out_shape=out_shape,
        in_specs=in_specs,
        out_specs=out_specs,
        scratch_shapes=list(scratch),
        name=name,
        compiler_params=pltpu.CompilerParams(vmem_limit_bytes=mib * MIB),
        cost_estimate=pl.CostEstimate(
            flops=microseconds * FLOPS_PER_US, bytes_accessed=moved if microseconds else 0, transcendentals=0
        ),
        **more,
    )(*operands)


def plain_loop(total, body):
    unroll = widest_divisor(total, PLAIN_UNROLL)

    @pl.loop(0, total // unroll)
    def _(group):
        for lane in range(unroll):
            body(group * unroll + lane)


def half_counts(facts_ref, half_slots):
    count, dp = facts_ref[0], facts_ref[2]
    own = dp * half_slots
    other = half_slots - own
    return count, ((own, 0), (other, 1))


def add_products(facts_ref, target_ref, source_ref, tile_refs, table, total, width):
    spare = total.shape[0] - 1
    half_slots = tile_refs[0].shape[0]
    unroll = widest_divisor(half_slots, ADD_UNROLL)
    count, halves = half_counts(facts_ref, half_slots)

    def clear(block):
        total[block] = jnp.zeros(total.shape[1:], jnp.float32)

    plain_loop(spare, clear)

    for first, which in halves:
        live = jnp.clip(count - first, 0, half_slots)

        @pl.loop(0, (live + unroll - 1) // unroll)
        def _(group):
            products = []
            places = []
            for lane in range(unroll):
                index = group * unroll + lane
                slot = first + index
                places.append(jnp.where(slot < count, target_ref[slot], spare))
                products.append(matmul(unpack(tile_refs[which][index]), table[source_ref[slot]]))
            for place, product in zip(places, products):
                total[place] += product


def forward_kernel(share_blocks, facts_ref, row_ref, col_ref, own_ref, other_ref, table_ref, *refs):
    along_x, along_y, own_a, own_b, relay_x, relay_y, total = refs
    half_blocks = share_blocks // 2
    add_products(facts_ref, row_ref, col_ref, (own_ref, other_ref), table_ref, total, table_ref.shape[2])
    me = facts_ref[1]
    for out_ref, share, half in (
        (along_x.at[0], 3, 0),
        (along_x.at[1], 1, 0),
        (along_y.at[0], 3, 1),
        (along_y.at[1], 2, 1),
        (own_a, 0, 0),
        (own_b, 0, 1),
        (relay_x, 1, 1),
        (relay_y, 2, 0),
    ):
        first = (me ^ share) * share_blocks + half * half_blocks

        def write(block, out_ref=out_ref, first=first):
            out_ref[block] = total[first + block].astype(out_ref.dtype)

        plain_loop(half_blocks, write)


def forward(facts, rows, cols, own, other, table, share_blocks, shares):
    blocks = share_blocks * shares
    width = table.shape[2]
    half = (share_blocks // 2, BLOCK, width)
    piece = jax.ShapeDtypeStruct(half, jnp.bfloat16)
    two = jax.ShapeDtypeStruct((2, *half), jnp.bfloat16)
    return call(
        functools.partial(forward_kernel, share_blocks),
        "forward",
        [two] * 2 + [piece] * 4,
        [SMEM] * 3 + [VMEM] * 3,
        [VMEM] * 6,
        (facts, rows, cols, own, other, table),
        16,
        0,
        [pltpu.VMEM((blocks + 1, BLOCK, width), jnp.float32)],
    )


def load_pieces(facts_ref, piece_refs, table, sem, share_blocks):
    half_blocks = share_blocks // 2
    me = facts_ref[1]
    places = ((0, 0, share_blocks), (1, 0, share_blocks), (2, 0, share_blocks))
    places += ((3, 0, half_blocks), (3, half_blocks, half_blocks))
    copies = []
    for number, (piece_ref, (share, start, length)) in enumerate(zip(piece_refs, places)):
        first = (me ^ share) * share_blocks + start
        copies.append(pltpu.make_async_copy(piece_ref, table.at[pl.ds(first, length)], sem.at[number]))
    for copy in copies:
        copy.start()
    return copies


def backward_kernel(share_blocks, facts_ref, row_ref, col_ref, own_ref, other_ref, *refs):
    *piece_refs, out_ref, total, table, sem = refs
    for copy in load_pieces(facts_ref, piece_refs, table, sem, share_blocks):
        copy.wait()
    add_products(facts_ref, col_ref, row_ref, (own_ref, other_ref), table, total, table.shape[2])
    pairs = out_ref.shape[1] // (2 * BLOCK)
    for pair in range(pairs):
        both = jnp.concatenate([total[2 * pair], total[2 * pair + 1]], axis=0)
        out_ref[:, pair * 2 * BLOCK : (pair + 1) * 2 * BLOCK] = both.T.astype(out_ref.dtype)


def backward(facts, rows, cols, own, other, pieces, share_blocks, in_blocks):
    width = pieces[0].shape[2]
    blocks = 4 * share_blocks
    return call(
        functools.partial(backward_kernel, share_blocks),
        "backward",
        jax.ShapeDtypeStruct((width, in_blocks * BLOCK), jnp.bfloat16),
        [SMEM] * 3 + [VMEM] * 2 + [HBM] * len(pieces),
        VMEM,
        (facts, rows, cols, own, other, *pieces),
        12,
        7,
        [
            pltpu.VMEM((in_blocks + 1, BLOCK, width), jnp.float32),
            pltpu.VMEM((blocks, BLOCK, width), jnp.bfloat16),
            pltpu.SemaphoreType.DMA((len(pieces),)),
        ],
    )


def outer_kernel(share_blocks, mine, adds, facts_ref, row_ref, col_ref, *refs):
    added_refs, (input_ref, *piece_refs) = refs[:adds], refs[adds:-3]
    out_ref, table, sem = refs[-3:]
    for copy in load_pieces(facts_ref, piece_refs, table, sem, share_blocks):
        copy.wait()
    half_slots = out_ref.shape[0]
    unroll = widest_divisor(half_slots, OUTER_UNROLL)
    count, halves = half_counts(facts_ref, half_slots)
    first_slot = halves[0][0] if mine else halves[1][0]

    @pl.loop(0, half_slots // unroll)
    def _(group):
        first = group * unroll

        @pl.when(first_slot + first < count)
        def _():
            for lane in range(unroll):
                index = first + lane
                slot = first_slot + index
                packed = pack(matmul_nt(table[row_ref[slot]], input_ref[col_ref[slot]]))
                for added_ref in added_refs:
                    packed += added_ref[index].astype(jnp.float32)
                out_ref[index] = jnp.where(slot < count, packed, 0.0).astype(out_ref.dtype)

        @pl.when(first_slot + first >= count)
        def _():
            for lane in range(unroll):
                out_ref[first + lane] = jnp.zeros(out_ref.shape[1:], out_ref.dtype)


def outer(facts, rows, cols, inputs, pieces, share_blocks, half_slots, mine, added, microseconds):
    blocks = 4 * share_blocks
    return call(
        functools.partial(outer_kernel, share_blocks, mine, len(added)),
        "outer_own" if mine else "outer_other",
        jax.ShapeDtypeStruct((half_slots, HALF, 2 * BLOCK), jnp.bfloat16),
        [SMEM] * 3 + [VMEM] * (len(added) + 1) + [HBM] * len(pieces),
        VMEM,
        (facts, rows, cols, *added, inputs, *pieces),
        12,
        microseconds,
        [
            pltpu.VMEM((blocks, BLOCK, inputs.shape[2]), jnp.bfloat16),
            pltpu.SemaphoreType.DMA((len(pieces),)),
        ],
    )


def transpose_kernel(unroll, own_ref, other_ref, own_out, other_out):
    row = lax.broadcasted_iota(jnp.int32, (BLOCK, BLOCK), 0)
    col = lax.broadcasted_iota(jnp.int32, (BLOCK, BLOCK), 1)
    unit = (row == col).astype(jnp.bfloat16)

    @pl.loop(0, own_ref.shape[0] // unroll)
    def _(group):
        for lane in range(unroll):
            index = group * unroll + lane
            for source, target in ((own_ref, own_out), (other_ref, other_out)):
                target[index] = pack(matmul_nt(unit, unpack(source[index]))).astype(jnp.bfloat16)


def transpose_tiles(own, other):
    shape = jax.ShapeDtypeStruct(own.shape, own.dtype)
    return call(
        functools.partial(transpose_kernel, widest_divisor(own.shape[0], TURN_UNROLL)),
        "transpose_tiles",
        [shape, shape],
        [VMEM] * 2,
        [VMEM] * 2,
        (own, other),
        10,
        0,
    )


def unit_order():
    row = lax.broadcasted_iota(jnp.int32, (2 * BLOCK, 2 * BLOCK), 0)
    col = lax.broadcasted_iota(jnp.int32, (2 * BLOCK, 2 * BLOCK), 1)
    kept = (row & BLOCK) + 2 * (row & (HALF - 1)) + ((row >> 5) & 1)
    return (kept == col).astype(jnp.bfloat16)


def token_rows_kernel(reorder, values_ref, select_ref, *out_refs):
    row = lax.broadcasted_iota(jnp.int32, (2 * BLOCK, 2 * BLOCK), 0)
    col = lax.broadcasted_iota(jnp.int32, (2 * BLOCK, 2 * BLOCK), 1)
    order = unit_order() if reorder else (row == col).astype(jnp.bfloat16)
    for pair in range(out_refs[0].shape[0] // 2):
        lanes = values_ref[:, pair * 2 * BLOCK : (pair + 1) * 2 * BLOCK]
        turned = matmul_nt(order, lanes).astype(jnp.bfloat16)
        for chunk, out_ref in enumerate(out_refs):
            picked = matmul(turned, select_ref[chunk]).astype(jnp.bfloat16)
            out_ref[2 * pair] = picked[:BLOCK]
            out_ref[2 * pair + 1] = picked[BLOCK:]


def token_rows(values, select, reorder):
    chunks, tokens, width = select.shape
    blocks = values.shape[1] // BLOCK
    shape = jax.ShapeDtypeStruct((blocks, BLOCK, width), jnp.bfloat16)
    return call(
        functools.partial(token_rows_kernel, reorder),
        "units_to_rows" if reorder else "features_to_rows",
        [shape] * chunks,
        [VMEM] * 2,
        [VMEM] * chunks,
        (values, select),
        6,
        0,
    )


def rows_to_units_kernel(select_ref, *refs):
    *act_refs, out_ref = refs
    order = unit_order()
    for pair in range(act_refs[0].shape[0] // 2):
        turned = 0.0
        for chunk, act_ref in enumerate(act_refs):
            both = jnp.concatenate([act_ref[2 * pair], act_ref[2 * pair + 1]], axis=0)
            turned = turned + matmul_nt(select_ref[chunk], both)
        out_ref[:, pair * 2 * BLOCK : (pair + 1) * 2 * BLOCK] = matmul(
            turned.astype(jnp.bfloat16), order
        ).astype(out_ref.dtype)


def rows_to_units(select, acts):
    chunks, tokens, width = select.shape
    units = acts[0].shape[0] * BLOCK
    return call(
        rows_to_units_kernel,
        "rows_to_units",
        jax.ShapeDtypeStruct((tokens, units), jnp.bfloat16),
        [VMEM] * (1 + len(acts)),
        VMEM,
        (select, *acts),
        6,
        0,
    )


def gelu_kernel(upstream_hbm, own_a, near_a, last_a, own_b, near_b, last_b, grad_out, act_out, upstream_ref, held, sem):
    half_blocks = own_a.shape[0]
    copies = [pltpu.make_async_copy(upstream_hbm, upstream_ref, sem.at[6])]
    for number, source in enumerate((own_a, near_a.at[1], last_a, own_b, near_b.at[1], last_b)):
        copies.append(pltpu.make_async_copy(source, held.at[number], sem.at[number]))
    for copy in copies:
        copy.start()
    for copy in copies:
        copy.wait()
    for half in range(2):

        def one(block, half=half):
            pre = held[3 * half, block].astype(jnp.float32) + held[3 * half + 1, block].astype(jnp.float32)
            pre = pre + held[3 * half + 2, block].astype(jnp.float32)
            square = pre * pre
            inner = jnp.tanh(COEFF * (pre + CUBIC * square * pre))
            front = 0.5 * (1.0 + inner)
            place = half * half_blocks + block
            act_out[place] = (front * pre).astype(act_out.dtype)
            slope = front + 0.5 * pre * (1.0 - inner * inner) * COEFF * (1.0 + 3.0 * CUBIC * square)
            grad_out[place] = (upstream_ref[place].astype(jnp.float32) * slope).astype(grad_out.dtype)

        plain_loop(half_blocks, one)


def gelu(upstream, parts):
    shape = jax.ShapeDtypeStruct(upstream.shape, jnp.bfloat16)
    return call(
        gelu_kernel,
        "gelu",
        [shape] * 2,
        [HBM] * 7,
        [VMEM] * 2,
        (upstream, *parts),
        8,
        0,
        [
            pltpu.VMEM(upstream.shape, jnp.bfloat16),
            pltpu.VMEM((6, *parts[0].shape), jnp.bfloat16),
            pltpu.SemaphoreType.DMA((7,)),
        ],
    )


def after(value, earlier):
    return lax.optimization_barrier((value, earlier))[0]


def token_select(tokens, rows):
    width = tokens // CHUNKS
    part = width // rows
    chunk = jnp.arange(CHUNKS)[:, None, None]
    token = jnp.arange(tokens)[None, :, None]
    lane = jnp.arange(width)[None, None, :]
    kept = (lane // part) * part * CHUNKS + chunk * part + lane % part
    return (kept == token).astype(jnp.bfloat16)


def local(inputs, weight_tiles, tile_rows, tile_cols, tile_counts, act_grad):
    tokens = inputs.shape[0]
    in_blocks = inputs.shape[1] // BLOCK
    shares = lax.axis_size("col")
    row_devices = lax.axis_size("row")
    dp_devices = lax.axis_size("dp")
    share = act_grad.shape[1]
    share_blocks = share // BLOCK
    slots = tile_rows.shape[2]
    half_slots = weight_tiles.shape[2]
    width = tokens // CHUNKS
    part = width // row_devices
    assert shares == 4 and dp_devices == 2 and share_blocks % 2 == 0
    rows = tile_rows.reshape(slots)
    cols = tile_cols.reshape(slots)
    facts = jnp.stack([tile_counts.reshape(()), lax.axis_index("col"), lax.axis_index("dp")]).astype(jnp.int32)

    def across(values, bit):
        return lax.ppermute(values, "col", [(place, place ^ bit) for place in range(shares)])

    def other_core(values):
        return lax.ppermute(values, "dp", [(0, 1), (1, 0)])

    own = weight_tiles.reshape(half_slots, HALF, 2 * BLOCK)
    other = other_core(own)
    select = token_select(tokens, row_devices)
    tables = token_rows(inputs, select, False)

    partials = [forward(facts, rows, cols, own, other, table, share_blocks, shares) for table in tables]
    upstream = list(token_rows(act_grad, after(select, partials[1][2]), True))
    own_t, other_t = transpose_tiles(after(own, upstream[1]), after(other, upstream[1]))

    terms = []
    for chunk in range(CHUNKS):
        along_x, along_y, own_a, own_b, relay_x, relay_y = partials[chunk]
        from_x, from_y = across(along_x, 1), across(along_y, 2)
        sum_y, sum_x = relay_y + from_x[0], relay_x + from_y[0]
        if chunk:
            sum_y = after(sum_y, own_t)
        last_a, last_b = across(sum_y, 2), across(sum_x, 1)
        terms.append((own_a, from_x, last_a, own_b, from_y, last_b))
    upstream[0] = after(upstream[0], terms[1])

    grads, acts = [], []
    for chunk in range(CHUNKS):
        grad, act = gelu(upstream[chunk], terms[chunk])
        acts.append(act)
        sent_x = sent_y = grad
        if chunk:
            sent_x, sent_y = after(grad, grads[0][1]), after(grad, grads[0][2])
        grads.append([grad, across(sent_x, 1), across(sent_y, 2)])

    activation = rows_to_units(select, acts)
    grads[0][1] = after(grads[0][1], activation)
    for chunk in range(CHUNKS):
        grad, grad_x, grad_y = grads[chunk]
        far_a = across(grad_x[: share_blocks // 2], 2)
        far_b = across(grad_y[share_blocks // 2 :], 1)
        grads[chunk] += [far_a, far_b]

    me_row = lax.axis_index("row")

    def take(values, index):
        return lax.dynamic_index_in_dim(values, index, 0, keepdims=False)

    def to_rows(partial, filler):
        if row_devices != 4:
            return [lax.psum_scatter(partial, "row", scatter_dimension=0, tiled=True)], partial, filler(partial)
        low, high = me_row & 1, me_row >> 1
        pieces = partial.reshape(2, 2, part, in_blocks * BLOCK)
        sent, kept = (lax.dynamic_index_in_dim(pieces, bit, 1, keepdims=False) for bit in (1 - low, low))
        moved = lax.ppermute(sent, "row", [(place, place ^ 1) for place in range(4)])
        filled = filler(sent)
        moved = after(moved, filled)
        both = take(kept, 1 - high).astype(jnp.float32) + take(moved, 1 - high).astype(jnp.float32)
        both = both.astype(jnp.bfloat16)
        last = lax.ppermute(both, "row", [(place, place ^ 2) for place in range(4)])
        return [last, take(kept, high), take(moved, high)], both, filled

    def add_up(parts, earlier):
        parts = [*parts[:-1], after(parts[-1], earlier)]
        return sum(part.astype(jnp.float32) for part in parts).astype(jnp.bfloat16)

    def input_sums(chunk):
        return backward(facts, rows, cols, own_t, other_t, grads[chunk], share_blocks, in_blocks)

    def tile_part(chunk, earlier, mine, added, microseconds=20):
        table = after(tables[chunk], earlier)
        return outer(facts, rows, cols, table, grads[chunk], share_blocks, half_slots, mine, added, microseconds)

    def first_filler(sent):
        return tile_part(0, (sent, grads[1][1], grads[1][2]), False, [], 5)

    first_terms, halfway, other_first = to_rows(input_sums(0), first_filler)
    grads[1][4] = after(grads[1][4], halfway)

    def second_filler(sent):
        first_sum = add_up(first_terms, sent)
        other_second = tile_part(1, first_sum, False, [])
        own_first = tile_part(0, other_second, True, [other_core(other_first)])
        return own_first, other_second, first_sum

    second_terms, halfway, (own_first, other_second, first_sum) = to_rows(input_sums(1), second_filler)
    own_second = tile_part(1, halfway, True, [own_first, other_core(other_second)])
    second_sum = add_up(second_terms, own_second)
    input_grad = jnp.concatenate([first_sum, second_sum], axis=0)
    tile_grads = own_second.reshape(1, 1, half_slots, 4096)
    return (activation, input_grad, tile_grads)


def solution(mesh):
    return jax.shard_map(
        local,
        mesh=mesh,
        in_specs=(
            P("dp", "col"),
            P("row", "col", "dp", None),
            P("row", "col", None),
            P("row", "col", None),
            P("row", "col"),
            P("dp", ("row", "col")),
        ),
        out_specs=(P("dp", ("row", "col")), P(("dp", "row"), "col"), P("row", "col", "dp", None)),
        check_vma=False,
    )
```

```python
import functools

import jax
import jax.numpy as jnp
from jax import lax
from jax.experimental import pallas as pl
from jax.experimental.pallas import tpu as pltpu
from jax.sharding import PartitionSpec as P

COEFF = 0.7978845608028654
CUBIC = 0.044715
BLOCK = 64
HALF = 32
CHUNKS = 2
ADD_UNROLL = 54
OUTER_UNROLL = 27
TURN_UNROLL = 27
PLAIN_UNROLL = 8
FLOPS_PER_US = 1_150_000_000
MIB = 1024 * 1024
VMEM = pl.BlockSpec(memory_space=pltpu.VMEM)
SMEM = pl.BlockSpec(memory_space=pltpu.SMEM)
HBM = pl.BlockSpec(memory_space=pltpu.HBM)
NT = (((1,), (1,)), ((), ()))


def widest_divisor(total, most):
    return max(divisor for divisor in range(1, most + 1) if total % divisor == 0)


def unpack(packed):
    return jnp.concatenate([packed[:, :BLOCK], packed[:, BLOCK:]], axis=0)


def pack(square):
    return jnp.concatenate([square[:HALF], square[HALF:]], axis=1)


def matmul(left, right):
    return jnp.dot(left, right, preferred_element_type=jnp.float32)


def matmul_nt(left, right):
    return lax.dot_general(left, right, NT, preferred_element_type=jnp.float32)


def call(kernel, name, out_shape, in_specs, out_specs, operands, mib, microseconds, scratch=(), **more):
    moved = sum(operand.size * operand.dtype.itemsize for operand in operands)
    moved += sum(leaf.size * leaf.dtype.itemsize for leaf in jax.tree.leaves(out_shape))
    return pl.pallas_call(
        kernel,
        out_shape=out_shape,
        in_specs=in_specs,
        out_specs=out_specs,
        scratch_shapes=list(scratch),
        name=name,
        compiler_params=pltpu.CompilerParams(vmem_limit_bytes=mib * MIB),
        cost_estimate=pl.CostEstimate(
            flops=microseconds * FLOPS_PER_US, bytes_accessed=moved if microseconds else 0, transcendentals=0
        ),
        **more,
    )(*operands)


def plain_loop(total, body):
    unroll = widest_divisor(total, PLAIN_UNROLL)

    @pl.loop(0, total // unroll)
    def _(group):
        for lane in range(unroll):
            body(group * unroll + lane)


def half_counts(facts_ref, half_slots):
    count, dp = facts_ref[0], facts_ref[2]
    own = dp * half_slots
    other = half_slots - own
    return count, ((own, 0), (other, 1))


def add_products(facts_ref, target_ref, source_ref, tile_refs, table, total, width):
    spare = total.shape[0] - 1
    half_slots = tile_refs[0].shape[0]
    unroll = widest_divisor(half_slots, ADD_UNROLL)
    count, halves = half_counts(facts_ref, half_slots)

    def clear(block):
        total[block] = jnp.zeros(total.shape[1:], jnp.float32)

    plain_loop(spare, clear)

    for first, which in halves:
        live = jnp.clip(count - first, 0, half_slots)

        @pl.loop(0, (live + unroll - 1) // unroll)
        def _(group):
            products = []
            places = []
            for lane in range(unroll):
                index = group * unroll + lane
                slot = first + index
                places.append(jnp.where(slot < count, target_ref[slot], spare))
                products.append(matmul(unpack(tile_refs[which][index]), table[source_ref[slot]]))
            for place, product in zip(places, products):
                total[place] += product


def forward_kernel(share_blocks, facts_ref, row_ref, col_ref, own_ref, other_ref, table_ref, *refs):
    along_x, along_y, own_a, own_b, relay_x, relay_y, total = refs
    half_blocks = share_blocks // 2
    add_products(facts_ref, row_ref, col_ref, (own_ref, other_ref), table_ref, total, table_ref.shape[2])
    me = facts_ref[1]
    for out_ref, share, half in (
        (along_x.at[0], 3, 0),
        (along_x.at[1], 1, 0),
        (along_y.at[0], 3, 1),
        (along_y.at[1], 2, 1),
        (own_a, 0, 0),
        (own_b, 0, 1),
        (relay_x, 1, 1),
        (relay_y, 2, 0),
    ):
        first = (me ^ share) * share_blocks + half * half_blocks

        def write(block, out_ref=out_ref, first=first):
            out_ref[block] = total[first + block].astype(out_ref.dtype)

        plain_loop(half_blocks, write)


def forward(facts, rows, cols, own, other, table, share_blocks, shares):
    blocks = share_blocks * shares
    width = table.shape[2]
    half = (share_blocks // 2, BLOCK, width)
    piece = jax.ShapeDtypeStruct(half, jnp.bfloat16)
    two = jax.ShapeDtypeStruct((2, *half), jnp.bfloat16)
    return call(
        functools.partial(forward_kernel, share_blocks),
        "forward",
        [two] * 2 + [piece] * 4,
        [SMEM] * 3 + [VMEM] * 3,
        [VMEM] * 6,
        (facts, rows, cols, own, other, table),
        16,
        0,
        [pltpu.VMEM((blocks + 1, BLOCK, width), jnp.float32)],
    )


def load_pieces(facts_ref, piece_refs, table, sem, share_blocks):
    half_blocks = share_blocks // 2
    me = facts_ref[1]
    places = ((0, 0, share_blocks), (1, 0, share_blocks), (2, 0, share_blocks))
    places += ((3, 0, half_blocks), (3, half_blocks, half_blocks))
    copies = []
    for number, (piece_ref, (share, start, length)) in enumerate(zip(piece_refs, places)):
        first = (me ^ share) * share_blocks + start
        copies.append(pltpu.make_async_copy(piece_ref, table.at[pl.ds(first, length)], sem.at[number]))
    for copy in copies:
        copy.start()
    return copies


def backward_kernel(share_blocks, facts_ref, row_ref, col_ref, own_ref, other_ref, *refs):
    *piece_refs, out_ref, total, table, sem = refs
    for copy in load_pieces(facts_ref, piece_refs, table, sem, share_blocks):
        copy.wait()
    add_products(facts_ref, col_ref, row_ref, (own_ref, other_ref), table, total, table.shape[2])
    pairs = out_ref.shape[1] // (2 * BLOCK)
    for pair in range(pairs):
        both = jnp.concatenate([total[2 * pair], total[2 * pair + 1]], axis=0)
        out_ref[:, pair * 2 * BLOCK : (pair + 1) * 2 * BLOCK] = both.T.astype(out_ref.dtype)


def backward(facts, rows, cols, own, other, pieces, share_blocks, in_blocks):
    width = pieces[0].shape[2]
    blocks = 4 * share_blocks
    return call(
        functools.partial(backward_kernel, share_blocks),
        "backward",
        jax.ShapeDtypeStruct((width, in_blocks * BLOCK), jnp.bfloat16),
        [SMEM] * 3 + [VMEM] * 2 + [HBM] * len(pieces),
        VMEM,
        (facts, rows, cols, own, other, *pieces),
        12,
        7,
        [
            pltpu.VMEM((in_blocks + 1, BLOCK, width), jnp.float32),
            pltpu.VMEM((blocks, BLOCK, width), jnp.bfloat16),
            pltpu.SemaphoreType.DMA((len(pieces),)),
        ],
    )


def outer_kernel(share_blocks, mine, adds, facts_ref, row_ref, col_ref, *refs):
    added_refs, (input_ref, *piece_refs) = refs[:adds], refs[adds:-3]
    out_ref, table, sem = refs[-3:]
    for copy in load_pieces(facts_ref, piece_refs, table, sem, share_blocks):
        copy.wait()
    half_slots = out_ref.shape[0]
    unroll = widest_divisor(half_slots, OUTER_UNROLL)
    count, halves = half_counts(facts_ref, half_slots)
    first_slot = halves[0][0] if mine else halves[1][0]

    @pl.loop(0, half_slots // unroll)
    def _(group):
        first = group * unroll

        @pl.when(first_slot + first < count)
        def _():
            for lane in range(unroll):
                index = first + lane
                slot = first_slot + index
                packed = pack(matmul_nt(table[row_ref[slot]], input_ref[col_ref[slot]]))
                for added_ref in added_refs:
                    packed += added_ref[index].astype(jnp.float32)
                out_ref[index] = jnp.where(slot < count, packed, 0.0).astype(out_ref.dtype)

        @pl.when(first_slot + first >= count)
        def _():
            for lane in range(unroll):
                out_ref[first + lane] = jnp.zeros(out_ref.shape[1:], out_ref.dtype)


def outer(facts, rows, cols, inputs, pieces, share_blocks, half_slots, mine, added, microseconds):
    blocks = 4 * share_blocks
    return call(
        functools.partial(outer_kernel, share_blocks, mine, len(added)),
        "outer_own" if mine else "outer_other",
        jax.ShapeDtypeStruct((half_slots, HALF, 2 * BLOCK), jnp.bfloat16),
        [SMEM] * 3 + [VMEM] * (len(added) + 1) + [HBM] * len(pieces),
        VMEM,
        (facts, rows, cols, *added, inputs, *pieces),
        12,
        microseconds,
        [
            pltpu.VMEM((blocks, BLOCK, inputs.shape[2]), jnp.bfloat16),
            pltpu.SemaphoreType.DMA((len(pieces),)),
        ],
    )


def transpose_kernel(unroll, own_ref, other_ref, own_out, other_out):
    row = lax.broadcasted_iota(jnp.int32, (BLOCK, BLOCK), 0)
    col = lax.broadcasted_iota(jnp.int32, (BLOCK, BLOCK), 1)
    unit = (row == col).astype(jnp.bfloat16)

    @pl.loop(0, own_ref.shape[0] // unroll)
    def _(group):
        for lane in range(unroll):
            index = group * unroll + lane
            for source, target in ((own_ref, own_out), (other_ref, other_out)):
                target[index] = pack(matmul_nt(unit, unpack(source[index]))).astype(jnp.bfloat16)


def transpose_tiles(own, other):
    shape = jax.ShapeDtypeStruct(own.shape, own.dtype)
    return call(
        functools.partial(transpose_kernel, widest_divisor(own.shape[0], TURN_UNROLL)),
        "transpose_tiles",
        [shape, shape],
        [VMEM] * 2,
        [VMEM] * 2,
        (own, other),
        10,
        0,
    )


def unit_order():
    row = lax.broadcasted_iota(jnp.int32, (2 * BLOCK, 2 * BLOCK), 0)
    col = lax.broadcasted_iota(jnp.int32, (2 * BLOCK, 2 * BLOCK), 1)
    kept = (row & BLOCK) + 2 * (row & (HALF - 1)) + ((row >> 5) & 1)
    return (kept == col).astype(jnp.bfloat16)


def token_rows_kernel(reorder, values_ref, select_ref, *out_refs):
    row = lax.broadcasted_iota(jnp.int32, (2 * BLOCK, 2 * BLOCK), 0)
    col = lax.broadcasted_iota(jnp.int32, (2 * BLOCK, 2 * BLOCK), 1)
    order = unit_order() if reorder else (row == col).astype(jnp.bfloat16)
    for pair in range(out_refs[0].shape[0] // 2):
        lanes = values_ref[:, pair * 2 * BLOCK : (pair + 1) * 2 * BLOCK]
        turned = matmul_nt(order, lanes).astype(jnp.bfloat16)
        for chunk, out_ref in enumerate(out_refs):
            picked = matmul(turned, select_ref[chunk]).astype(jnp.bfloat16)
            out_ref[2 * pair] = picked[:BLOCK]
            out_ref[2 * pair + 1] = picked[BLOCK:]


def token_rows(values, select, reorder):
    chunks, tokens, width = select.shape
    blocks = values.shape[1] // BLOCK
    shape = jax.ShapeDtypeStruct((blocks, BLOCK, width), jnp.bfloat16)
    return call(
        functools.partial(token_rows_kernel, reorder),
        "units_to_rows" if reorder else "features_to_rows",
        [shape] * chunks,
        [VMEM] * 2,
        [VMEM] * chunks,
        (values, select),
        6,
        0,
    )


def rows_to_units_kernel(select_ref, *refs):
    *act_refs, out_ref = refs
    order = unit_order()
    for pair in range(act_refs[0].shape[0] // 2):
        turned = 0.0
        for chunk, act_ref in enumerate(act_refs):
            both = jnp.concatenate([act_ref[2 * pair], act_ref[2 * pair + 1]], axis=0)
            turned = turned + matmul_nt(select_ref[chunk], both)
        out_ref[:, pair * 2 * BLOCK : (pair + 1) * 2 * BLOCK] = matmul(
            turned.astype(jnp.bfloat16), order
        ).astype(out_ref.dtype)


def rows_to_units(select, acts):
    chunks, tokens, width = select.shape
    units = acts[0].shape[0] * BLOCK
    return call(
        rows_to_units_kernel,
        "rows_to_units",
        jax.ShapeDtypeStruct((tokens, units), jnp.bfloat16),
        [VMEM] * (1 + len(acts)),
        VMEM,
        (select, *acts),
        6,
        0,
    )


def gelu_kernel(upstream_hbm, own_a, near_a, last_a, own_b, near_b, last_b, grad_out, act_out, upstream_ref, held, sem):
    half_blocks = own_a.shape[0]
    copies = [pltpu.make_async_copy(upstream_hbm, upstream_ref, sem.at[6])]
    for number, source in enumerate((own_a, near_a.at[1], last_a, own_b, near_b.at[1], last_b)):
        copies.append(pltpu.make_async_copy(source, held.at[number], sem.at[number]))
    for copy in copies:
        copy.start()
    for copy in copies:
        copy.wait()
    for half in range(2):

        def one(block, half=half):
            pre = held[3 * half, block].astype(jnp.float32) + held[3 * half + 1, block].astype(jnp.float32)
            pre = pre + held[3 * half + 2, block].astype(jnp.float32)
            square = pre * pre
            inner = jnp.tanh(COEFF * (pre + CUBIC * square * pre))
            front = 0.5 * (1.0 + inner)
            place = half * half_blocks + block
            act_out[place] = (front * pre).astype(act_out.dtype)
            slope = front + 0.5 * pre * (1.0 - inner * inner) * COEFF * (1.0 + 3.0 * CUBIC * square)
            grad_out[place] = (upstream_ref[place].astype(jnp.float32) * slope).astype(grad_out.dtype)

        plain_loop(half_blocks, one)


def gelu(upstream, parts):
    shape = jax.ShapeDtypeStruct(upstream.shape, jnp.bfloat16)
    return call(
        gelu_kernel,
        "gelu",
        [shape] * 2,
        [HBM] * 7,
        [VMEM] * 2,
        (upstream, *parts),
        8,
        0,
        [
            pltpu.VMEM(upstream.shape, jnp.bfloat16),
            pltpu.VMEM((6, *parts[0].shape), jnp.bfloat16),
            pltpu.SemaphoreType.DMA((7,)),
        ],
    )


def after(value, earlier):
    return lax.optimization_barrier((value, earlier))[0]


def token_select(tokens, rows):
    width = tokens // CHUNKS
    part = width // rows
    chunk = jnp.arange(CHUNKS)[:, None, None]
    token = jnp.arange(tokens)[None, :, None]
    lane = jnp.arange(width)[None, None, :]
    kept = (lane // part) * part * CHUNKS + chunk * part + lane % part
    return (kept == token).astype(jnp.bfloat16)


def local(inputs, weight_tiles, tile_rows, tile_cols, tile_counts, act_grad):
    tokens = inputs.shape[0]
    in_blocks = inputs.shape[1] // BLOCK
    shares = lax.axis_size("col")
    row_devices = lax.axis_size("row")
    dp_devices = lax.axis_size("dp")
    share = act_grad.shape[1]
    share_blocks = share // BLOCK
    slots = tile_rows.shape[2]
    half_slots = weight_tiles.shape[2]
    width = tokens // CHUNKS
    part = width // row_devices
    assert shares == 4 and dp_devices == 2 and share_blocks % 2 == 0
    rows = tile_rows.reshape(slots)
    cols = tile_cols.reshape(slots)
    facts = jnp.stack([tile_counts.reshape(()), lax.axis_index("col"), lax.axis_index("dp")]).astype(jnp.int32)

    def across(values, bit):
        return lax.ppermute(values, "col", [(place, place ^ bit) for place in range(shares)])

    def other_core(values):
        return lax.ppermute(values, "dp", [(0, 1), (1, 0)])

    own = weight_tiles.reshape(half_slots, HALF, 2 * BLOCK)
    other = other_core(own)
    select = token_select(tokens, row_devices)
    tables = token_rows(inputs, select, False)

    partials = [forward(facts, rows, cols, own, other, table, share_blocks, shares) for table in tables]
    upstream = list(token_rows(act_grad, after(select, partials[1][2]), True))
    own_t, other_t = transpose_tiles(after(own, upstream[1]), after(other, upstream[1]))

    terms = []
    for chunk in range(CHUNKS):
        along_x, along_y, own_a, own_b, relay_x, relay_y = partials[chunk]
        from_x, from_y = across(along_x, 1), across(along_y, 2)
        sum_y, sum_x = relay_y + from_x[0], relay_x + from_y[0]
        if chunk:
            sum_y = after(sum_y, own_t)
        last_a, last_b = across(sum_y, 2), across(sum_x, 1)
        terms.append((own_a, from_x, last_a, own_b, from_y, last_b))
    upstream[0] = after(upstream[0], terms[1])

    grads, acts = [], []
    for chunk in range(CHUNKS):
        grad, act = gelu(upstream[chunk], terms[chunk])
        acts.append(act)
        sent_x = sent_y = grad
        if chunk:
            sent_x, sent_y = after(grad, grads[0][1]), after(grad, grads[0][2])
        grads.append([grad, across(sent_x, 1), across(sent_y, 2)])

    activation = rows_to_units(select, acts)
    grads[0][1] = after(grads[0][1], activation)
    for chunk in range(CHUNKS):
        grad, grad_x, grad_y = grads[chunk]
        far_a = across(grad_x[: share_blocks // 2], 2)
        far_b = across(grad_y[share_blocks // 2 :], 1)
        grads[chunk] += [far_a, far_b]

    me_row = lax.axis_index("row")

    def take(values, index):
        return lax.dynamic_index_in_dim(values, index, 0, keepdims=False)

    def to_rows(partial, filler):
        if row_devices != 4:
            return [lax.psum_scatter(partial, "row", scatter_dimension=0, tiled=True)], partial, filler(partial)
        low, high = me_row & 1, me_row >> 1
        pieces = partial.reshape(2, 2, part, in_blocks * BLOCK)
        sent, kept = (lax.dynamic_index_in_dim(pieces, bit, 1, keepdims=False) for bit in (1 - low, low))
        moved = lax.ppermute(sent, "row", [(place, place ^ 1) for place in range(4)])
        filled = filler(sent)
        moved = after(moved, filled)
        both = take(kept, 1 - high).astype(jnp.float32) + take(moved, 1 - high).astype(jnp.float32)
        both = both.astype(jnp.bfloat16)
        last = lax.ppermute(both, "row", [(place, place ^ 2) for place in range(4)])
        return [last, take(kept, high), take(moved, high)], both, filled

    def add_up(parts, earlier):
        parts = [*parts[:-1], after(parts[-1], earlier)]
        return sum(part.astype(jnp.float32) for part in parts).astype(jnp.bfloat16)

    def input_sums(chunk):
        return backward(facts, rows, cols, own_t, other_t, grads[chunk], share_blocks, in_blocks)

    def tile_part(chunk, earlier, mine, added, microseconds=20):
        table = after(tables[chunk], earlier)
        return outer(facts, rows, cols, table, grads[chunk], share_blocks, half_slots, mine, added, microseconds)

    def first_filler(sent):
        return tile_part(0, (sent, grads[1][1], grads[1][2]), False, [], 5)

    first_terms, halfway, other_first = to_rows(input_sums(0), first_filler)
    grads[1][4] = after(grads[1][4], halfway)

    def second_filler(sent):
        other_second = tile_part(1, sent, False, [])
        first_sum = add_up(first_terms, other_second)
        own_first = tile_part(0, first_sum, True, [other_core(other_first)])
        return own_first, other_second, first_sum

    second_terms, halfway, (own_first, other_second, first_sum) = to_rows(input_sums(1), second_filler)
    own_second = tile_part(1, halfway, True, [own_first, other_core(other_second)])
    second_sum = add_up(second_terms, own_second)
    input_grad = jnp.concatenate([first_sum, second_sum], axis=0)
    tile_grads = own_second.reshape(1, 1, half_slots, 4096)
    return (activation, input_grad, tile_grads)


def solution(mesh):
    return jax.shard_map(
        local,
        mesh=mesh,
        in_specs=(
            P("dp", "col"),
            P("row", "col", "dp", None),
            P("row", "col", None),
            P("row", "col", None),
            P("row", "col"),
            P("dp", ("row", "col")),
        ),
        out_specs=(P("dp", ("row", "col")), P(("dp", "row"), "col"), P("row", "col", "dp", None)),
        check_vma=False,
    )
```

```python
import functools

import jax
import jax.numpy as jnp
from jax import lax
from jax.experimental import pallas as pl
from jax.experimental.pallas import tpu as pltpu
from jax.sharding import PartitionSpec as P

COEFF = 0.7978845608028654
CUBIC = 0.044715
BLOCK = 64
HALF = 32
CHUNKS = 2
ADD_UNROLL = 54
OUTER_UNROLL = 27
TURN_UNROLL = 27
PLAIN_UNROLL = 8
FLOPS_PER_US = 1_150_000_000
MIB = 1024 * 1024
VMEM = pl.BlockSpec(memory_space=pltpu.VMEM)
SMEM = pl.BlockSpec(memory_space=pltpu.SMEM)
HBM = pl.BlockSpec(memory_space=pltpu.HBM)
NT = (((1,), (1,)), ((), ()))


def widest_divisor(total, most):
    return max(divisor for divisor in range(1, most + 1) if total % divisor == 0)


def unpack(packed):
    return jnp.concatenate([packed[:, :BLOCK], packed[:, BLOCK:]], axis=0)


def pack(square):
    return jnp.concatenate([square[:HALF], square[HALF:]], axis=1)


def matmul(left, right):
    return jnp.dot(left, right, preferred_element_type=jnp.float32)


def matmul_nt(left, right):
    return lax.dot_general(left, right, NT, preferred_element_type=jnp.float32)


def call(kernel, name, out_shape, in_specs, out_specs, operands, mib, microseconds, scratch=(), **more):
    moved = sum(operand.size * operand.dtype.itemsize for operand in operands)
    moved += sum(leaf.size * leaf.dtype.itemsize for leaf in jax.tree.leaves(out_shape))
    return pl.pallas_call(
        kernel,
        out_shape=out_shape,
        in_specs=in_specs,
        out_specs=out_specs,
        scratch_shapes=list(scratch),
        name=name,
        compiler_params=pltpu.CompilerParams(vmem_limit_bytes=mib * MIB),
        cost_estimate=pl.CostEstimate(
            flops=microseconds * FLOPS_PER_US, bytes_accessed=moved if microseconds else 0, transcendentals=0
        ),
        **more,
    )(*operands)


def plain_loop(total, body):
    unroll = widest_divisor(total, PLAIN_UNROLL)

    @pl.loop(0, total // unroll)
    def _(group):
        for lane in range(unroll):
            body(group * unroll + lane)


def half_counts(facts_ref, half_slots):
    count, dp = facts_ref[0], facts_ref[2]
    own = dp * half_slots
    other = half_slots - own
    return count, ((own, 0), (other, 1))


def add_products(facts_ref, target_ref, source_ref, tile_refs, table, total, width):
    spare = total.shape[0] - 1
    half_slots = tile_refs[0].shape[0]
    unroll = widest_divisor(half_slots, ADD_UNROLL)
    count, halves = half_counts(facts_ref, half_slots)

    def clear(block):
        total[block] = jnp.zeros(total.shape[1:], jnp.float32)

    plain_loop(spare, clear)

    for first, which in halves:
        live = jnp.clip(count - first, 0, half_slots)

        @pl.loop(0, (live + unroll - 1) // unroll)
        def _(group):
            products = []
            places = []
            for lane in range(unroll):
                index = group * unroll + lane
                slot = first + index
                places.append(jnp.where(slot < count, target_ref[slot], spare))
                products.append(matmul(unpack(tile_refs[which][index]), table[source_ref[slot]]))
            for place, product in zip(places, products):
                total[place] += product


def forward_kernel(share_blocks, facts_ref, row_ref, col_ref, own_ref, other_ref, table_ref, *refs):
    along_x, along_y, own_a, own_b, relay_x, relay_y, total = refs
    half_blocks = share_blocks // 2
    add_products(facts_ref, row_ref, col_ref, (own_ref, other_ref), table_ref, total, table_ref.shape[2])
    me = facts_ref[1]
    for out_ref, share, half in (
        (along_x.at[0], 3, 0),
        (along_x.at[1], 1, 0),
        (along_y.at[0], 3, 1),
        (along_y.at[1], 2, 1),
        (own_a, 0, 0),
        (own_b, 0, 1),
        (relay_x, 1, 1),
        (relay_y, 2, 0),
    ):
        first = (me ^ share) * share_blocks + half * half_blocks

        def write(block, out_ref=out_ref, first=first):
            out_ref[block] = total[first + block].astype(out_ref.dtype)

        plain_loop(half_blocks, write)


def forward(facts, rows, cols, own, other, table, share_blocks, shares):
    blocks = share_blocks * shares
    width = table.shape[2]
    half = (share_blocks // 2, BLOCK, width)
    piece = jax.ShapeDtypeStruct(half, jnp.bfloat16)
    two = jax.ShapeDtypeStruct((2, *half), jnp.bfloat16)
    return call(
        functools.partial(forward_kernel, share_blocks),
        "forward",
        [two] * 2 + [piece] * 4,
        [SMEM] * 3 + [VMEM] * 3,
        [VMEM] * 6,
        (facts, rows, cols, own, other, table),
        16,
        0,
        [pltpu.VMEM((blocks + 1, BLOCK, width), jnp.float32)],
    )


def load_pieces(facts_ref, piece_refs, table, sem, share_blocks):
    half_blocks = share_blocks // 2
    me = facts_ref[1]
    places = [(share, half * half_blocks, half_blocks) for share in range(4) for half in range(2)]
    copies = []
    for number, (piece_ref, (share, start, length)) in enumerate(zip(piece_refs, places)):
        first = (me ^ share) * share_blocks + start
        copies.append(pltpu.make_async_copy(piece_ref, table.at[pl.ds(first, length)], sem.at[number]))
    for copy in copies:
        copy.start()
    return copies


def backward_kernel(share_blocks, facts_ref, row_ref, col_ref, own_ref, other_ref, *refs):
    *piece_refs, out_ref, total, table, sem = refs
    for copy in load_pieces(facts_ref, piece_refs, table, sem, share_blocks):
        copy.wait()
    add_products(facts_ref, col_ref, row_ref, (own_ref, other_ref), table, total, table.shape[2])
    pairs = out_ref.shape[1] // (2 * BLOCK)
    for pair in range(pairs):
        both = jnp.concatenate([total[2 * pair], total[2 * pair + 1]], axis=0)
        out_ref[:, pair * 2 * BLOCK : (pair + 1) * 2 * BLOCK] = both.T.astype(out_ref.dtype)


def backward(facts, rows, cols, own, other, pieces, share_blocks, in_blocks):
    width = pieces[0].shape[2]
    blocks = 4 * share_blocks
    return call(
        functools.partial(backward_kernel, share_blocks),
        "backward",
        jax.ShapeDtypeStruct((width, in_blocks * BLOCK), jnp.bfloat16),
        [SMEM] * 3 + [VMEM] * 2 + [HBM] * len(pieces),
        VMEM,
        (facts, rows, cols, own, other, *pieces),
        12,
        7,
        [
            pltpu.VMEM((in_blocks + 1, BLOCK, width), jnp.float32),
            pltpu.VMEM((blocks, BLOCK, width), jnp.bfloat16),
            pltpu.SemaphoreType.DMA((len(pieces),)),
        ],
    )


def outer_kernel(share_blocks, mine, adds, facts_ref, row_ref, col_ref, *refs):
    added_refs, (input_ref, *piece_refs) = refs[:adds], refs[adds:-3]
    out_ref, table, sem = refs[-3:]
    for copy in load_pieces(facts_ref, piece_refs, table, sem, share_blocks):
        copy.wait()
    half_slots = out_ref.shape[0]
    unroll = widest_divisor(half_slots, OUTER_UNROLL)
    count, halves = half_counts(facts_ref, half_slots)
    first_slot = halves[0][0] if mine else halves[1][0]

    @pl.loop(0, half_slots // unroll)
    def _(group):
        first = group * unroll

        @pl.when(first_slot + first < count)
        def _():
            for lane in range(unroll):
                index = first + lane
                slot = first_slot + index
                packed = pack(matmul_nt(table[row_ref[slot]], input_ref[col_ref[slot]]))
                for added_ref in added_refs:
                    packed += added_ref[index].astype(jnp.float32)
                out_ref[index] = jnp.where(slot < count, packed, 0.0).astype(out_ref.dtype)

        @pl.when(first_slot + first >= count)
        def _():
            for lane in range(unroll):
                out_ref[first + lane] = jnp.zeros(out_ref.shape[1:], out_ref.dtype)


def outer(facts, rows, cols, inputs, pieces, share_blocks, half_slots, mine, added, microseconds):
    blocks = 4 * share_blocks
    return call(
        functools.partial(outer_kernel, share_blocks, mine, len(added)),
        "outer_own" if mine else "outer_other",
        jax.ShapeDtypeStruct((half_slots, HALF, 2 * BLOCK), jnp.bfloat16),
        [SMEM] * 3 + [VMEM] * (len(added) + 1) + [HBM] * len(pieces),
        VMEM,
        (facts, rows, cols, *added, inputs, *pieces),
        12,
        microseconds,
        [
            pltpu.VMEM((blocks, BLOCK, inputs.shape[2]), jnp.bfloat16),
            pltpu.SemaphoreType.DMA((len(pieces),)),
        ],
    )


def transpose_kernel(unroll, own_ref, other_ref, own_out, other_out):
    row = lax.broadcasted_iota(jnp.int32, (BLOCK, BLOCK), 0)
    col = lax.broadcasted_iota(jnp.int32, (BLOCK, BLOCK), 1)
    unit = (row == col).astype(jnp.bfloat16)

    @pl.loop(0, own_ref.shape[0] // unroll)
    def _(group):
        for lane in range(unroll):
            index = group * unroll + lane
            for source, target in ((own_ref, own_out), (other_ref, other_out)):
                target[index] = pack(matmul_nt(unit, unpack(source[index]))).astype(jnp.bfloat16)


def transpose_tiles(own, other):
    shape = jax.ShapeDtypeStruct(own.shape, own.dtype)
    return call(
        functools.partial(transpose_kernel, widest_divisor(own.shape[0], TURN_UNROLL)),
        "transpose_tiles",
        [shape, shape],
        [VMEM] * 2,
        [VMEM] * 2,
        (own, other),
        10,
        0,
    )


def unit_order():
    row = lax.broadcasted_iota(jnp.int32, (2 * BLOCK, 2 * BLOCK), 0)
    col = lax.broadcasted_iota(jnp.int32, (2 * BLOCK, 2 * BLOCK), 1)
    kept = (row & BLOCK) + 2 * (row & (HALF - 1)) + ((row >> 5) & 1)
    return (kept == col).astype(jnp.bfloat16)


def token_rows_kernel(reorder, values_ref, select_ref, *out_refs):
    row = lax.broadcasted_iota(jnp.int32, (2 * BLOCK, 2 * BLOCK), 0)
    col = lax.broadcasted_iota(jnp.int32, (2 * BLOCK, 2 * BLOCK), 1)
    order = unit_order() if reorder else (row == col).astype(jnp.bfloat16)
    for pair in range(out_refs[0].shape[0] // 2):
        lanes = values_ref[:, pair * 2 * BLOCK : (pair + 1) * 2 * BLOCK]
        turned = matmul_nt(order, lanes).astype(jnp.bfloat16)
        for chunk, out_ref in enumerate(out_refs):
            picked = matmul(turned, select_ref[chunk]).astype(jnp.bfloat16)
            out_ref[2 * pair] = picked[:BLOCK]
            out_ref[2 * pair + 1] = picked[BLOCK:]


def token_rows(values, select, reorder):
    chunks, tokens, width = select.shape
    blocks = values.shape[1] // BLOCK
    shape = jax.ShapeDtypeStruct((blocks, BLOCK, width), jnp.bfloat16)
    return call(
        functools.partial(token_rows_kernel, reorder),
        "units_to_rows" if reorder else "features_to_rows",
        [shape] * chunks,
        [VMEM] * 2,
        [VMEM] * chunks,
        (values, select),
        6,
        0,
    )


def rows_to_units_kernel(select_ref, *refs):
    *act_refs, out_ref = refs
    order = unit_order()
    for pair in range(act_refs[0].shape[0] // 2):
        turned = 0.0
        for chunk, act_ref in enumerate(act_refs):
            both = jnp.concatenate([act_ref[2 * pair], act_ref[2 * pair + 1]], axis=0)
            turned = turned + matmul_nt(select_ref[chunk], both)
        out_ref[:, pair * 2 * BLOCK : (pair + 1) * 2 * BLOCK] = matmul(
            turned.astype(jnp.bfloat16), order
        ).astype(out_ref.dtype)


def rows_to_units(select, acts):
    chunks, tokens, width = select.shape
    units = acts[0].shape[0] * BLOCK
    return call(
        rows_to_units_kernel,
        "rows_to_units",
        jax.ShapeDtypeStruct((tokens, units), jnp.bfloat16),
        [VMEM] * (1 + len(acts)),
        VMEM,
        (select, *acts),
        6,
        0,
    )


def gelu_kernel(upstream_hbm, own_a, near_a, last_a, own_b, near_b, last_b, grad_a, grad_b, act_out, upstream_ref, held, sem):
    half_blocks = own_a.shape[0]
    copies = [pltpu.make_async_copy(upstream_hbm, upstream_ref, sem.at[6])]
    for number, source in enumerate((own_a, near_a.at[1], last_a, own_b, near_b.at[1], last_b)):
        copies.append(pltpu.make_async_copy(source, held.at[number], sem.at[number]))
    for copy in copies:
        copy.start()
    for copy in copies:
        copy.wait()
    for half, grad_out in enumerate((grad_a, grad_b)):

        def one(block, half=half, grad_out=grad_out):
            pre = held[3 * half, block].astype(jnp.float32) + held[3 * half + 1, block].astype(jnp.float32)
            pre = pre + held[3 * half + 2, block].astype(jnp.float32)
            square = pre * pre
            inner = jnp.tanh(COEFF * (pre + CUBIC * square * pre))
            front = 0.5 * (1.0 + inner)
            place = half * half_blocks + block
            act_out[place] = (front * pre).astype(act_out.dtype)
            slope = front + 0.5 * pre * (1.0 - inner * inner) * COEFF * (1.0 + 3.0 * CUBIC * square)
            grad_out[block] = (upstream_ref[place].astype(jnp.float32) * slope).astype(grad_out.dtype)

        plain_loop(half_blocks, one)


def gelu(upstream, parts):
    half = jax.ShapeDtypeStruct(parts[0].shape, jnp.bfloat16)
    return call(
        gelu_kernel,
        "gelu",
        [half, half, jax.ShapeDtypeStruct(upstream.shape, jnp.bfloat16)],
        [HBM] * 7,
        [VMEM] * 3,
        (upstream, *parts),
        8,
        0,
        [
            pltpu.VMEM(upstream.shape, jnp.bfloat16),
            pltpu.VMEM((6, *parts[0].shape), jnp.bfloat16),
            pltpu.SemaphoreType.DMA((7,)),
        ],
    )


def after(value, earlier):
    return lax.optimization_barrier((value, earlier))[0]


def token_select(tokens, rows):
    width = tokens // CHUNKS
    part = width // rows
    chunk = jnp.arange(CHUNKS)[:, None, None]
    token = jnp.arange(tokens)[None, :, None]
    lane = jnp.arange(width)[None, None, :]
    kept = (lane // part) * part * CHUNKS + chunk * part + lane % part
    return (kept == token).astype(jnp.bfloat16)


def local(inputs, weight_tiles, tile_rows, tile_cols, tile_counts, act_grad):
    tokens = inputs.shape[0]
    in_blocks = inputs.shape[1] // BLOCK
    shares = lax.axis_size("col")
    row_devices = lax.axis_size("row")
    dp_devices = lax.axis_size("dp")
    share = act_grad.shape[1]
    share_blocks = share // BLOCK
    slots = tile_rows.shape[2]
    half_slots = weight_tiles.shape[2]
    width = tokens // CHUNKS
    part = width // row_devices
    assert shares == 4 and dp_devices == 2 and share_blocks % 2 == 0
    rows = tile_rows.reshape(slots)
    cols = tile_cols.reshape(slots)
    facts = jnp.stack([tile_counts.reshape(()), lax.axis_index("col"), lax.axis_index("dp")]).astype(jnp.int32)

    def across(values, bit):
        return lax.ppermute(values, "col", [(place, place ^ bit) for place in range(shares)])

    def other_core(values):
        return lax.ppermute(values, "dp", [(0, 1), (1, 0)])

    own = weight_tiles.reshape(half_slots, HALF, 2 * BLOCK)
    other = other_core(own)
    select = token_select(tokens, row_devices)
    tables = token_rows(inputs, select, False)

    partials = [forward(facts, rows, cols, own, other, table, share_blocks, shares) for table in tables]
    upstream = list(token_rows(act_grad, after(select, partials[1][2]), True))
    own_t, other_t = transpose_tiles(after(own, upstream[1]), after(other, upstream[1]))

    terms = []
    for chunk in range(CHUNKS):
        along_x, along_y, own_a, own_b, relay_x, relay_y = partials[chunk]
        from_x, from_y = across(along_x, 1), across(along_y, 2)
        sum_y, sum_x = relay_y + from_x[0], relay_x + from_y[0]
        if chunk:
            sum_y = after(sum_y, own_t)
        last_a, last_b = across(sum_y, 2), across(sum_x, 1)
        terms.append((own_a, from_x, last_a, own_b, from_y, last_b))
    upstream[0] = after(upstream[0], terms[1])

    grads, acts = [], []
    for chunk in range(CHUNKS):
        grad_a, grad_b, act = gelu(upstream[chunk], terms[chunk])
        acts.append(act)
        x_a, y_b, x_b, y_a = grad_a, grad_b, grad_b, grad_a
        if chunk:
            x_a, x_b = after(grad_a, grads[0][3]), after(grad_b, grads[0][3])
            y_a, y_b = after(grad_a, grads[0][4]), after(grad_b, grads[0][4])
        x_a, y_b = across(x_a, 1), across(y_b, 2)
        x_b, y_a = across(x_b, 1), across(y_a, 2)
        grads.append([grad_a, grad_b, x_a, x_b, y_a, y_b])

    activation = rows_to_units(select, acts)
    for chunk in range(CHUNKS):
        x_a, y_b = grads[chunk][2], grads[chunk][5]
        grads[chunk] += [across(x_a, 2), across(y_b, 1)]
    grads[0][7] = after(grads[0][7], activation)

    me_row = lax.axis_index("row")

    def take(values, index):
        return lax.dynamic_index_in_dim(values, index, 0, keepdims=False)

    def to_rows(partial, filler):
        if row_devices != 4:
            return [lax.psum_scatter(partial, "row", scatter_dimension=0, tiled=True)], partial, filler(partial)
        low, high = me_row & 1, me_row >> 1
        pieces = partial.reshape(2, 2, part, in_blocks * BLOCK)
        sent, kept = (lax.dynamic_index_in_dim(pieces, bit, 1, keepdims=False) for bit in (1 - low, low))
        moved = lax.ppermute(sent, "row", [(place, place ^ 1) for place in range(4)])
        filled = filler(sent)
        moved = after(moved, filled)
        both = take(kept, 1 - high).astype(jnp.float32) + take(moved, 1 - high).astype(jnp.float32)
        both = both.astype(jnp.bfloat16)
        last = lax.ppermute(both, "row", [(place, place ^ 2) for place in range(4)])
        return [last, take(kept, high), take(moved, high)], both, filled

    def add_up(parts, earlier):
        parts = [*parts[:-1], after(parts[-1], earlier)]
        return sum(part.astype(jnp.float32) for part in parts).astype(jnp.bfloat16)

    def input_sums(chunk):
        return backward(facts, rows, cols, own_t, other_t, grads[chunk], share_blocks, in_blocks)

    def tile_part(chunk, earlier, mine, added, microseconds=20):
        table = after(tables[chunk], earlier)
        return outer(facts, rows, cols, table, grads[chunk], share_blocks, half_slots, mine, added, microseconds)

    def first_filler(sent):
        return tile_part(0, (sent, grads[1][2:6]), False, [], 5)

    first_terms, halfway, other_first = to_rows(input_sums(0), first_filler)
    grads[1][7] = after(grads[1][7], halfway)

    def second_filler(sent):
        other_second = tile_part(1, sent, False, [])
        first_sum = add_up(first_terms, other_second)
        own_first = tile_part(0, first_sum, True, [other_core(other_first)])
        return own_first, other_second, first_sum

    second_terms, halfway, (own_first, other_second, first_sum) = to_rows(input_sums(1), second_filler)
    own_second = tile_part(1, halfway, True, [own_first, other_core(other_second)])
    second_sum = add_up(second_terms, own_second)
    input_grad = jnp.concatenate([first_sum, second_sum], axis=0)
    tile_grads = own_second.reshape(1, 1, half_slots, 4096)
    return (activation, input_grad, tile_grads)


def solution(mesh):
    return jax.shard_map(
        local,
        mesh=mesh,
        in_specs=(
            P("dp", "col"),
            P("row", "col", "dp", None),
            P("row", "col", None),
            P("row", "col", None),
            P("row", "col"),
            P("dp", ("row", "col")),
        ),
        out_specs=(P("dp", ("row", "col")), P(("dp", "row"), "col"), P("row", "col", "dp", None)),
        check_vma=False,
    )
```

```python
import functools

import jax
import jax.numpy as jnp
from jax import lax
from jax.experimental import pallas as pl
from jax.experimental.pallas import tpu as pltpu
from jax.sharding import PartitionSpec as P

COEFF = 0.7978845608028654
CUBIC = 0.044715
BLOCK = 64
HALF = 32
CHUNKS = 2
ADD_UNROLL = 54
OUTER_UNROLL = 27
TURN_UNROLL = 27
PLAIN_UNROLL = 8
FLOPS_PER_US = 1_150_000_000
MIB = 1024 * 1024
VMEM = pl.BlockSpec(memory_space=pltpu.VMEM)
SMEM = pl.BlockSpec(memory_space=pltpu.SMEM)
HBM = pl.BlockSpec(memory_space=pltpu.HBM)
NT = (((1,), (1,)), ((), ()))


def widest_divisor(total, most):
    return max(divisor for divisor in range(1, most + 1) if total % divisor == 0)


def unpack(packed):
    return jnp.concatenate([packed[:, :BLOCK], packed[:, BLOCK:]], axis=0)


def pack(square):
    return jnp.concatenate([square[:HALF], square[HALF:]], axis=1)


def matmul(left, right):
    return jnp.dot(left, right, preferred_element_type=jnp.float32)


def matmul_nt(left, right):
    return lax.dot_general(left, right, NT, preferred_element_type=jnp.float32)


def call(kernel, name, out_shape, in_specs, out_specs, operands, mib, microseconds, scratch=(), **more):
    moved = sum(operand.size * operand.dtype.itemsize for operand in operands)
    moved += sum(leaf.size * leaf.dtype.itemsize for leaf in jax.tree.leaves(out_shape))
    return pl.pallas_call(
        kernel,
        out_shape=out_shape,
        in_specs=in_specs,
        out_specs=out_specs,
        scratch_shapes=list(scratch),
        name=name,
        compiler_params=pltpu.CompilerParams(vmem_limit_bytes=mib * MIB),
        cost_estimate=pl.CostEstimate(
            flops=microseconds * FLOPS_PER_US, bytes_accessed=moved if microseconds else 0, transcendentals=0
        ),
        **more,
    )(*operands)


def plain_loop(total, body):
    unroll = widest_divisor(total, PLAIN_UNROLL)

    @pl.loop(0, total // unroll)
    def _(group):
        for lane in range(unroll):
            body(group * unroll + lane)


def half_counts(facts_ref, half_slots):
    count, dp = facts_ref[0], facts_ref[2]
    own = dp * half_slots
    other = half_slots - own
    return count, ((own, 0), (other, 1))


def add_products(facts_ref, target_ref, source_ref, tile_refs, table, total, width):
    spare = total.shape[0] - 1
    half_slots = tile_refs[0].shape[0]
    unroll = widest_divisor(half_slots, ADD_UNROLL)
    count, halves = half_counts(facts_ref, half_slots)

    def clear(block):
        total[block] = jnp.zeros(total.shape[1:], jnp.float32)

    plain_loop(spare, clear)

    for first, which in halves:
        live = jnp.clip(count - first, 0, half_slots)

        @pl.loop(0, (live + unroll - 1) // unroll)
        def _(group):
            products = []
            places = []
            for lane in range(unroll):
                index = group * unroll + lane
                slot = first + index
                places.append(jnp.where(slot < count, target_ref[slot], spare))
                products.append(matmul(unpack(tile_refs[which][index]), table[source_ref[slot]]))
            for place, product in zip(places, products):
                total[place] += product


def forward_kernel(share_blocks, facts_ref, row_ref, col_ref, own_ref, other_ref, table_ref, *refs):
    along_x, along_y, own_a, own_b, relay_x, relay_y, total = refs
    half_blocks = share_blocks // 2
    add_products(facts_ref, row_ref, col_ref, (own_ref, other_ref), table_ref, total, table_ref.shape[2])
    me = facts_ref[1]
    for out_ref, share, half in (
        (along_x.at[0], 3, 0),
        (along_x.at[1], 1, 0),
        (along_y.at[0], 3, 1),
        (along_y.at[1], 2, 1),
        (own_a, 0, 0),
        (own_b, 0, 1),
        (relay_x, 1, 1),
        (relay_y, 2, 0),
    ):
        first = (me ^ share) * share_blocks + half * half_blocks

        def write(block, out_ref=out_ref, first=first):
            out_ref[block] = total[first + block].astype(out_ref.dtype)

        plain_loop(half_blocks, write)


def forward(facts, rows, cols, own, other, table, share_blocks, shares):
    blocks = share_blocks * shares
    width = table.shape[2]
    half = (share_blocks // 2, BLOCK, width)
    piece = jax.ShapeDtypeStruct(half, jnp.bfloat16)
    two = jax.ShapeDtypeStruct((2, *half), jnp.bfloat16)
    return call(
        functools.partial(forward_kernel, share_blocks),
        "forward",
        [two] * 2 + [piece] * 4,
        [SMEM] * 3 + [VMEM] * 3,
        [VMEM] * 6,
        (facts, rows, cols, own, other, table),
        16,
        0,
        [pltpu.VMEM((blocks + 1, BLOCK, width), jnp.float32)],
    )


def load_pieces(facts_ref, piece_refs, table, sem, share_blocks):
    half_blocks = share_blocks // 2
    me = facts_ref[1]
    places = [(share, half * half_blocks, half_blocks) for share in range(4) for half in range(2)]
    copies = []
    for number, (piece_ref, (share, start, length)) in enumerate(zip(piece_refs, places)):
        first = (me ^ share) * share_blocks + start
        copies.append(pltpu.make_async_copy(piece_ref, table.at[pl.ds(first, length)], sem.at[number]))
    for copy in copies:
        copy.start()
    return copies


def backward_kernel(share_blocks, facts_ref, row_ref, col_ref, own_ref, other_ref, *refs):
    *piece_refs, out_ref, total, table, sem = refs
    for copy in load_pieces(facts_ref, piece_refs, table, sem, share_blocks):
        copy.wait()
    add_products(facts_ref, col_ref, row_ref, (own_ref, other_ref), table, total, table.shape[2])
    pairs = out_ref.shape[1] // (2 * BLOCK)
    for pair in range(pairs):
        both = jnp.concatenate([total[2 * pair], total[2 * pair + 1]], axis=0)
        out_ref[:, pair * 2 * BLOCK : (pair + 1) * 2 * BLOCK] = both.T.astype(out_ref.dtype)


def backward(facts, rows, cols, own, other, pieces, share_blocks, in_blocks):
    width = pieces[0].shape[2]
    blocks = 4 * share_blocks
    return call(
        functools.partial(backward_kernel, share_blocks),
        "backward",
        jax.ShapeDtypeStruct((width, in_blocks * BLOCK), jnp.bfloat16),
        [SMEM] * 3 + [VMEM] * 2 + [HBM] * len(pieces),
        VMEM,
        (facts, rows, cols, own, other, *pieces),
        12,
        7,
        [
            pltpu.VMEM((in_blocks + 1, BLOCK, width), jnp.float32),
            pltpu.VMEM((blocks, BLOCK, width), jnp.bfloat16),
            pltpu.SemaphoreType.DMA((len(pieces),)),
        ],
    )


def outer_kernel(share_blocks, mine, adds, facts_ref, row_ref, col_ref, *refs):
    added_refs, (input_ref, *piece_refs) = refs[:adds], refs[adds:-3]
    out_ref, table, sem = refs[-3:]
    for copy in load_pieces(facts_ref, piece_refs, table, sem, share_blocks):
        copy.wait()
    half_slots = out_ref.shape[0]
    unroll = widest_divisor(half_slots, OUTER_UNROLL)
    count, halves = half_counts(facts_ref, half_slots)
    first_slot = halves[0][0] if mine else halves[1][0]

    @pl.loop(0, half_slots // unroll)
    def _(group):
        first = group * unroll

        @pl.when(first_slot + first < count)
        def _():
            for lane in range(unroll):
                index = first + lane
                slot = first_slot + index
                packed = pack(matmul_nt(table[row_ref[slot]], input_ref[col_ref[slot]]))
                for added_ref in added_refs:
                    packed += added_ref[index].astype(jnp.float32)
                out_ref[index] = jnp.where(slot < count, packed, 0.0).astype(out_ref.dtype)

        @pl.when(first_slot + first >= count)
        def _():
            for lane in range(unroll):
                out_ref[first + lane] = jnp.zeros(out_ref.shape[1:], out_ref.dtype)


def outer(facts, rows, cols, inputs, pieces, share_blocks, half_slots, mine, added, microseconds):
    blocks = 4 * share_blocks
    return call(
        functools.partial(outer_kernel, share_blocks, mine, len(added)),
        "outer_own" if mine else "outer_other",
        jax.ShapeDtypeStruct((half_slots, HALF, 2 * BLOCK), jnp.bfloat16),
        [SMEM] * 3 + [VMEM] * (len(added) + 1) + [HBM] * len(pieces),
        VMEM,
        (facts, rows, cols, *added, inputs, *pieces),
        12,
        microseconds,
        [
            pltpu.VMEM((blocks, BLOCK, inputs.shape[2]), jnp.bfloat16),
            pltpu.SemaphoreType.DMA((len(pieces),)),
        ],
    )


def transpose_kernel(unroll, own_ref, other_ref, own_out, other_out):
    row = lax.broadcasted_iota(jnp.int32, (BLOCK, BLOCK), 0)
    col = lax.broadcasted_iota(jnp.int32, (BLOCK, BLOCK), 1)
    unit = (row == col).astype(jnp.bfloat16)

    @pl.loop(0, own_ref.shape[0] // unroll)
    def _(group):
        for lane in range(unroll):
            index = group * unroll + lane
            for source, target in ((own_ref, own_out), (other_ref, other_out)):
                target[index] = pack(matmul_nt(unit, unpack(source[index]))).astype(jnp.bfloat16)


def transpose_tiles(own, other):
    shape = jax.ShapeDtypeStruct(own.shape, own.dtype)
    return call(
        functools.partial(transpose_kernel, widest_divisor(own.shape[0], TURN_UNROLL)),
        "transpose_tiles",
        [shape, shape],
        [VMEM] * 2,
        [VMEM] * 2,
        (own, other),
        10,
        0,
    )


def unit_order():
    row = lax.broadcasted_iota(jnp.int32, (2 * BLOCK, 2 * BLOCK), 0)
    col = lax.broadcasted_iota(jnp.int32, (2 * BLOCK, 2 * BLOCK), 1)
    kept = (row & BLOCK) + 2 * (row & (HALF - 1)) + ((row >> 5) & 1)
    return (kept == col).astype(jnp.bfloat16)


def token_rows_kernel(reorder, values_ref, select_ref, *out_refs):
    row = lax.broadcasted_iota(jnp.int32, (2 * BLOCK, 2 * BLOCK), 0)
    col = lax.broadcasted_iota(jnp.int32, (2 * BLOCK, 2 * BLOCK), 1)
    order = unit_order() if reorder else (row == col).astype(jnp.bfloat16)
    for pair in range(out_refs[0].shape[0] // 2):
        lanes = values_ref[:, pair * 2 * BLOCK : (pair + 1) * 2 * BLOCK]
        turned = matmul_nt(order, lanes).astype(jnp.bfloat16)
        for chunk, out_ref in enumerate(out_refs):
            picked = matmul(turned, select_ref[chunk]).astype(jnp.bfloat16)
            out_ref[2 * pair] = picked[:BLOCK]
            out_ref[2 * pair + 1] = picked[BLOCK:]


def token_rows(values, select, reorder):
    chunks, tokens, width = select.shape
    blocks = values.shape[1] // BLOCK
    shape = jax.ShapeDtypeStruct((blocks, BLOCK, width), jnp.bfloat16)
    return call(
        functools.partial(token_rows_kernel, reorder),
        "units_to_rows" if reorder else "features_to_rows",
        [shape] * chunks,
        [VMEM] * 2,
        [VMEM] * chunks,
        (values, select),
        6,
        0,
    )


def rows_to_units_kernel(select_ref, *refs):
    *act_refs, out_ref = refs
    order = unit_order()
    for pair in range(act_refs[0].shape[0] // 2):
        turned = 0.0
        for chunk, act_ref in enumerate(act_refs):
            both = jnp.concatenate([act_ref[2 * pair], act_ref[2 * pair + 1]], axis=0)
            turned = turned + matmul_nt(select_ref[chunk], both)
        out_ref[:, pair * 2 * BLOCK : (pair + 1) * 2 * BLOCK] = matmul(
            turned.astype(jnp.bfloat16), order
        ).astype(out_ref.dtype)


def rows_to_units(select, acts):
    chunks, tokens, width = select.shape
    units = acts[0].shape[0] * BLOCK
    return call(
        rows_to_units_kernel,
        "rows_to_units",
        jax.ShapeDtypeStruct((tokens, units), jnp.bfloat16),
        [VMEM] * (1 + len(acts)),
        VMEM,
        (select, *acts),
        6,
        0,
    )


def gelu_kernel(upstream_hbm, own_a, near_a, last_a, own_b, near_b, last_b, grad_a, grad_b, act_out, upstream_ref, held, sem):
    half_blocks = own_a.shape[0]
    copies = [pltpu.make_async_copy(upstream_hbm, upstream_ref, sem.at[6])]
    for number, source in enumerate((own_a, near_a.at[1], last_a, own_b, near_b.at[1], last_b)):
        copies.append(pltpu.make_async_copy(source, held.at[number], sem.at[number]))
    for copy in copies:
        copy.start()
    for copy in copies:
        copy.wait()
    for half, grad_out in enumerate((grad_a, grad_b)):

        def one(block, half=half, grad_out=grad_out):
            pre = held[3 * half, block].astype(jnp.float32) + held[3 * half + 1, block].astype(jnp.float32)
            pre = pre + held[3 * half + 2, block].astype(jnp.float32)
            square = pre * pre
            inner = jnp.tanh(COEFF * (pre + CUBIC * square * pre))
            front = 0.5 * (1.0 + inner)
            place = half * half_blocks + block
            act_out[place] = (front * pre).astype(act_out.dtype)
            slope = front + 0.5 * pre * (1.0 - inner * inner) * COEFF * (1.0 + 3.0 * CUBIC * square)
            grad_out[block] = (upstream_ref[place].astype(jnp.float32) * slope).astype(grad_out.dtype)

        plain_loop(half_blocks, one)


def gelu(upstream, parts):
    half = jax.ShapeDtypeStruct(parts[0].shape, jnp.bfloat16)
    return call(
        gelu_kernel,
        "gelu",
        [half, half, jax.ShapeDtypeStruct(upstream.shape, jnp.bfloat16)],
        [HBM] * 7,
        [VMEM] * 3,
        (upstream, *parts),
        8,
        0,
        [
            pltpu.VMEM(upstream.shape, jnp.bfloat16),
            pltpu.VMEM((6, *parts[0].shape), jnp.bfloat16),
            pltpu.SemaphoreType.DMA((7,)),
        ],
    )


def after(value, earlier):
    return lax.optimization_barrier((value, earlier))[0]


def token_select(tokens, rows):
    width = tokens // CHUNKS
    part = width // rows
    chunk = jnp.arange(CHUNKS)[:, None, None]
    token = jnp.arange(tokens)[None, :, None]
    lane = jnp.arange(width)[None, None, :]
    kept = (lane // part) * part * CHUNKS + chunk * part + lane % part
    return (kept == token).astype(jnp.bfloat16)


def local(inputs, weight_tiles, tile_rows, tile_cols, tile_counts, act_grad):
    tokens = inputs.shape[0]
    in_blocks = inputs.shape[1] // BLOCK
    shares = lax.axis_size("col")
    row_devices = lax.axis_size("row")
    dp_devices = lax.axis_size("dp")
    share = act_grad.shape[1]
    share_blocks = share // BLOCK
    slots = tile_rows.shape[2]
    half_slots = weight_tiles.shape[2]
    width = tokens // CHUNKS
    part = width // row_devices
    assert shares == 4 and dp_devices == 2 and share_blocks % 2 == 0
    rows = tile_rows.reshape(slots)
    cols = tile_cols.reshape(slots)
    facts = jnp.stack([tile_counts.reshape(()), lax.axis_index("col"), lax.axis_index("dp")]).astype(jnp.int32)

    def across(values, bit):
        return lax.ppermute(values, "col", [(place, place ^ bit) for place in range(shares)])

    def other_core(values):
        return lax.ppermute(values, "dp", [(0, 1), (1, 0)])

    own = weight_tiles.reshape(half_slots, HALF, 2 * BLOCK)
    other = other_core(own)
    select = token_select(tokens, row_devices)
    tables = token_rows(inputs, select, False)

    partials = [forward(facts, rows, cols, own, other, table, share_blocks, shares) for table in tables]
    upstream = list(token_rows(act_grad, after(select, partials[1][2]), True))
    own_t, other_t = transpose_tiles(after(own, upstream[1]), after(other, upstream[1]))

    terms = []
    for chunk in range(CHUNKS):
        along_x, along_y, own_a, own_b, relay_x, relay_y = partials[chunk]
        from_x, from_y = across(along_x, 1), across(along_y, 2)
        sum_y, sum_x = relay_y + from_x[0], relay_x + from_y[0]
        if chunk:
            sum_y = after(sum_y, own_t)
        last_a, last_b = across(sum_y, 2), across(sum_x, 1)
        terms.append((own_a, from_x, last_a, own_b, from_y, last_b))
    upstream[0] = after(upstream[0], terms[1])

    grads, acts = [], []
    for chunk in range(CHUNKS):
        grad_a, grad_b, act = gelu(upstream[chunk], terms[chunk])
        acts.append(act)
        x_a, y_b, x_b, y_a = grad_a, grad_b, grad_b, grad_a
        if chunk:
            x_a, x_b = after(grad_a, grads[0][3]), after(grad_b, grads[0][3])
            y_a, y_b = after(grad_a, grads[0][4]), after(grad_b, grads[0][4])
        x_a, y_b = across(x_a, 1), across(y_b, 2)
        x_b, y_a = across(x_b, 1), across(y_a, 2)
        grads.append([grad_a, grad_b, x_a, x_b, y_a, y_b])

    activation = rows_to_units(select, acts)
    for chunk in range(CHUNKS):
        x_a, y_b = grads[chunk][2], grads[chunk][5]
        if chunk == 0:
            x_a, y_b = after(x_a, activation), after(y_b, activation)
        grads[chunk] += [across(x_a, 2), across(y_b, 1)]

    me_row = lax.axis_index("row")

    def take(values, index):
        return lax.dynamic_index_in_dim(values, index, 0, keepdims=False)

    def to_rows(partial, filler):
        if row_devices != 4:
            return [lax.psum_scatter(partial, "row", scatter_dimension=0, tiled=True)], partial, filler(partial)
        low, high = me_row & 1, me_row >> 1
        pieces = partial.reshape(2, 2, part, in_blocks * BLOCK)
        sent, kept = (lax.dynamic_index_in_dim(pieces, bit, 1, keepdims=False) for bit in (1 - low, low))
        moved = lax.ppermute(sent, "row", [(place, place ^ 1) for place in range(4)])
        filled = filler(sent)
        moved = after(moved, filled)
        both = take(kept, 1 - high).astype(jnp.float32) + take(moved, 1 - high).astype(jnp.float32)
        both = both.astype(jnp.bfloat16)
        last = lax.ppermute(both, "row", [(place, place ^ 2) for place in range(4)])
        return [last, take(kept, high), take(moved, high)], both, filled

    def add_up(parts, earlier):
        parts = [*parts[:-1], after(parts[-1], earlier)]
        return sum(part.astype(jnp.float32) for part in parts).astype(jnp.bfloat16)

    def input_sums(chunk):
        return backward(facts, rows, cols, own_t, other_t, grads[chunk], share_blocks, in_blocks)

    def tile_part(chunk, earlier, mine, added, microseconds=20):
        table = after(tables[chunk], earlier)
        return outer(facts, rows, cols, table, grads[chunk], share_blocks, half_slots, mine, added, microseconds)

    def first_filler(sent):
        return tile_part(0, (sent, grads[1][2:6]), False, [], 5)

    first_terms, halfway, other_first = to_rows(input_sums(0), first_filler)
    grads[1][7] = after(grads[1][7], halfway)

    def second_filler(sent):
        other_second = tile_part(1, sent, False, [])
        first_sum = add_up(first_terms, other_second)
        own_first = tile_part(0, first_sum, True, [other_core(other_first)])
        return own_first, other_second, first_sum

    second_terms, halfway, (own_first, other_second, first_sum) = to_rows(input_sums(1), second_filler)
    own_second = tile_part(1, halfway, True, [own_first, other_core(other_second)])
    second_sum = add_up(second_terms, own_second)
    input_grad = jnp.concatenate([first_sum, second_sum], axis=0)
    tile_grads = own_second.reshape(1, 1, half_slots, 4096)
    return (activation, input_grad, tile_grads)


def solution(mesh):
    return jax.shard_map(
        local,
        mesh=mesh,
        in_specs=(
            P("dp", "col"),
            P("row", "col", "dp", None),
            P("row", "col", None),
            P("row", "col", None),
            P("row", "col"),
            P("dp", ("row", "col")),
        ),
        out_specs=(P("dp", ("row", "col")), P(("dp", "row"), "col"), P("row", "col", "dp", None)),
        check_vma=False,
    )
```
